256 devices in a mesh: prop: 8 (over x, core), dom: 32 (over z, y).
Axes of the slice: x: 4, y: 4, z: 8, core: 2. Of those that a mesh axis runs over, the one named last changes fastest.
Arguments:
- states: float32 [8, 128, 64, 128], P('prop', 'dom'), may hold values from -4 to 4
- accepted: int32 [1], replicated, may hold values from 0 to 7
- noise: float32 [8, 128, 64, 128], P('prop', 'dom'), may hold values from -5 to 5
- source: float32 [128, 64, 128], P('dom'), may hold values from -6 to 6
Outputs:
- pressure: float32 [8, 128, 64, 128], P('prop', 'dom')
The draws below stay inside these ranges and needn't reach their ends.
All inputs are finite; a program needn't handle non-finite values.
Results may differ from the reference program's by a relative error of at most 0.0003.
Values sent between devices are 32-bit elements; how exact they have to be, the bound alone decides.
A program may use at most 128 MiB of HBM per device.

```python
import math
import jax
import jax.numpy as jnp
from jax import lax

NX = 64
NY = 128
LEVELS = 4
SWEEPS = 2
COARSE_SWEEPS = 64
PROPS = 8
NZ = 128


def steps_of(own_key, shape, pieces, least, top_value):
    def one(position, blocks):
        steps = jax.random.uniform(jax.random.fold_in(jax.random.fold_in(own_key, 6), position), (blocks,), jnp.float32, least / len(pieces), top_value / len(pieces))
        return jnp.repeat(jnp.exp(steps), shape[position] // blocks).reshape((-1,) + (1,) * (len(shape) - position - 1))

    gain = one(*pieces[0])
    for cut in pieces[1:]:
        gain = gain * one(*cut)
    return gain


def bell_draw(own_key, extent, spread, limit, shards=(), held_as=jnp.bfloat16):
    array = spread * jax.random.normal(own_key, extent, jnp.float32)
    if shards:
        array = array * steps_of(own_key, extent, shards, -0.22, 0.18)
    return jnp.clip(array, -limit, limit).astype(held_as)


def setup_inputs(seed: int = 0) -> dict:
    key_list = jax.random.split(jax.random.key(seed), 5)
    states = bell_draw(key_list[0], (PROPS, NZ, NX, NY), 0.7, 4.0, ((0, 8), (1, 32)), jnp.float32)
    accepted = jax.random.randint(key_list[1], (1,), 0, PROPS).astype(jnp.int32)
    noise = bell_draw(key_list[2], (PROPS, NZ, NX, NY), 1.0, 5.0, ((0, 8), (1, 32)), jnp.float32)
    source = bell_draw(key_list[3], (NZ, NX, NY), 1.0, 6.0, ((0, 32),), jnp.float32)
    return dict(states=states, accepted=accepted, noise=noise, source=source)


OMEGA = 0.7
BETA = 0.4
SHRINK = math.sqrt(1.0 - BETA * BETA)
ZSCALE = 16.0

def shift_lower(values, axis):
    axis = values.ndim + axis
    count = values.shape[axis]
    kept = lax.slice_in_dim(values, 0, count - 1, axis=axis)
    return jnp.concatenate([jnp.zeros_like(lax.slice_in_dim(values, 0, 1, axis=axis)), kept], axis=axis)

def shift_upper(values, axis):
    axis = values.ndim + axis
    count = values.shape[axis]
    kept = lax.slice_in_dim(values, 1, count, axis=axis)
    return jnp.concatenate([kept, jnp.zeros_like(lax.slice_in_dim(values, 0, 1, axis=axis))], axis=axis)

def harmonic(first, second):
    return 2.0 * first * second / (first + second)

def coefficients(perm, padded, scale):
    inner_x = harmonic(perm[..., 1:, :], perm[..., :-1, :])
    west = jnp.concatenate([perm[..., :1, :], inner_x], axis=-2)
    east = jnp.concatenate([inner_x, perm[..., -1:, :]], axis=-2)
    inner_y = harmonic(perm[..., 1:], perm[..., :-1])
    south = jnp.concatenate([perm[..., :1], inner_y], axis=-1)
    north = jnp.concatenate([inner_y, perm[..., -1:]], axis=-1)
    below = harmonic(padded[..., :-2, :, :], perm)
    above = harmonic(padded[..., 2:, :, :], perm)
    zfactor = ZSCALE * scale
    parts = [west * scale, east * scale, south * scale, north * scale, below * zfactor, above * zfactor]
    diagonal = parts[0] + parts[1] + parts[2] + parts[3] + parts[4] + parts[5]
    return parts + [diagonal, OMEGA / diagonal]

def apply_op(values, padded, coefs):
    result = coefs[6] * values - coefs[0] * shift_lower(values, -2) - coefs[1] * shift_upper(values, -2)
    result = result - coefs[2] * shift_lower(values, -1) - coefs[3] * shift_upper(values, -1)
    return result - coefs[4] * padded[..., :-2, :, :] - coefs[5] * padded[..., 2:, :, :]

def sweep(values, right, coefs, pad_z):
    return values + coefs[7] * (right - apply_op(values, pad_z(values), coefs))

def sum_children(values):
    shape = values.shape
    split = values.reshape(shape[:-3] + (shape[-3] // 2, 2, shape[-2] // 2, 2, shape[-1] // 2, 2))
    return split.sum(axis=(-5, -3, -1))

def prolong(values):
    return jnp.repeat(jnp.repeat(jnp.repeat(values, 2, axis=-3), 2, axis=-2), 2, axis=-1)

def zero_pad(values):
    widths = [(0, 0)] * (values.ndim - 3) + [(1, 1), (0, 0), (0, 0)]
    return jnp.pad(values, widths)

def coarse_solve(right, perm, level, pad_z, pad_perm):
    coefs = coefficients(perm, pad_perm(perm), 4.0 ** level)
    start = coefs[7] * right
    return lax.fori_loop(0, COARSE_SWEEPS - 1, lambda step, values: sweep(values, right, coefs, pad_z), start)

def level_cycle(right, perm, level, pad_z, pad_perm, deeper):
    coefs = coefficients(perm, pad_perm(perm), 4.0 ** level)
    values = coefs[7] * right
    for step in range(SWEEPS - 1):
        values = sweep(values, right, coefs, pad_z)
    residue = right - apply_op(values, pad_z(values), coefs)
    update = deeper(sum_children(residue), sum_children(perm) * 0.125, level + 1)
    values = values + prolong(update)
    for step in range(SWEEPS):
        values = sweep(values, right, coefs, pad_z)
    return values

def local_cycle(right, perm, level):
    if level == LEVELS - 1:
        return coarse_solve(right, perm, level, zero_pad, zero_pad)
    return level_cycle(right, perm, level, zero_pad, zero_pad, local_cycle)

def reference(states, accepted, noise, source):
    current = lax.dynamic_index_in_dim(states, accepted[0], 0, keepdims=False)
    theta = SHRINK * current[None] + BETA * noise
    return lax.map(lambda field: local_cycle(source, jnp.exp(field), 0), theta)
```

```python
import functools
import math

import jax
import jax.numpy as jnp
from jax import lax
from jax.experimental import pallas as pl
from jax.experimental.pallas import tpu as pltpu
from jax.sharding import PartitionSpec as P

OMEGA = 0.7
BETA = 0.4
SHRINK = math.sqrt(1.0 - BETA * BETA)
KEEP = 1.0 - OMEGA
COARSE_SWEEPS = 64
F32 = jnp.float32
BF16 = jnp.bfloat16
MESH = pl.DeviceIdType.MESH


def iota(shape, axis):
    return lax.broadcasted_iota(jnp.int32, shape, axis)


def ones_where(mask):
    return jnp.where(mask, 1.0, 0.0).astype(BF16)


def dot3(x, matrix):
    rows = x.shape[0]
    hi = x.astype(BF16).astype(F32)
    rest = x - hi
    mid = rest.astype(BF16).astype(F32)
    stacked = jnp.concatenate([hi, mid, rest - mid], axis=0).astype(BF16)
    y = jnp.dot(stacked, matrix, preferred_element_type=F32)
    return y[:rows] + y[rows : 2 * rows] + y[2 * rows :]


def up(v, axis, by=1):
    return pltpu.roll(v, v.shape[axis] - by, axis)


def down(v, axis, by=1):
    return pltpu.roll(v, by, axis)


def harmonic(a, b):
    return 2.0 * a * b / (a + b)


def pair_rows(ref, rows):
    return ref[pl.ds(0, rows, stride=2), :] + ref[pl.ds(1, rows, stride=2), :]


def repeat_rows(ref, value):
    rows = value.shape[0]
    ref[pl.ds(0, rows, stride=2), :] = value
    ref[pl.ds(1, rows, stride=2), :] = value


def zup1(v):
    swapped = pltpu.roll(v, 64, 1)
    return jnp.where(iota(v.shape, 1) < 64, swapped, up(swapped, 0, 32))


def zdown1(v):
    swapped = pltpu.roll(v, 64, 1)
    return jnp.where(iota(v.shape, 1) < 64, down(swapped, 0, 32), swapped)


def zup2(v):
    moved = up(v, 1, 32)
    return jnp.where(iota(v.shape, 1) < 96, moved, up(moved, 0, 16))


def zdown2(v):
    moved = down(v, 1, 32)
    return jnp.where(iota(v.shape, 1) < 32, down(moved, 0, 16), moved)


def flat_coefs(perm, scale, nx, ny, zup, zdown, top):
    x = lax.rem(iota(perm.shape, 0), nx)
    y = lax.rem(iota(perm.shape, 1), ny)
    east = jnp.where(x < nx - 1, scale * harmonic(perm, up(perm, 0)), 0.0)
    north = jnp.where(y < ny - 1, scale * harmonic(perm, up(perm, 1)), 0.0)
    above = jnp.where(top, 0.0, (16.0 * scale) * harmonic(perm, zup(perm)))
    west, south, below = down(east, 0), down(north, 1), zdown(above)
    edges = jnp.where(x == 0, scale, 0.0) + jnp.where(x == nx - 1, scale, 0.0)
    edges = edges + jnp.where(y == 0, scale, 0.0) + jnp.where(y == ny - 1, scale, 0.0)
    diag = west + east + south + north + below + above + edges * perm
    return west, east, south, north, below, above, diag, OMEGA / diag


def around(v, c, zup, zdown):
    a = c[0] * down(v, 0) + c[1] * up(v, 0)
    b = c[2] * down(v, 1) + c[3] * up(v, 1)
    return (a + b) + (c[4] * zdown(v) + c[5] * zup(v))


def kernel(
    props, doms, acc_ref, states, noise, source, out_ref,
    rx, cur, nz, perm, src, cw, ce, cs, cn, cu, dg, cc, va, vb, tmp,
    perm1, right1, tmp1, co1, v1s, tmp2, gp2, gr2, tmp3, e2s,
    loc, s1, d1, s2, d2, ss, ds_, sn, dn, sf, df, sq, dq, sp, dp, sr, dr, sg, dgs,
):
    me = lax.axis_index("prop")
    dom = lax.axis_index("dom")

    def peer(o):
        return lax.rem(me + o, props)

    def slab(o):
        return lax.rem(dom + (o + doms), doms)

    def remote(from_ref, to_ref, send, recv, p, d):
        return pltpu.make_async_remote_copy(
            src_ref=from_ref, dst_ref=to_ref, send_sem=send, recv_sem=recv,
            device_id=(p, d), device_id_type=MESH,
        )

    load_noise = pltpu.make_async_copy(noise, nz, loc.at[0])
    load_source = pltpu.make_async_copy(source, src.at[pl.ds(4, 4)], loc.at[1])
    load_piece = pltpu.make_async_copy(states.at[me], rx.at[me], loc.at[2])
    load_piece.start()
    load_noise.start()
    load_source.start()

    barrier = pltpu.get_barrier_semaphore()
    for o in range(1, props):
        pl.semaphore_signal(barrier, inc=1, device_id=(peer(o), dom), device_id_type=MESH)

    def greet(o, carry):
        pl.semaphore_signal(barrier, inc=1, device_id=(me, slab(o)), device_id_type=MESH)
        return carry

    lax.fori_loop(1, doms, greet, 0)
    pl.semaphore_wait(barrier, props + doms - 2)

    sends1 = []
    for o in range(1, props):
        copy = remote(states.at[peer(o)], rx.at[me], s1.at[o - 1], d1.at[o - 1], peer(o), dom)
        copy.start()
        sends1.append(copy)
    sends_src = [
        remote(source, src.at[pl.ds(0, 4)], ss.at[0], ds_.at[0], me, slab(1)),
        remote(source, src.at[pl.ds(8, 4)], ss.at[1], ds_.at[1], me, slab(-1)),
    ]
    for copy in sends_src:
        copy.start()

    r01, l01 = iota((256, 128), 0), iota((256, 128), 1)
    c01 = ones_where(l01 == (r01 // 128) * 64 + lax.rem(r01, 128) // 2)
    r12, l12 = iota((128, 32), 0), iota((128, 32), 1)
    c12 = ones_where(l12 == lax.rem(r12, 64) // 2)
    r23, l23 = iota((128, 256), 0), iota((128, 256), 1)
    c23 = ones_where((r23 // 64 == l23 // 128) & (lax.rem(r23, 32) // 2 == lax.rem(l23, 16)))
    r32, l32 = iota((256, 128), 0), iota((256, 128), 1)
    c32 = ones_where((l32 // 64 == r32 // 128) & (lax.rem(l32, 32) // 2 == lax.rem(r32, 16)))
    r21, l21 = iota((128, 128), 0), iota((128, 128), 1)
    c21 = ones_where(lax.rem(l21, 64) // 2 == lax.rem(r21, 32))
    r10, l10 = iota((128, 256), 0), iota((128, 256), 1)
    c10 = ones_where((r10 // 64 == l10 // 128) & (lax.rem(r10, 64) == lax.rem(l10, 128) // 2))
    row, lane = iota((64, 128), 0), iota((64, 128), 1)
    east_in, north_in = row < 63, lane < 127
    edges = jnp.where(row == 0, 1.0, 0.0) + jnp.where(row == 63, 1.0, 0.0)
    edges = edges + jnp.where(lane == 0, 1.0, 0.0) + jnp.where(lane == 127, 1.0, 0.0)

    load_piece.wait()
    for copy in sends1:
        copy.wait_recv()
    cur[me] = rx[acc_ref[0]]
    sends2 = []
    for o in range(1, props):
        copy = remote(cur.at[me], cur.at[me], s2.at[o - 1], d2.at[o - 1], peer(o), dom)
        copy.start()
        sends2.append(copy)
    load_noise.wait()
    for copy in sends2:
        copy.wait_recv()

    theta = SHRINK * cur[...] + BETA * nz[...]
    perm[pl.ds(4, 4)] = jnp.exp(theta).reshape(4, 64, 128)

    near = [
        remote(perm.at[pl.ds(5, 3)], perm.at[pl.ds(1, 3)], sn.at[0], dn.at[0], me, slab(1)),
        remote(perm.at[pl.ds(4, 3)], perm.at[pl.ds(8, 3)], sn.at[1], dn.at[1], me, slab(-1)),
    ]
    far = [
        remote(perm.at[4], perm.at[0], sf.at[0], df.at[0], me, slab(1)),
        remote(perm.at[7], perm.at[11], sf.at[1], df.at[1], me, slab(-1)),
    ]
    for copy in near:
        copy.start()

    def restrict01(planes):
        sums = []
        for i in range(2):
            tmp[...] = planes[2 * i] + planes[2 * i + 1]
            sums.append(pair_rows(tmp, 32))
        return dot3(jnp.concatenate(sums, axis=1), c01)

    def restrict12(value):
        tmp2[pl.ds(0, 32)] = value
        return dot3(pair_rows(tmp2, 16), c12)

    own1 = 0.125 * restrict01([perm[k] for k in range(4, 8)])
    perm1[3] = own1
    sends_q = []
    for i, o in enumerate((1, -1, 2, -2, 3, -3)):
        copy = remote(perm1.at[3], perm1.at[3 - o], sq.at[i], dq.at[i], me, slab(o))
        copy.start()
        sends_q.append(copy)
    for copy in far:
        copy.start()
    gp2[dom] = 0.125 * restrict12(own1)

    def gather_to(buf, send, recv):
        def go(o, carry):
            remote(buf.at[dom], buf.at[dom], send, recv, me, slab(o)).start()
            return carry

        lax.fori_loop(1, doms, go, 0)

    def gather_wait(buf, send, recv):
        part = buf.at[pl.ds(0, doms - 1)]
        return remote(part, part, send, recv, me, slab(1))

    gather_to(gp2, sp.at[0], dp.at[0])

    def sides(k):
        p = perm[k]
        east = jnp.where(east_in, harmonic(p, up(p, 0)), 0.0)
        north = jnp.where(north_in, harmonic(p, up(p, 1)), 0.0)
        ce[k] = east
        cn[k] = north
        cw[k] = down(east, 0)
        cs[k] = down(north, 1)

    inside_low = jnp.where(dom == 0, 0.0, 16.0)
    inside_high = jnp.where(dom == doms - 1, 0.0, 16.0)

    def face(k):
        factor = {3: inside_low, 7: inside_high}.get(k, 16.0)
        cu[k] = factor * harmonic(perm[k], perm[k + 1])

    def finish(k):
        diag = cw[k] + ce[k] + cs[k] + cn[k] + cu[k - 1] + cu[k] + edges * perm[k]
        dg[k] = diag
        scaled = OMEGA / diag
        cc[k] = scaled
        va[k] = scaled * src[k]

    def around0(v, k):
        x = v[k]
        a = cw[k] * down(x, 0) + ce[k] * up(x, 0)
        b = cs[k] * down(x, 1) + cn[k] * up(x, 1)
        return x, (a + b) + (cu[k - 1] * v[k - 1] + cu[k] * v[k + 1])

    def sweep0(v, k):
        x, total = around0(v, k)
        return KEEP * x + cc[k] * (src[k] + total)

    for k in range(4, 8):
        sides(k)
    for k in range(4, 7):
        face(k)
    load_source.wait()
    for copy in sends_src:
        copy.wait_recv()
    finish(5)
    finish(6)
    for copy in near:
        copy.wait_recv()
    for k in (2, 3, 8, 9):
        sides(k)
    for k in (1, 2, 3, 7, 8, 9):
        face(k)
    for k in (2, 3, 4, 7, 8, 9):
        finish(k)
    for k in range(3, 9):
        vb[k] = sweep0(va, k)
    rest = []
    for k in range(4, 8):
        x, total = around0(vb, k)
        rest.append(src[k] - dg[k] * x + total)
    right1[2] = restrict01(rest)
    sends_r = []
    for i, o in enumerate((1, -1, 2, -2)):
        copy = remote(right1.at[2], right1.at[2 - o], sr.at[i], dr.at[i], me, slab(o))
        copy.start()
        sends_r.append(copy)

    for copy in sends_q:
        copy.wait_recv()
    wide = perm1[...].reshape(7 * 32, 128)
    pair = lax.rem(dom + (doms - 3) + iota(wide.shape, 0) // 32, doms)
    top1 = (pair == doms - 1) & (iota(wide.shape, 1) >= 64)
    for i, value in enumerate(flat_coefs(wide, 4.0, 32, 64, zup1, zdown1, top1)):
        co1[i] = value[32:192]
    for copy in far:
        copy.wait_recv()
    for k in (1, 10):
        sides(k)
    for k in (0, 10):
        face(k)
    for k in (1, 10):
        finish(k)
    for k in (2, 9):
        vb[k] = sweep0(va, k)

    for copy in sends_r:
        copy.wait_recv()
    b1 = right1[...].reshape(160, 128)
    first = co1[7] * b1
    v1 = KEEP * first + co1[7] * (b1 + around(first, co1, zup1, zdown1))
    v1s[...] = v1
    res1 = b1 - co1[6] * v1 + around(v1, co1, zup1, zdown1)
    gr2[dom] = restrict12(res1[64:96])
    gather_to(gr2, sg.at[0], dgs.at[0])

    def whole(buf):
        groups = []
        for g in range(doms // 4):
            groups.append(jnp.concatenate([buf[4 * g + i] for i in range(4)], axis=1))
        return jnp.concatenate(groups, axis=0)

    rows3, lanes3 = iota((64, 256), 0), iota((64, 256), 1)
    mask3 = rows3 // 8 == lax.rem(lanes3, 128) // 16

    def restrict23(value):
        tmp3[...] = value
        y = jnp.where(mask3, dot3(pair_rows(tmp3, 64), c23), 0.0)
        total = y[0:8]
        for g in range(1, 8):
            total = total + y[8 * g : 8 * g + 8]
        return total[:, :128], total[:, 128:]

    gather_wait(gp2, sp.at[0], dp.at[0]).wait_recv()
    p2 = whole(gp2)
    top2 = (iota(p2.shape, 0) >= 112) & (iota(p2.shape, 1) >= 96)
    co2 = flat_coefs(p2, 16.0, 16, 32, zup2, zdown2, top2)
    pa, pb = restrict23(p2)
    pa, pb = 0.125 * pa, 0.125 * pb
    x3, lane3 = iota((8, 128), 0), iota((8, 128), 1)
    y3 = lax.rem(lane3, 16)
    scale = 64.0
    edges3 = jnp.where(x3 == 0, scale, 0.0) + jnp.where(x3 == 7, scale, 0.0)
    edges3 = edges3 + jnp.where(y3 == 0, scale, 0.0) + jnp.where(y3 == 15, scale, 0.0)

    def sides3(p):
        east = jnp.where(x3 < 7, scale * harmonic(p, up(p, 0)), 0.0)
        north = jnp.where(y3 < 15, scale * harmonic(p, up(p, 1)), 0.0)
        return [down(east, 0), east, down(north, 1), north]

    mid = (16.0 * scale) * harmonic(pa, pb)
    high = jnp.where(lane3 < 112, (16.0 * scale) * harmonic(pb, up(pa, 1, 16)), 0.0)
    low = down(high, 1, 16)
    ca = sides3(pa) + [low, mid]
    cb = sides3(pb) + [mid, high]

    def scaled3(c, p):
        inverse = OMEGA / ((c[0] + c[1]) + (c[2] + c[3]) + (c[4] + c[5]) + edges3 * p)
        return inverse, [inverse * value for value in c]

    ia, ca = scaled3(ca, pa)
    ib, cb = scaled3(cb, pb)

    gather_wait(gr2, sg.at[0], dgs.at[0]).wait_recv()
    b2 = whole(gr2)
    first = co2[7] * b2
    v2 = KEEP * first + co2[7] * (b2 + around(first, co2, zup2, zdown2))
    res2 = b2 - co2[6] * v2 + around(v2, co2, zup2, zdown2)
    ra, rb = restrict23(res2)
    ga, gb = ia * ra, ib * rb

    def near3(v, c, base):
        a = c[0] * down(v, 0) + c[1] * up(v, 0)
        b = c[2] * down(v, 1) + c[3] * up(v, 1)
        return (a + b) + (KEEP * v + base)

    def coarse(step, pair_):
        a, b = pair_
        new_a = near3(a, ca, ga) + (ca[4] * down(b, 1, 16) + ca[5] * b)
        new_b = near3(b, cb, gb) + (cb[4] * a + cb[5] * up(a, 1, 16))
        return new_a, new_b

    ea, eb = lax.fori_loop(0, COARSE_SWEEPS - 1, coarse, (ga, gb))
    e3 = jnp.concatenate([jnp.concatenate([ea, eb], axis=1)] * 8, axis=0)
    repeat_rows(tmp3, dot3(jnp.where(mask3, e3, 0.0), c32))
    v2 = v2 + tmp3[...]
    for _ in range(2):
        v2 = KEEP * v2 + co2[7] * (b2 + around(v2, co2, zup2, zdown2))
    e2s[...] = v2

    parts = []
    lane2 = iota((16, 128), 1) // 32
    for j in range(-2, 3):
        z = slab(j)
        value = e2s[pl.ds(pl.multiple_of((z // 4) * 16, 16), 16), :]
        parts.append(jnp.where(lane2 == lax.rem(z, 4), value, 0.0))
    repeat_rows(tmp1, dot3(jnp.concatenate(parts, axis=0), c21))
    v1 = v1s[...] + tmp1[...]
    b1 = right1[...].reshape(160, 128)
    for _ in range(2):
        v1 = KEEP * v1 + co1[7] * (b1 + around(v1, co1, zup1, zdown1))

    fine = dot3(v1[32:128], c10)
    for k, i, half in ((2, 0, 1), (4, 1, 0), (6, 1, 1), (8, 2, 0)):
        repeat_rows(tmp, fine[32 * i : 32 * i + 32, 128 * half : 128 * half + 128])
        add = tmp[...]
        vb[k] = vb[k] + add
        vb[k + 1] = vb[k + 1] + add
    for k in range(3, 9):
        va[k] = sweep0(vb, k)
    for k in range(4, 8):
        out_ref[k - 4] = sweep0(va, k)

    for copies in (sends1, sends2, sends_src, near, far, sends_q, sends_r):
        for copy in copies:
            copy.wait_send()
    gather_wait(gp2, sp.at[0], dp.at[0]).wait_send()
    gather_wait(gr2, sg.at[0], dgs.at[0]).wait_send()


def body(states, accepted, noise, source):
    props, doms = lax.axis_size("prop"), lax.axis_size("dom")
    rows = 256 // props
    dma = pltpu.SemaphoreType.DMA
    plane = lambda n: pltpu.VMEM((n, 64, 128), F32)
    scratch = [
        pltpu.VMEM((props, rows, 128), F32),
        pltpu.VMEM((props, rows, 128), F32),
        pltpu.VMEM((props, rows, 128), F32),
        plane(12), plane(12),
        plane(12), plane(12), plane(12), plane(12), plane(12), plane(12), plane(12),
        plane(12), plane(12),
        pltpu.VMEM((64, 128), F32),
        pltpu.VMEM((7, 32, 128), F32),
        pltpu.VMEM((5, 32, 128), F32),
        pltpu.VMEM((160, 128), F32),
        pltpu.VMEM((8, 160, 128), F32),
        pltpu.VMEM((160, 128), F32),
        pltpu.VMEM((32, 128), F32),
        pltpu.VMEM((doms, 16, 32), F32),
        pltpu.VMEM((doms, 16, 32), F32),
        pltpu.VMEM((128, 128), F32),
        pltpu.VMEM((128, 128), F32),
        dma((3,)),
        dma((props - 1,)), dma((props - 1,)), dma((props - 1,)), dma((props - 1,)),
        dma((2,)), dma((2,)), dma((2,)), dma((2,)), dma((2,)), dma((2,)),
        dma((6,)), dma((6,)), dma((1,)), dma((1,)), dma((4,)), dma((4,)), dma((1,)), dma((1,)),
    ]
    hbm = pl.BlockSpec(memory_space=pl.ANY)
    out = pl.pallas_call(
        functools.partial(kernel, props, doms),
        out_shape=jax.ShapeDtypeStruct((4, 64, 128), F32),
        in_specs=[pl.BlockSpec(memory_space=pltpu.SMEM), hbm, hbm, hbm],
        out_specs=pl.BlockSpec(memory_space=pltpu.VMEM),
        scratch_shapes=scratch,
        compiler_params=pltpu.CompilerParams(collective_id=0, has_side_effects=True),
        name="mcmc_step",
    )(
        accepted,
        states.reshape(props, rows, 128),
        noise.reshape(props, rows, 128),
        source,
    )
    return out[None]


def solution(mesh):
    in_specs = (
        P("prop", "dom", None, None),
        P(),
        P("prop", "dom", None, None),
        P("dom", None, None),
    )
    out_specs = P("prop", "dom", None, None)
    return jax.shard_map(body, mesh=mesh, in_specs=in_specs, out_specs=out_specs, check_vma=False)
```

```python
import functools
import math

import jax
import jax.numpy as jnp
from jax import lax
from jax.experimental import pallas as pl
from jax.experimental.pallas import tpu as pltpu
from jax.sharding import PartitionSpec as P

OMEGA = 0.7
BETA = 0.4
SHRINK = math.sqrt(1.0 - BETA * BETA)
KEEP = 1.0 - OMEGA
COARSE_SWEEPS = 64
F32 = jnp.float32
BF16 = jnp.bfloat16
MESH = pl.DeviceIdType.MESH


def iota(shape, axis):
    return lax.broadcasted_iota(jnp.int32, shape, axis)


def ones_where(mask):
    return jnp.where(mask, 1.0, 0.0).astype(BF16)


def dot3(x, matrix):
    rows = x.shape[0]
    hi = x.astype(BF16).astype(F32)
    rest = x - hi
    mid = rest.astype(BF16).astype(F32)
    stacked = jnp.concatenate([hi, mid, rest - mid], axis=0).astype(BF16)
    y = jnp.dot(stacked, matrix, preferred_element_type=F32)
    return y[:rows] + y[rows : 2 * rows] + y[2 * rows :]


def up(v, axis, by=1):
    return pltpu.roll(v, v.shape[axis] - by, axis)


def down(v, axis, by=1):
    return pltpu.roll(v, by, axis)


def harmonic(a, b):
    return 2.0 * a * b / (a + b)


def pair_rows(ref, rows):
    return ref[pl.ds(0, rows, stride=2), :] + ref[pl.ds(1, rows, stride=2), :]


def repeat_rows(ref, value):
    rows = value.shape[0]
    ref[pl.ds(0, rows, stride=2), :] = value
    ref[pl.ds(1, rows, stride=2), :] = value


def zup1(v):
    swapped = pltpu.roll(v, 64, 1)
    return jnp.where(iota(v.shape, 1) < 64, swapped, up(swapped, 0, 32))


def zdown1(v):
    swapped = pltpu.roll(v, 64, 1)
    return jnp.where(iota(v.shape, 1) < 64, down(swapped, 0, 32), swapped)


def xup2(v):
    moved = up(v, 1, 32)
    return jnp.where(iota(v.shape, 1) < 96, moved, up(moved, 0))


def xdown2(v):
    moved = down(v, 1, 32)
    return jnp.where(iota(v.shape, 1) < 32, down(moved, 0), moved)


def zup2(v):
    return up(v, 0, 4)


def zdown2(v):
    return down(v, 0, 4)


def xup1(v):
    return up(v, 0)


def xdown1(v):
    return down(v, 0)


MOVES1 = (xdown1, xup1, zdown1, zup1)
MOVES2 = (xdown2, xup2, zdown2, zup2)


def flat_coefs(perm, scale, x, y, nx, ny, moves, top):
    xdown, xup, zdown, zup = moves
    east = jnp.where(x < nx - 1, scale * harmonic(perm, xup(perm)), 0.0)
    north = jnp.where(y < ny - 1, scale * harmonic(perm, up(perm, 1)), 0.0)
    above = jnp.where(top, 0.0, (16.0 * scale) * harmonic(perm, zup(perm)))
    west, south, below = xdown(east), down(north, 1), zdown(above)
    edges = jnp.where(x == 0, scale, 0.0) + jnp.where(x == nx - 1, scale, 0.0)
    edges = edges + jnp.where(y == 0, scale, 0.0) + jnp.where(y == ny - 1, scale, 0.0)
    diag = west + east + south + north + below + above + edges * perm
    return west, east, south, north, below, above, diag, OMEGA / diag


def around(v, c, moves):
    xdown, xup, zdown, zup = moves
    a = c[0] * xdown(v) + c[1] * xup(v)
    b = c[2] * down(v, 1) + c[3] * up(v, 1)
    return (a + b) + (c[4] * zdown(v) + c[5] * zup(v))


def sweep(v, right, c, moves):
    return KEEP * v + c[7] * (right + around(v, c, moves))


def shifted(pair, parity, offset, cache):
    dx, dy, dz = offset
    source = (parity + dz) % 2
    lanes = dy + 16 * ((parity + dz - source) // 2)
    if (source, lanes) not in cache:
        value = pair[source]
        cache[source, lanes] = value if lanes == 0 else pltpu.roll(value, -lanes % 128, 1)
    value = cache[source, lanes]
    return value if dx == 0 else pltpu.roll(value, -dx % 8, 0)


def tree_sum(terms):
    while len(terms) > 1:
        terms = [a + b for a, b in zip(terms[::2], terms[1::2])] + terms[len(terms) & ~1 :]
    return terms[0]


def apply3(operator, pair, base):
    cache = {}
    out = []
    for parity in range(2):
        terms = [base[parity]]
        terms += [c[parity] * shifted(pair, parity, o, cache) for o, c in operator.items()]
        out.append(tree_sum(terms))
    return tuple(out)


def compose3(first, second):
    out = {}
    for o2, c2 in second.items():
        cache = {}
        for o1, c1 in first.items():
            term = [c1[parity] * shifted(c2, parity, o1, cache) for parity in range(2)]
            key = tuple(a + b for a, b in zip(o1, o2))
            out[key] = [a + b for a, b in zip(out[key], term)] if key in out else term
    return out


def kernel(
    props, doms, acc_ref, states, noise, source, out_ref,
    rx, cur, nz, perm, src, cw, ce, cs, cn, cu, dg, cc, va, vb, tmp,
    perm1, right1, tmp1, co1, v1s, tmp2, gp2, gr2, co2, m2, tmp3, e2s,
    loc, s1, d1, s2, d2, ss, ds_, sn, dn, sf, df, sq, dq, sp, dp, sr, dr, sg, dgs,
):
    me = lax.axis_index("prop")
    dom = lax.axis_index("dom")

    def peer(o):
        return lax.rem(me + o, props)

    def slab(o):
        return lax.rem(dom + (o + doms), doms)

    def remote(from_ref, to_ref, send, recv, p, d):
        return pltpu.make_async_remote_copy(
            src_ref=from_ref, dst_ref=to_ref, send_sem=send, recv_sem=recv,
            device_id=(p, d), device_id_type=MESH,
        )

    load_noise = pltpu.make_async_copy(noise, nz, loc.at[0])
    load_source = pltpu.make_async_copy(source, src.at[pl.ds(4, 4)], loc.at[1])
    load_piece = pltpu.make_async_copy(states.at[me], rx.at[me], loc.at[2])
    load_piece.start()
    load_noise.start()
    load_source.start()

    barrier = pltpu.get_barrier_semaphore()
    for o in range(1, props):
        pl.semaphore_signal(barrier, inc=1, device_id=(peer(o), dom), device_id_type=MESH)

    def greet(o, carry):
        pl.semaphore_signal(barrier, inc=1, device_id=(me, slab(o)), device_id_type=MESH)
        return carry

    lax.fori_loop(1, doms, greet, 0)
    pl.semaphore_wait(barrier, props + doms - 2)

    sends1 = []
    for o in range(1, props):
        copy = remote(states.at[peer(o)], rx.at[me], s1.at[o - 1], d1.at[o - 1], peer(o), dom)
        copy.start()
        sends1.append(copy)
    sends_src = [
        remote(source, src.at[pl.ds(0, 4)], ss.at[0], ds_.at[0], me, slab(1)),
        remote(source, src.at[pl.ds(8, 4)], ss.at[1], ds_.at[1], me, slab(-1)),
    ]
    for copy in sends_src:
        copy.start()

    r01, l01 = iota((256, 128), 0), iota((256, 128), 1)
    c01 = ones_where(l01 == (r01 >> 1))
    r12, l12 = iota((512, 128), 0), iota((512, 128), 1)
    c12 = ones_where(((r12 >> 7) == (l12 >> 5)) & (((r12 & 63) >> 1) == (l12 & 31)))
    r23, l23 = iota((128, 256), 0), iota((128, 256), 1)
    c23 = ones_where(((r23 >> 6) == (l23 >> 7)) & (((r23 & 31) >> 1) == (l23 & 15)))
    r32, l32 = iota((256, 128), 0), iota((256, 128), 1)
    c32 = ones_where(((l32 >> 6) == (r32 >> 7)) & (((l32 & 31) >> 1) == (r32 & 15)))
    r21, l21 = iota((128, 512), 0), iota((128, 512), 1)
    c21 = ones_where(((r21 >> 5) == (l21 >> 7)) & ((r21 & 31) == ((l21 & 63) >> 1)))
    r10, l10 = iota((128, 256), 0), iota((128, 256), 1)
    c10 = ones_where(r10 == (l10 >> 1))
    row, lane = iota((64, 128), 0), iota((64, 128), 1)
    east_in, north_in = row < 63, lane < 127
    edges = jnp.where(row == 0, 1.0, 0.0) + jnp.where(row == 63, 1.0, 0.0)
    edges = edges + jnp.where(lane == 0, 1.0, 0.0) + jnp.where(lane == 127, 1.0, 0.0)

    load_piece.wait()
    for copy in sends1:
        copy.wait_recv()
    cur[me] = rx[acc_ref[0]]
    sends2 = []
    for o in range(1, props):
        copy = remote(cur.at[me], cur.at[me], s2.at[o - 1], d2.at[o - 1], peer(o), dom)
        copy.start()
        sends2.append(copy)
    load_noise.wait()
    for copy in sends2:
        copy.wait_recv()

    theta = SHRINK * cur[...] + BETA * nz[...]
    perm[pl.ds(4, 4)] = jnp.exp(theta).reshape(4, 64, 128)

    near = [
        remote(perm.at[pl.ds(5, 3)], perm.at[pl.ds(1, 3)], sn.at[0], dn.at[0], me, slab(1)),
        remote(perm.at[pl.ds(4, 3)], perm.at[pl.ds(8, 3)], sn.at[1], dn.at[1], me, slab(-1)),
    ]
    far = [
        remote(perm.at[4], perm.at[0], sf.at[0], df.at[0], me, slab(1)),
        remote(perm.at[7], perm.at[11], sf.at[1], df.at[1], me, slab(-1)),
    ]
    for copy in near:
        copy.start()

    def restrict01(planes):
        sums = []
        for i in range(2):
            tmp[...] = planes[2 * i] + planes[2 * i + 1]
            sums.append(pair_rows(tmp, 32))
        return dot3(jnp.concatenate(sums, axis=1), c01)

    def restrict12(value):
        tmp2[...] = value
        parts = []
        for q in range(4):
            low = tmp2[pl.ds(2 * q, 4, stride=8), :]
            parts.append(low + tmp2[pl.ds(2 * q + 1, 4, stride=8), :])
        return dot3(jnp.concatenate(parts, axis=1), c12)

    own1 = 0.125 * restrict01([perm[k] for k in range(4, 8)])
    perm1[3] = own1
    sends_q = []
    for i, o in enumerate((1, -1, 2, -2, 3, -3)):
        copy = remote(perm1.at[3], perm1.at[3 - o], sq.at[i], dq.at[i], me, slab(o))
        copy.start()
        sends_q.append(copy)
    gp2[dom] = 0.125 * restrict12(own1)

    def gather_to(buf, send, recv):
        def go(o, carry):
            remote(buf.at[dom], buf.at[dom], send, recv, me, slab(o)).start()
            return carry

        lax.fori_loop(1, doms, go, 0)

    def gather_wait(buf, send, recv):
        part = buf.at[pl.ds(0, doms - 1)]
        return remote(part, part, send, recv, me, slab(1))

    def sides(k):
        p = perm[k]
        east = jnp.where(east_in, harmonic(p, up(p, 0)), 0.0)
        north = jnp.where(north_in, harmonic(p, up(p, 1)), 0.0)
        ce[k] = east
        cn[k] = north
        cw[k] = down(east, 0)
        cs[k] = down(north, 1)

    inside_low = jnp.where(dom == 0, 0.0, 16.0)
    inside_high = jnp.where(dom == doms - 1, 0.0, 16.0)

    def face(k):
        factor = {3: inside_low, 7: inside_high}.get(k, 16.0)
        cu[k] = factor * harmonic(perm[k], perm[k + 1])

    def finish(k):
        diag = cw[k] + ce[k] + cs[k] + cn[k] + cu[k - 1] + cu[k] + edges * perm[k]
        dg[k] = diag
        scaled = OMEGA / diag
        cc[k] = scaled
        va[k] = scaled * src[k]

    def around0(v, k):
        x = v[k]
        a = cw[k] * down(x, 0) + ce[k] * up(x, 0)
        b = cs[k] * down(x, 1) + cn[k] * up(x, 1)
        return x, (a + b) + (cu[k - 1] * v[k - 1] + cu[k] * v[k + 1])

    def sweep0(v, k):
        x, total = around0(v, k)
        return KEEP * x + cc[k] * (src[k] + total)

    for k in range(4, 8):
        sides(k)
    for k in range(4, 7):
        face(k)
    load_source.wait()
    for copy in sends_src:
        copy.wait_recv()
    finish(5)
    finish(6)
    for copy in near:
        copy.wait_recv()
    for k in (2, 3, 8, 9):
        sides(k)
    for k in (1, 2, 3, 7, 8, 9):
        face(k)
    for k in (2, 3, 4, 7, 8, 9):
        finish(k)
    for k in range(3, 9):
        vb[k] = sweep0(va, k)
    rest = []
    for k in range(4, 8):
        x, total = around0(vb, k)
        rest.append(src[k] - dg[k] * x + total)
    right1[2] = restrict01(rest)
    sends_r = []
    for i, o in enumerate((1, -1, 2, -2)):
        copy = remote(right1.at[2], right1.at[2 - o], sr.at[i], dr.at[i], me, slab(o))
        copy.start()
        sends_r.append(copy)
    for copy in far:
        copy.start()
    gather_to(gp2, sp.at[0], dp.at[0])

    for copy in sends_q:
        copy.wait_recv()
    wide = perm1[...].reshape(7 * 32, 128)
    wide_row, wide_lane = iota(wide.shape, 0), iota(wide.shape, 1)
    pair = (dom + (doms - 3) + (wide_row >> 5)) & (doms - 1)
    top1 = (pair == doms - 1) & (wide_lane >= 64)
    coefs1 = flat_coefs(wide, 4.0, wide_row & 31, wide_lane & 63, 32, 64, MOVES1, top1)
    for i, value in enumerate(coefs1):
        co1[i] = value[32:192]

    for copy in sends_r[:2]:
        copy.wait_recv()
    b1 = right1[pl.ds(1, 3)].reshape(96, 128)
    inner = [co1[i, 32:128] for i in range(8)]
    v1 = sweep(inner[7] * b1, b1, inner, MOVES1)
    res1 = b1 - inner[6] * v1 + around(v1, inner, MOVES1)
    gr2[dom] = restrict12(res1[32:64])
    gather_to(gr2, sg.at[0], dgs.at[0])

    for copy in sends_r[2:]:
        copy.wait_recv()
    b1 = right1[...].reshape(160, 128)
    all1 = [co1[i] for i in range(8)]
    v1s[...] = sweep(all1[7] * b1, b1, all1, MOVES1)
    for copy in far:
        copy.wait_recv()
    for k in (1, 10):
        sides(k)
    for k in (0, 10):
        face(k)
    for k in (1, 10):
        finish(k)
    for k in (2, 9):
        vb[k] = sweep0(va, k)

    row8, row128 = iota((8, 128), 0), iota((128, 128), 0)
    lane8, lane128 = iota((8, 128), 1), iota((128, 128), 1)
    group = [(iota((8, 256), 1) & 127) >> 4 == g for g in range(8)]

    def restrict23(value):
        both = value + up(value, 0, 4)
        moved = down(both, 0, 4)
        parts = []
        for g in range(8):
            low, high = both[16 * g : 16 * g + 8], moved[16 * g + 8 : 16 * g + 16]
            parts.append(jnp.where(row8 < 4, low, high))
        y = dot3(jnp.concatenate(parts, axis=0), c23)
        total = tree_sum([jnp.where(group[g], y[8 * g : 8 * g + 8], 0.0) for g in range(8)])
        for parity in range(2):
            for q in range(2):
                piece = total[4 * parity : 4 * parity + 4, 128 * q : 128 * q + 128]
                tmp3[pl.ds(8 * parity + q, 4, stride=2), :] = piece
        return tmp3[pl.ds(0, 8), :], tmp3[pl.ds(8, 8), :]

    def prolong23(pair_):
        tmp3[pl.ds(0, 8), :] = pair_[0]
        tmp3[pl.ds(8, 8), :] = pair_[1]
        halves = []
        for q in range(2):
            rows = [tmp3[pl.ds(8 * parity + q, 4, stride=2), :] for parity in range(2)]
            halves.append(jnp.concatenate(rows, axis=0))
        e = jnp.concatenate(halves, axis=1)
        y = dot3(jnp.concatenate([jnp.where(m, e, 0.0) for m in group], axis=0), c32)
        parts = []
        for g in range(8):
            value = y[8 * g : 8 * g + 8]
            other = pltpu.roll(value, 4, 0)
            parts.append(jnp.where(row8 < 4, value, other))
            parts.append(jnp.where(row8 < 4, other, value))
        return jnp.concatenate(parts, axis=0)

    gather_wait(gp2, sp.at[0], dp.at[0]).wait_recv()
    p2 = gp2[...].reshape(128, 128)
    x2 = 4 * (row128 & 3) + (lane128 >> 5)
    coefs2 = flat_coefs(p2, 16.0, x2, lane128 & 31, 16, 32, MOVES2, row128 >= 124)
    for i, value in enumerate(coefs2):
        co2[i] = value
    pa, pb = restrict23(p2)
    pa, pb = 0.125 * pa, 0.125 * pb
    y3 = lane8 & 15
    scale = 64.0
    edges3 = jnp.where(row8 == 0, scale, 0.0) + jnp.where(row8 == 7, scale, 0.0)
    edges3 = edges3 + jnp.where(y3 == 0, scale, 0.0) + jnp.where(y3 == 15, scale, 0.0)

    def sides3(p):
        east = jnp.where(row8 < 7, scale * harmonic(p, up(p, 0)), 0.0)
        north = jnp.where(y3 < 15, scale * harmonic(p, up(p, 1)), 0.0)
        return [down(east, 0), east, down(north, 1), north]

    mid = (16.0 * scale) * harmonic(pa, pb)
    high = jnp.where(lane8 < 112, (16.0 * scale) * harmonic(pb, up(pa, 1, 16)), 0.0)
    low = down(high, 1, 16)
    ca = sides3(pa) + [low, mid]
    cb = sides3(pb) + [mid, high]

    def scaled3(c, p):
        total = (c[0] + c[1]) + (c[2] + c[3]) + (c[4] + c[5]) + edges3 * p
        inverse = OMEGA / total
        return inverse, [inverse * value for value in c]

    ia, ca = scaled3(ca, pa)
    ib, cb = scaled3(cb, pb)
    keep = jnp.full((8, 128), KEEP, F32)
    offsets = ((-1, 0, 0), (1, 0, 0), (0, -1, 0), (0, 1, 0), (0, 0, -1), (0, 0, 1))
    once = {(0, 0, 0): (keep, keep)}
    once.update({o: (a, b) for o, a, b in zip(offsets, ca, cb)})
    twice = compose3(once, once)
    keys = list(twice)
    for i, key in enumerate(keys):
        for parity in range(2):
            m2[parity, i] = twice[key][parity]

    gather_wait(gr2, sg.at[0], dgs.at[0]).wait_recv()
    b2 = gr2[...].reshape(128, 128)
    all2 = [co2[i] for i in range(8)]
    v2 = sweep(all2[7] * b2, b2, all2, MOVES2)
    res2 = b2 - all2[6] * v2 + around(v2, all2, MOVES2)
    ra, rb = restrict23(res2)
    base = (ia * ra, ib * rb)
    base = apply3(once, base, base)

    def coarse(step, value):
        operator = {key: (m2[0, i], m2[1, i]) for i, key in enumerate(keys)}
        return apply3(operator, value, base)

    v2 = v2 + prolong23(lax.fori_loop(0, (COARSE_SWEEPS - 2) // 2, coarse, base))
    for _ in range(2):
        v2 = sweep(v2, b2, all2, MOVES2)
    e2s[...] = v2

    parts = []
    for j in range(-2, 3):
        z = slab(j)
        value = e2s[pl.ds(pl.multiple_of((z // 2) * 8, 8), 8), :]
        parts.append(jnp.where(lax.rem(z, 2) == 0, value, pltpu.roll(value, 4, 0)))
    wide1 = dot3(jnp.concatenate(parts, axis=0), c21)
    for j in range(5):
        for q in range(4):
            piece = wide1[8 * j : 8 * j + 4, 128 * q : 128 * q + 128]
            for i in range(2):
                tmp1[pl.ds(32 * j + 2 * q + i, 4, stride=8), :] = piece
    v1 = v1s[...] + tmp1[...]
    b1 = right1[...].reshape(160, 128)
    all1 = [co1[i] for i in range(8)]
    for _ in range(2):
        v1 = sweep(v1, b1, all1, MOVES1)

    fine = dot3(v1[32:128], c10)
    for k, i, half in ((2, 0, 1), (4, 1, 0), (6, 1, 1), (8, 2, 0)):
        repeat_rows(tmp, fine[32 * i : 32 * i + 32, 128 * half : 128 * half + 128])
        add = tmp[...]
        vb[k] = vb[k] + add
        vb[k + 1] = vb[k + 1] + add
    for k in range(3, 9):
        va[k] = sweep0(vb, k)
    for k in range(4, 8):
        out_ref[k - 4] = sweep0(va, k)

    for copies in (sends1, sends2, sends_src, near, far, sends_q, sends_r):
        for copy in copies:
            copy.wait_send()
    gather_wait(gp2, sp.at[0], dp.at[0]).wait_send()
    gather_wait(gr2, sg.at[0], dgs.at[0]).wait_send()


def body(states, accepted, noise, source):
    props, doms = lax.axis_size("prop"), lax.axis_size("dom")
    rows = 256 // props
    dma = pltpu.SemaphoreType.DMA
    plane = lambda n: pltpu.VMEM((n, 64, 128), F32)
    scratch = [
        pltpu.VMEM((props, rows, 128), F32),
        pltpu.VMEM((props, rows, 128), F32),
        pltpu.VMEM((props, rows, 128), F32),
        plane(12), plane(12),
        plane(12), plane(12), plane(12), plane(12), plane(12), plane(12), plane(12),
        plane(12), plane(12),
        pltpu.VMEM((64, 128), F32),
        pltpu.VMEM((7, 32, 128), F32),
        pltpu.VMEM((5, 32, 128), F32),
        pltpu.VMEM((160, 128), F32),
        pltpu.VMEM((8, 160, 128), F32),
        pltpu.VMEM((160, 128), F32),
        pltpu.VMEM((32, 128), F32),
        pltpu.VMEM((doms, 4, 128), F32),
        pltpu.VMEM((doms, 4, 128), F32),
        pltpu.VMEM((8, 128, 128), F32),
        pltpu.VMEM((2, 25, 8, 128), F32),
        pltpu.VMEM((16, 128), F32),
        pltpu.VMEM((128, 128), F32),
        dma((3,)),
        dma((props - 1,)), dma((props - 1,)), dma((props - 1,)), dma((props - 1,)),
        dma((2,)), dma((2,)), dma((2,)), dma((2,)), dma((2,)), dma((2,)),
        dma((6,)), dma((6,)), dma((1,)), dma((1,)), dma((4,)), dma((4,)), dma((1,)), dma((1,)),
    ]
    hbm = pl.BlockSpec(memory_space=pl.ANY)
    out = pl.pallas_call(
        functools.partial(kernel, props, doms),
        out_shape=jax.ShapeDtypeStruct((4, 64, 128), F32),
        in_specs=[pl.BlockSpec(memory_space=pltpu.SMEM), hbm, hbm, hbm],
        out_specs=pl.BlockSpec(memory_space=pltpu.VMEM),
        scratch_shapes=scratch,
        compiler_params=pltpu.CompilerParams(collective_id=0, has_side_effects=True),
        name="mcmc_step",
    )(
        accepted,
        states.reshape(props, rows, 128),
        noise.reshape(props, rows, 128),
        source,
    )
    return out[None]


def solution(mesh):
    in_specs = (
        P("prop", "dom", None, None),
        P(),
        P("prop", "dom", None, None),
        P("dom", None, None),
    )
    out_specs = P("prop", "dom", None, None)
    return jax.shard_map(body, mesh=mesh, in_specs=in_specs, out_specs=out_specs, check_vma=False)
```

```python
import functools
import math

import jax
import jax.numpy as jnp
from jax import lax
from jax.experimental import pallas as pl
from jax.experimental.pallas import tpu as pltpu
from jax.sharding import PartitionSpec as P

OMEGA = 0.7
BETA = 0.4
SHRINK = math.sqrt(1.0 - BETA * BETA)
KEEP = 1.0 - OMEGA
COARSE_SWEEPS = 64
F32 = jnp.float32
BF16 = jnp.bfloat16
MESH = pl.DeviceIdType.MESH


def iota(shape, axis):
    return lax.broadcasted_iota(jnp.int32, shape, axis)


def ones_where(mask):
    return jnp.where(mask, 1.0, 0.0).astype(BF16)


def dot3(x, matrix):
    rows = x.shape[0]
    hi = x.astype(BF16).astype(F32)
    rest = x - hi
    mid = rest.astype(BF16).astype(F32)
    stacked = jnp.concatenate([hi, mid, rest - mid], axis=0).astype(BF16)
    y = jnp.dot(stacked, matrix, preferred_element_type=F32)
    return y[:rows] + y[rows : 2 * rows] + y[2 * rows :]


def up(v, axis, by=1):
    return pltpu.roll(v, v.shape[axis] - by, axis)


def down(v, axis, by=1):
    return pltpu.roll(v, by, axis)


def harmonic(a, b):
    return 2.0 * a * b / (a + b)


def pair_rows(ref, rows):
    return ref[pl.ds(0, rows, stride=2), :] + ref[pl.ds(1, rows, stride=2), :]


def repeat_rows(ref, value):
    rows = value.shape[0]
    ref[pl.ds(0, rows, stride=2), :] = value
    ref[pl.ds(1, rows, stride=2), :] = value


def zup1(v):
    swapped = pltpu.roll(v, 64, 1)
    return jnp.where(iota(v.shape, 1) < 64, swapped, up(swapped, 0, 32))


def zdown1(v):
    swapped = pltpu.roll(v, 64, 1)
    return jnp.where(iota(v.shape, 1) < 64, down(swapped, 0, 32), swapped)


def xup2(v):
    moved = up(v, 1, 32)
    return jnp.where(iota(v.shape, 1) < 96, moved, up(moved, 0))


def xdown2(v):
    moved = down(v, 1, 32)
    return jnp.where(iota(v.shape, 1) < 32, down(moved, 0), moved)


def zup2(v):
    return up(v, 0, 4)


def zdown2(v):
    return down(v, 0, 4)


def xup1(v):
    return up(v, 0)


def xdown1(v):
    return down(v, 0)


MOVES1 = (xdown1, xup1, zdown1, zup1)
MOVES2 = (xdown2, xup2, zdown2, zup2)


def flat_coefs(perm, scale, x, y, nx, ny, moves, top):
    xdown, xup, zdown, zup = moves
    east = jnp.where(x < nx - 1, scale * harmonic(perm, xup(perm)), 0.0)
    north = jnp.where(y < ny - 1, scale * harmonic(perm, up(perm, 1)), 0.0)
    above = jnp.where(top, 0.0, (16.0 * scale) * harmonic(perm, zup(perm)))
    west, south, below = xdown(east), down(north, 1), zdown(above)
    edges = jnp.where(x == 0, scale, 0.0) + jnp.where(x == nx - 1, scale, 0.0)
    edges = edges + jnp.where(y == 0, scale, 0.0) + jnp.where(y == ny - 1, scale, 0.0)
    diag = west + east + south + north + below + above + edges * perm
    return west, east, south, north, below, above, diag, OMEGA / diag


def around(v, c, moves):
    xdown, xup, zdown, zup = moves
    a = c[0] * xdown(v) + c[1] * xup(v)
    b = c[2] * down(v, 1) + c[3] * up(v, 1)
    return (a + b) + (c[4] * zdown(v) + c[5] * zup(v))


def sweep(v, right, c, moves):
    return KEEP * v + c[7] * (right + around(v, c, moves))


def shifted(pair, parity, offset, cache):
    dx, dy, dz = offset
    source = (parity + dz) % 2
    lanes = dy + 16 * ((parity + dz - source) // 2)
    if (source, lanes) not in cache:
        value = pair[source]
        cache[source, lanes] = value if lanes == 0 else pltpu.roll(value, -lanes % 128, 1)
    value = cache[source, lanes]
    return value if dx == 0 else pltpu.roll(value, -dx % 8, 0)


def tree_sum(terms):
    while len(terms) > 1:
        terms = [a + b for a, b in zip(terms[::2], terms[1::2])] + terms[len(terms) & ~1 :]
    return terms[0]


def apply3(operator, pair, base):
    cache = {}
    out = []
    for parity in range(2):
        terms = [base[parity]]
        terms += [c[parity] * shifted(pair, parity, o, cache) for o, c in operator.items()]
        out.append(tree_sum(terms))
    return tuple(out)


def compose3(first, second):
    out = {}
    for o2, c2 in second.items():
        cache = {}
        for o1, c1 in first.items():
            term = [c1[parity] * shifted(c2, parity, o1, cache) for parity in range(2)]
            key = tuple(a + b for a, b in zip(o1, o2))
            out[key] = [a + b for a, b in zip(out[key], term)] if key in out else term
    return out


def kernel(
    props, doms, acc_ref, states, noise, source, out_ref,
    rx, cur, nz, perm, src, cw, ce, cs, cn, cu, dg, cc, va, vb, tmp,
    perm1, right1, tmp1, co1, v1s, tmp2, gp2, gr2, co2, m2, tmp3, e2s,
    loc, s1, d1, s2, d2, ss, ds_, sn, dn, sf, df, sq, dq, sp, dp, sr, dr, sg, dgs, word,
):
    me = lax.axis_index("prop")
    dom = lax.axis_index("dom")

    peers = sorted(range(1, props), key=lambda o: -min(o, props - o))

    def peer(o):
        return lax.rem(me + o, props)

    def slab(o):
        return lax.rem(dom + (o + doms), doms)

    def remote(from_ref, to_ref, send, recv, p, d):
        return pltpu.make_async_remote_copy(
            src_ref=from_ref, dst_ref=to_ref, send_sem=send, recv_sem=recv,
            device_id=(p, d), device_id_type=MESH,
        )

    load_noise = pltpu.make_async_copy(noise, nz, loc.at[0])
    load_source = pltpu.make_async_copy(source, src.at[pl.ds(4, 4)], loc.at[1])
    load_piece = pltpu.make_async_copy(states.at[me], rx.at[me], loc.at[2])
    load_piece.start()
    load_noise.start()
    load_source.start()

    barrier = pltpu.get_barrier_semaphore()
    for o in range(1, props):
        pl.semaphore_signal(barrier, inc=1, device_id=(peer(o), dom), device_id_type=MESH)

    for o in (1, -1, 2, -2, 3, -3):
        pl.semaphore_signal(barrier, inc=1, device_id=(me, slab(o)), device_id_type=MESH)
    pl.semaphore_wait(barrier, props + 5)

    reach = (3, 6, 12)

    def tell(i):
        for side, o in enumerate((reach[i], -reach[i])):
            target = (me, slab(o))
            pl.semaphore_signal(word.at[i, side], inc=1, device_id=target, device_id_type=MESH)

    def hear(i):
        for side in range(2):
            pl.semaphore_wait(word.at[i, side], 1)

    tell(0)

    sends1 = []
    for o in peers:
        copy = remote(states.at[peer(o)], rx.at[me], s1.at[o - 1], d1.at[o - 1], peer(o), dom)
        copy.start()
        sends1.append(copy)
    sends_src = [
        remote(source, src.at[pl.ds(0, 4)], ss.at[0], ds_.at[0], me, slab(1)),
        remote(source, src.at[pl.ds(8, 4)], ss.at[1], ds_.at[1], me, slab(-1)),
    ]

    r01, l01 = iota((256, 128), 0), iota((256, 128), 1)
    c01 = ones_where(l01 == (r01 >> 1))
    r12, l12 = iota((512, 128), 0), iota((512, 128), 1)
    c12 = ones_where(((r12 >> 7) == (l12 >> 5)) & (((r12 & 63) >> 1) == (l12 & 31)))
    r23, l23 = iota((128, 256), 0), iota((128, 256), 1)
    c23 = ones_where(((r23 >> 6) == (l23 >> 7)) & (((r23 & 31) >> 1) == (l23 & 15)))
    r32, l32 = iota((256, 128), 0), iota((256, 128), 1)
    c32 = ones_where(((l32 >> 6) == (r32 >> 7)) & (((l32 & 31) >> 1) == (r32 & 15)))
    r21, l21 = iota((128, 512), 0), iota((128, 512), 1)
    c21 = ones_where(((r21 >> 5) == (l21 >> 7)) & ((r21 & 31) == ((l21 & 63) >> 1)))
    r10, l10 = iota((128, 256), 0), iota((128, 256), 1)
    c10 = ones_where(r10 == (l10 >> 1))
    row, lane = iota((64, 128), 0), iota((64, 128), 1)
    east_in, north_in = row < 63, lane < 127
    edges = jnp.where(row == 0, 1.0, 0.0) + jnp.where(row == 63, 1.0, 0.0)
    edges = edges + jnp.where(lane == 0, 1.0, 0.0) + jnp.where(lane == 127, 1.0, 0.0)

    load_piece.wait()
    for copy in sends1:
        copy.wait_recv()
    cur[me] = rx[acc_ref[0]]
    hear(0)
    tell(1)
    sends2 = {}
    for o in peers:
        copy = remote(cur.at[me], cur.at[me], s2.at[o - 1], d2.at[o - 1], peer(o), dom)
        copy.start()
        sends2[o] = copy
    for copy in sends_src:
        copy.start()
    load_noise.wait()
    hear(1)
    tell(2)

    per_plane = 64 // cur.shape[1]
    for o in [0] + peers[::-1]:
        if o:
            sends2[o].wait_recv()
        j = peer(-o + props)
        rows = pl.ds(pl.multiple_of(lax.rem(j, per_plane) * cur.shape[1], 32), cur.shape[1])
        plane = j // per_plane
        perm[4 + plane, rows] = jnp.exp(SHRINK * cur[j] + BETA * nz[j])
        here = perm.at[4 + plane, rows]
        low, high = (plane == 0).astype(jnp.int32), (plane == 3).astype(jnp.int32)
        remote(here, perm.at[plane, rows], sn.at[low], dn.at[low], me, slab(1)).start()
        remote(here, perm.at[8 + plane, rows], sf.at[high], df.at[high], me, slab(-1)).start()
    sends2 = [sends2[o] for o in peers]
    near = [
        remote(perm.at[pl.ds(5, 3)], perm.at[pl.ds(1, 3)], sn.at[0], dn.at[0], me, slab(1)),
        remote(perm.at[pl.ds(4, 3)], perm.at[pl.ds(8, 3)], sf.at[0], df.at[0], me, slab(-1)),
    ]
    far = [
        remote(perm.at[4], perm.at[0], sn.at[1], dn.at[1], me, slab(1)),
        remote(perm.at[7], perm.at[11], sf.at[1], df.at[1], me, slab(-1)),
    ]

    def restrict01(planes):
        sums = []
        for i in range(2):
            tmp[...] = planes[2 * i] + planes[2 * i + 1]
            sums.append(pair_rows(tmp, 32))
        return dot3(jnp.concatenate(sums, axis=1), c01)

    def restrict12(value):
        tmp2[...] = value
        parts = []
        for q in range(4):
            low = tmp2[pl.ds(2 * q, 4, stride=8), :]
            parts.append(low + tmp2[pl.ds(2 * q + 1, 4, stride=8), :])
        return dot3(jnp.concatenate(parts, axis=1), c12)

    own1 = 0.125 * restrict01([perm[k] for k in range(4, 8)])
    perm1[3] = own1
    sends_q = []
    for i, o in enumerate((1, -1, 2, -2, 3, -3)):
        copy = remote(perm1.at[3], perm1.at[3 - o], sq.at[i], dq.at[i], me, slab(o))
        copy.start()
        sends_q.append(copy)
    gp2[dom] = 0.125 * restrict12(own1)

    def gather_to(buf, send, recv):
        def go(i, carry):
            step = (i + 1) // 2 * (2 * lax.rem(i, 2) - 1)
            remote(buf.at[dom], buf.at[dom], send, recv, me, slab(doms // 2 + step)).start()
            return carry

        lax.fori_loop(0, doms - 1, go, 0)

    def gather_wait(buf, send, recv):
        part = buf.at[pl.ds(0, doms - 1)]
        return remote(part, part, send, recv, me, slab(1))

    hear(2)
    gather_to(gp2, sp.at[0], dp.at[0])

    def sides(k):
        p = perm[k]
        east = jnp.where(east_in, harmonic(p, up(p, 0)), 0.0)
        north = jnp.where(north_in, harmonic(p, up(p, 1)), 0.0)
        ce[k] = east
        cn[k] = north
        cw[k] = down(east, 0)
        cs[k] = down(north, 1)

    inside_low = jnp.where(dom == 0, 0.0, 16.0)
    inside_high = jnp.where(dom == doms - 1, 0.0, 16.0)

    def face(k):
        factor = {3: inside_low, 7: inside_high}.get(k, 16.0)
        cu[k] = factor * harmonic(perm[k], perm[k + 1])

    def finish(k):
        diag = cw[k] + ce[k] + cs[k] + cn[k] + cu[k - 1] + cu[k] + edges * perm[k]
        dg[k] = diag
        scaled = OMEGA / diag
        cc[k] = scaled
        va[k] = scaled * src[k]

    def around0(v, k):
        x = v[k]
        a = cw[k] * down(x, 0) + ce[k] * up(x, 0)
        b = cs[k] * down(x, 1) + cn[k] * up(x, 1)
        return x, (a + b) + (cu[k - 1] * v[k - 1] + cu[k] * v[k + 1])

    def sweep0(v, k):
        x, total = around0(v, k)
        return KEEP * x + cc[k] * (src[k] + total)

    for k in range(4, 8):
        sides(k)
    for k in range(4, 7):
        face(k)
    load_source.wait()
    for copy in sends_src:
        copy.wait_recv()
    finish(5)
    finish(6)
    for copy in near:
        copy.wait_recv()
    for k in (2, 3, 8, 9):
        sides(k)
    for k in (1, 2, 3, 7, 8, 9):
        face(k)
    for k in (2, 3, 4, 7, 8, 9):
        finish(k)
    for k in range(3, 9):
        vb[k] = sweep0(va, k)
    rest = []
    for k in range(4, 8):
        x, total = around0(vb, k)
        rest.append(src[k] - dg[k] * x + total)
    right1[2] = restrict01(rest)
    sends_r = []
    for i, o in enumerate((1, -1, 2, -2)):
        copy = remote(right1.at[2], right1.at[2 - o], sr.at[i], dr.at[i], me, slab(o))
        copy.start()
        sends_r.append(copy)

    for copy in sends_q:
        copy.wait_recv()
    wide = perm1[...].reshape(7 * 32, 128)
    wide_row, wide_lane = iota(wide.shape, 0), iota(wide.shape, 1)
    pair = (dom + (doms - 3) + (wide_row >> 5)) & (doms - 1)
    top1 = (pair == doms - 1) & (wide_lane >= 64)
    coefs1 = flat_coefs(wide, 4.0, wide_row & 31, wide_lane & 63, 32, 64, MOVES1, top1)
    for i, value in enumerate(coefs1):
        co1[i] = value[32:192]

    for copy in sends_r[:2]:
        copy.wait_recv()
    b1 = right1[pl.ds(1, 3)].reshape(96, 128)
    inner = [co1[i, 32:128] for i in range(8)]
    v1 = sweep(inner[7] * b1, b1, inner, MOVES1)
    res1 = b1 - inner[6] * v1 + around(v1, inner, MOVES1)
    gr2[dom] = restrict12(res1[32:64])
    gather_to(gr2, sg.at[0], dgs.at[0])

    for copy in sends_r[2:]:
        copy.wait_recv()
    b1 = right1[...].reshape(160, 128)
    all1 = [co1[i] for i in range(8)]
    v1s[...] = sweep(all1[7] * b1, b1, all1, MOVES1)
    for copy in far:
        copy.wait_recv()
    for k in (1, 10):
        sides(k)
    for k in (0, 10):
        face(k)
    for k in (1, 10):
        finish(k)
    for k in (2, 9):
        vb[k] = sweep0(va, k)

    row8, row128 = iota((8, 128), 0), iota((128, 128), 0)
    lane8, lane128 = iota((8, 128), 1), iota((128, 128), 1)
    group = [(iota((8, 256), 1) & 127) >> 4 == g for g in range(8)]

    def restrict23(value):
        both = value + up(value, 0, 4)
        moved = down(both, 0, 4)
        parts = []
        for g in range(8):
            low, high = both[16 * g : 16 * g + 8], moved[16 * g + 8 : 16 * g + 16]
            parts.append(jnp.where(row8 < 4, low, high))
        y = dot3(jnp.concatenate(parts, axis=0), c23)
        total = tree_sum([jnp.where(group[g], y[8 * g : 8 * g + 8], 0.0) for g in range(8)])
        for parity in range(2):
            for q in range(2):
                piece = total[4 * parity : 4 * parity + 4, 128 * q : 128 * q + 128]
                tmp3[pl.ds(8 * parity + q, 4, stride=2), :] = piece
        return tmp3[pl.ds(0, 8), :], tmp3[pl.ds(8, 8), :]

    def prolong23(pair_):
        tmp3[pl.ds(0, 8), :] = pair_[0]
        tmp3[pl.ds(8, 8), :] = pair_[1]
        halves = []
        for q in range(2):
            rows = [tmp3[pl.ds(8 * parity + q, 4, stride=2), :] for parity in range(2)]
            halves.append(jnp.concatenate(rows, axis=0))
        e = jnp.concatenate(halves, axis=1)
        y = dot3(jnp.concatenate([jnp.where(m, e, 0.0) for m in group], axis=0), c32)
        parts = []
        for g in range(8):
            value = y[8 * g : 8 * g + 8]
            other = pltpu.roll(value, 4, 0)
            parts.append(jnp.where(row8 < 4, value, other))
            parts.append(jnp.where(row8 < 4, other, value))
        return jnp.concatenate(parts, axis=0)

    gather_wait(gp2, sp.at[0], dp.at[0]).wait_recv()
    p2 = gp2[...].reshape(128, 128)
    x2 = 4 * (row128 & 3) + (lane128 >> 5)
    coefs2 = flat_coefs(p2, 16.0, x2, lane128 & 31, 16, 32, MOVES2, row128 >= 124)
    for i, value in enumerate(coefs2):
        co2[i] = value
    pa, pb = restrict23(p2)
    pa, pb = 0.125 * pa, 0.125 * pb
    y3 = lane8 & 15
    scale = 64.0
    edges3 = jnp.where(row8 == 0, scale, 0.0) + jnp.where(row8 == 7, scale, 0.0)
    edges3 = edges3 + jnp.where(y3 == 0, scale, 0.0) + jnp.where(y3 == 15, scale, 0.0)

    def sides3(p):
        east = jnp.where(row8 < 7, scale * harmonic(p, up(p, 0)), 0.0)
        north = jnp.where(y3 < 15, scale * harmonic(p, up(p, 1)), 0.0)
        return [down(east, 0), east, down(north, 1), north]

    mid = (16.0 * scale) * harmonic(pa, pb)
    high = jnp.where(lane8 < 112, (16.0 * scale) * harmonic(pb, up(pa, 1, 16)), 0.0)
    low = down(high, 1, 16)
    ca = sides3(pa) + [low, mid]
    cb = sides3(pb) + [mid, high]

    def scaled3(c, p):
        total = (c[0] + c[1]) + (c[2] + c[3]) + (c[4] + c[5]) + edges3 * p
        inverse = OMEGA / total
        return inverse, [inverse * value for value in c]

    ia, ca = scaled3(ca, pa)
    ib, cb = scaled3(cb, pb)
    keep = jnp.full((8, 128), KEEP, F32)
    offsets = ((-1, 0, 0), (1, 0, 0), (0, -1, 0), (0, 1, 0), (0, 0, -1), (0, 0, 1))
    once = {(0, 0, 0): (keep, keep)}
    once.update({o: (a, b) for o, a, b in zip(offsets, ca, cb)})
    twice = compose3(once, once)
    keys = list(twice)
    for i, key in enumerate(keys):
        for parity in range(2):
            m2[parity, i] = twice[key][parity]

    gather_wait(gr2, sg.at[0], dgs.at[0]).wait_recv()
    b2 = gr2[...].reshape(128, 128)
    all2 = [co2[i] for i in range(8)]
    v2 = sweep(all2[7] * b2, b2, all2, MOVES2)
    res2 = b2 - all2[6] * v2 + around(v2, all2, MOVES2)
    ra, rb = restrict23(res2)
    base = (ia * ra, ib * rb)
    base = apply3(once, base, base)

    def coarse(step, value):
        operator = {key: (m2[0, i], m2[1, i]) for i, key in enumerate(keys)}
        return apply3(operator, value, base)

    v2 = v2 + prolong23(lax.fori_loop(0, (COARSE_SWEEPS - 2) // 2, coarse, base))
    for _ in range(2):
        v2 = sweep(v2, b2, all2, MOVES2)
    e2s[...] = v2

    parts = []
    for j in range(-2, 3):
        z = slab(j)
        value = e2s[pl.ds(pl.multiple_of((z // 2) * 8, 8), 8), :]
        parts.append(jnp.where(lax.rem(z, 2) == 0, value, pltpu.roll(value, 4, 0)))
    wide1 = dot3(jnp.concatenate(parts, axis=0), c21)
    for j in range(5):
        for q in range(4):
            piece = wide1[8 * j : 8 * j + 4, 128 * q : 128 * q + 128]
            for i in range(2):
                tmp1[pl.ds(32 * j + 2 * q + i, 4, stride=8), :] = piece
    v1 = v1s[...] + tmp1[...]
    b1 = right1[...].reshape(160, 128)
    all1 = [co1[i] for i in range(8)]
    for _ in range(2):
        v1 = sweep(v1, b1, all1, MOVES1)

    fine = dot3(v1[32:128], c10)
    for k, i, half in ((2, 0, 1), (4, 1, 0), (6, 1, 1), (8, 2, 0)):
        repeat_rows(tmp, fine[32 * i : 32 * i + 32, 128 * half : 128 * half + 128])
        add = tmp[...]
        vb[k] = vb[k] + add
        vb[k + 1] = vb[k + 1] + add
    for k in range(3, 9):
        va[k] = sweep0(vb, k)
    for k in range(4, 8):
        out_ref[k - 4] = sweep0(va, k)

    for copies in (sends1, sends2, sends_src, near, far, sends_q, sends_r):
        for copy in copies:
            copy.wait_send()
    gather_wait(gp2, sp.at[0], dp.at[0]).wait_send()
    gather_wait(gr2, sg.at[0], dgs.at[0]).wait_send()


def body(states, accepted, noise, source):
    props, doms = lax.axis_size("prop"), lax.axis_size("dom")
    rows = 256 // props
    dma = pltpu.SemaphoreType.DMA
    plane = lambda n: pltpu.VMEM((n, 64, 128), F32)
    scratch = [
        pltpu.VMEM((props, rows, 128), F32),
        pltpu.VMEM((props, rows, 128), F32),
        pltpu.VMEM((props, rows, 128), F32),
        plane(12), plane(12),
        plane(12), plane(12), plane(12), plane(12), plane(12), plane(12), plane(12),
        plane(12), plane(12),
        pltpu.VMEM((64, 128), F32),
        pltpu.VMEM((7, 32, 128), F32),
        pltpu.VMEM((5, 32, 128), F32),
        pltpu.VMEM((160, 128), F32),
        pltpu.VMEM((8, 160, 128), F32),
        pltpu.VMEM((160, 128), F32),
        pltpu.VMEM((32, 128), F32),
        pltpu.VMEM((doms, 4, 128), F32),
        pltpu.VMEM((doms, 4, 128), F32),
        pltpu.VMEM((8, 128, 128), F32),
        pltpu.VMEM((2, 25, 8, 128), F32),
        pltpu.VMEM((16, 128), F32),
        pltpu.VMEM((128, 128), F32),
        dma((3,)),
        dma((props - 1,)), dma((props - 1,)), dma((props - 1,)), dma((props - 1,)),
        dma((2,)), dma((2,)), dma((2,)), dma((2,)), dma((2,)), dma((2,)),
        dma((6,)), dma((6,)), dma((1,)), dma((1,)), dma((4,)), dma((4,)), dma((1,)), dma((1,)),
        pltpu.SemaphoreType.REGULAR((3, 2)),
    ]
    hbm = pl.BlockSpec(memory_space=pl.ANY)
    out = pl.pallas_call(
        functools.partial(kernel, props, doms),
        out_shape=pltpu.VMEM((4, 64, 128), F32),
        in_specs=[pl.BlockSpec(memory_space=pltpu.SMEM), hbm, hbm, hbm],
        out_specs=pl.BlockSpec(memory_space=pltpu.VMEM),
        scratch_shapes=scratch,
        compiler_params=pltpu.CompilerParams(collective_id=0, has_side_effects=True),
        name="mcmc_step",
    )(
        accepted,
        states.reshape(props, rows, 128),
        noise.reshape(props, rows, 128),
        source,
    )
    return out[None]


def solution(mesh):
    in_specs = (
        P("prop", "dom", None, None),
        P(),
        P("prop", "dom", None, None),
        P("dom", None, None),
    )
    out_specs = P("prop", "dom", None, None)
    return jax.shard_map(body, mesh=mesh, in_specs=in_specs, out_specs=out_specs, check_vma=False)
```

```python
import functools
import math

import jax
import jax.numpy as jnp
from jax import lax
from jax.experimental import pallas as pl
from jax.experimental.pallas import tpu as pltpu
from jax.sharding import PartitionSpec as P

OMEGA = 0.7
BETA = 0.4
SHRINK = math.sqrt(1.0 - BETA * BETA)
KEEP = 1.0 - OMEGA
COARSE_SWEEPS = 64
F32 = jnp.float32
BF16 = jnp.bfloat16
MESH = pl.DeviceIdType.MESH


def iota(shape, axis):
    return lax.broadcasted_iota(jnp.int32, shape, axis)


def ones_where(mask):
    return jnp.where(mask, 1.0, 0.0).astype(BF16)


def dot3(x, matrix):
    rows = x.shape[0]
    hi = x.astype(BF16).astype(F32)
    rest = x - hi
    mid = rest.astype(BF16).astype(F32)
    stacked = jnp.concatenate([hi, mid, rest - mid], axis=0).astype(BF16)
    y = jnp.dot(stacked, matrix, preferred_element_type=F32)
    return y[:rows] + y[rows : 2 * rows] + y[2 * rows :]


def up(v, axis, by=1):
    return pltpu.roll(v, v.shape[axis] - by, axis)


def down(v, axis, by=1):
    return pltpu.roll(v, by, axis)


def harmonic(a, b):
    return 2.0 * a * b / (a + b)


def pair_rows(ref, rows):
    return ref[pl.ds(0, rows, stride=2), :] + ref[pl.ds(1, rows, stride=2), :]


def repeat_rows(ref, value):
    rows = value.shape[0]
    ref[pl.ds(0, rows, stride=2), :] = value
    ref[pl.ds(1, rows, stride=2), :] = value


def zup1(v):
    swapped = pltpu.roll(v, 64, 1)
    return jnp.where(iota(v.shape, 1) < 64, swapped, up(swapped, 0, 32))


def zdown1(v):
    swapped = pltpu.roll(v, 64, 1)
    return jnp.where(iota(v.shape, 1) < 64, down(swapped, 0, 32), swapped)


def xup2(v):
    moved = up(v, 1, 32)
    return jnp.where(iota(v.shape, 1) < 96, moved, up(moved, 0))


def xdown2(v):
    moved = down(v, 1, 32)
    return jnp.where(iota(v.shape, 1) < 32, down(moved, 0), moved)


def zup2(v):
    return up(v, 0, 4)


def zdown2(v):
    return down(v, 0, 4)


def xup1(v):
    return up(v, 0)


def xdown1(v):
    return down(v, 0)


MOVES1 = (xdown1, xup1, zdown1, zup1)
MOVES2 = (xdown2, xup2, zdown2, zup2)


def flat_coefs(perm, scale, x, y, nx, ny, moves, top):
    xdown, xup, zdown, zup = moves
    east = jnp.where(x < nx - 1, scale * harmonic(perm, xup(perm)), 0.0)
    north = jnp.where(y < ny - 1, scale * harmonic(perm, up(perm, 1)), 0.0)
    above = jnp.where(top, 0.0, (16.0 * scale) * harmonic(perm, zup(perm)))
    west, south, below = xdown(east), down(north, 1), zdown(above)
    edges = jnp.where(x == 0, scale, 0.0) + jnp.where(x == nx - 1, scale, 0.0)
    edges = edges + jnp.where(y == 0, scale, 0.0) + jnp.where(y == ny - 1, scale, 0.0)
    diag = west + east + south + north + below + above + edges * perm
    return west, east, south, north, below, above, diag, OMEGA / diag


def around(v, c, moves):
    xdown, xup, zdown, zup = moves
    a = c[0] * xdown(v) + c[1] * xup(v)
    b = c[2] * down(v, 1) + c[3] * up(v, 1)
    return (a + b) + (c[4] * zdown(v) + c[5] * zup(v))


def sweep(v, right, c, moves):
    return KEEP * v + c[7] * (right + around(v, c, moves))


def shifted(pair, parity, offset, cache):
    dx, dy, dz = offset
    source = (parity + dz) % 2
    lanes = dy + 16 * ((parity + dz - source) // 2)
    if (source, lanes) not in cache:
        value = pair[source]
        cache[source, lanes] = value if lanes == 0 else pltpu.roll(value, -lanes % 128, 1)
    value = cache[source, lanes]
    return value if dx == 0 else pltpu.roll(value, -dx % 8, 0)


def tree_sum(terms):
    while len(terms) > 1:
        terms = [a + b for a, b in zip(terms[::2], terms[1::2])] + terms[len(terms) & ~1 :]
    return terms[0]


def apply3(operator, pair, base):
    cache = {}
    out = []
    for parity in range(2):
        terms = [base[parity]]
        terms += [c[parity] * shifted(pair, parity, o, cache) for o, c in operator.items()]
        out.append(tree_sum(terms))
    return tuple(out)


def compose3(first, second):
    out = {}
    for o2, c2 in second.items():
        cache = {}
        for o1, c1 in first.items():
            term = [c1[parity] * shifted(c2, parity, o1, cache) for parity in range(2)]
            key = tuple(a + b for a, b in zip(o1, o2))
            out[key] = [a + b for a, b in zip(out[key], term)] if key in out else term
    return out


def kernel(
    props, doms, root, states, noise, source, out_ref,
    cur, nz, perm, src, cw, ce, cs, cn, cu, dg, cc, va, vb, tmp,
    perm1, right1, tmp1, co1, v1s, tmp2, gp2, gr2, co2, m2, tmp3, e2s,
    loc, s1, d1, ss, ds_, sn, dn, sf, df, sq, dq, sp, dp, sr, dr, sg, dgs, word,
):
    me = lax.axis_index("prop")
    dom = lax.axis_index("dom")

    spread = lambda p: -min((p - root) % props, (root - p) % props)
    peers = sorted((p for p in range(props) if p != root), key=spread)

    def slab(o):
        return lax.rem(dom + (o + doms), doms)

    def remote(from_ref, to_ref, send, recv, p, d):
        return pltpu.make_async_remote_copy(
            src_ref=from_ref, dst_ref=to_ref, send_sem=send, recv_sem=recv,
            device_id=(p, d), device_id_type=MESH,
        )

    load_noise = pltpu.make_async_copy(noise, nz, loc.at[0])
    load_source = pltpu.make_async_copy(source, src.at[pl.ds(4, 4)], loc.at[1])
    load_noise.start()
    load_source.start()
    order = (1, 2, 3, 0)

    def load_plane(k):
        return pltpu.make_async_copy(states.at[k], cur.at[k], d1.at[k])

    barrier = pltpu.get_barrier_semaphore()

    @pl.when(me != root)
    def _():
        pl.semaphore_signal(barrier, inc=1, device_id=(root, dom), device_id_type=MESH)

    for o in (1, -1, 2, -2, 3, -3):
        pl.semaphore_signal(barrier, inc=1, device_id=(me, slab(o)), device_id_type=MESH)
    pl.semaphore_wait(barrier, jnp.where(me == root, props + 5, 6))

    @pl.when(me == root)
    def _():
        for k in order:
            for p in peers:
                remote(states.at[k], cur.at[k], s1.at[p], d1.at[k], p, dom).start()
            load_plane(k).start()

    reach = (3, 6, 12)

    def tell(i):
        for side, o in enumerate((reach[i], -reach[i])):
            target = (me, slab(o))
            pl.semaphore_signal(word.at[i, side], inc=1, device_id=target, device_id_type=MESH)

    def hear(i):
        for side in range(2):
            pl.semaphore_wait(word.at[i, side], 1)

    tell(0)

    sends_src = [
        remote(source, src.at[pl.ds(0, 4)], ss.at[0], ds_.at[0], me, slab(1)),
        remote(source, src.at[pl.ds(8, 4)], ss.at[1], ds_.at[1], me, slab(-1)),
    ]
    for copy in sends_src:
        copy.start()

    r01, l01 = iota((256, 128), 0), iota((256, 128), 1)
    c01 = ones_where(l01 == (r01 >> 1))
    r12, l12 = iota((512, 128), 0), iota((512, 128), 1)
    c12 = ones_where(((r12 >> 7) == (l12 >> 5)) & (((r12 & 63) >> 1) == (l12 & 31)))
    r23, l23 = iota((128, 256), 0), iota((128, 256), 1)
    c23 = ones_where(((r23 >> 6) == (l23 >> 7)) & (((r23 & 31) >> 1) == (l23 & 15)))
    r32, l32 = iota((256, 128), 0), iota((256, 128), 1)
    c32 = ones_where(((l32 >> 6) == (r32 >> 7)) & (((l32 & 31) >> 1) == (r32 & 15)))
    r21, l21 = iota((128, 512), 0), iota((128, 512), 1)
    c21 = ones_where(((r21 >> 5) == (l21 >> 7)) & ((r21 & 31) == ((l21 & 63) >> 1)))
    r10, l10 = iota((128, 256), 0), iota((128, 256), 1)
    c10 = ones_where(r10 == (l10 >> 1))
    row, lane = iota((64, 128), 0), iota((64, 128), 1)
    east_in, north_in = row < 63, lane < 127
    edges = jnp.where(row == 0, 1.0, 0.0) + jnp.where(row == 63, 1.0, 0.0)
    edges = edges + jnp.where(lane == 0, 1.0, 0.0) + jnp.where(lane == 127, 1.0, 0.0)

    load_noise.wait()
    hear(0)
    tell(1)
    for k in order:
        load_plane(k).wait()
        perm[4 + k] = jnp.exp(SHRINK * cur[k] + BETA * nz[k])
        low, high = int(k == 0), int(k == 3)
        here = perm.at[4 + k]
        remote(here, perm.at[k], sn.at[low], dn.at[low], me, slab(1)).start()
        remote(here, perm.at[8 + k], sf.at[high], df.at[high], me, slab(-1)).start()
    hear(1)
    tell(2)
    near = [
        remote(perm.at[pl.ds(5, 3)], perm.at[pl.ds(1, 3)], sn.at[0], dn.at[0], me, slab(1)),
        remote(perm.at[pl.ds(4, 3)], perm.at[pl.ds(8, 3)], sf.at[0], df.at[0], me, slab(-1)),
    ]
    far = [
        remote(perm.at[4], perm.at[0], sn.at[1], dn.at[1], me, slab(1)),
        remote(perm.at[7], perm.at[11], sf.at[1], df.at[1], me, slab(-1)),
    ]

    def restrict01(planes):
        sums = []
        for i in range(2):
            tmp[...] = planes[2 * i] + planes[2 * i + 1]
            sums.append(pair_rows(tmp, 32))
        return dot3(jnp.concatenate(sums, axis=1), c01)

    def restrict12(value):
        tmp2[...] = value
        parts = []
        for q in range(4):
            low = tmp2[pl.ds(2 * q, 4, stride=8), :]
            parts.append(low + tmp2[pl.ds(2 * q + 1, 4, stride=8), :])
        return dot3(jnp.concatenate(parts, axis=1), c12)

    own1 = 0.125 * restrict01([perm[k] for k in range(4, 8)])
    perm1[3] = own1
    sends_q = []
    for i, o in enumerate((1, -1, 2, -2, 3, -3)):
        copy = remote(perm1.at[3], perm1.at[3 - o], sq.at[i], dq.at[i], me, slab(o))
        copy.start()
        sends_q.append(copy)
    gp2[dom] = 0.125 * restrict12(own1)

    def gather_to(buf, send, recv):
        def go(i, carry):
            step = (i + 1) // 2 * (2 * lax.rem(i, 2) - 1)
            remote(buf.at[dom], buf.at[dom], send, recv, me, slab(doms // 2 + step)).start()
            return carry

        lax.fori_loop(0, doms - 1, go, 0)

    def gather_wait(buf, send, recv):
        part = buf.at[pl.ds(0, doms - 1)]
        return remote(part, part, send, recv, me, slab(1))

    hear(2)
    gather_to(gp2, sp.at[0], dp.at[0])

    def sides(k):
        p = perm[k]
        east = jnp.where(east_in, harmonic(p, up(p, 0)), 0.0)
        north = jnp.where(north_in, harmonic(p, up(p, 1)), 0.0)
        ce[k] = east
        cn[k] = north
        cw[k] = down(east, 0)
        cs[k] = down(north, 1)

    inside_low = jnp.where(dom == 0, 0.0, 16.0)
    inside_high = jnp.where(dom == doms - 1, 0.0, 16.0)

    def face(k):
        factor = {3: inside_low, 7: inside_high}.get(k, 16.0)
        cu[k] = factor * harmonic(perm[k], perm[k + 1])

    def finish(k):
        diag = cw[k] + ce[k] + cs[k] + cn[k] + cu[k - 1] + cu[k] + edges * perm[k]
        dg[k] = diag
        scaled = OMEGA / diag
        cc[k] = scaled
        va[k] = scaled * src[k]

    def around0(v, k):
        x = v[k]
        a = cw[k] * down(x, 0) + ce[k] * up(x, 0)
        b = cs[k] * down(x, 1) + cn[k] * up(x, 1)
        return x, (a + b) + (cu[k - 1] * v[k - 1] + cu[k] * v[k + 1])

    def sweep0(v, k):
        x, total = around0(v, k)
        return KEEP * x + cc[k] * (src[k] + total)

    for k in range(4, 8):
        sides(k)
    for k in range(4, 7):
        face(k)
    load_source.wait()
    for copy in sends_src:
        copy.wait_recv()
    finish(5)
    finish(6)
    for copy in near:
        copy.wait_recv()
    for k in (2, 3, 8, 9):
        sides(k)
    for k in (1, 2, 3, 7, 8, 9):
        face(k)
    for k in (2, 3, 4, 7, 8, 9):
        finish(k)
    for k in range(3, 9):
        vb[k] = sweep0(va, k)
    rest = []
    for k in range(4, 8):
        x, total = around0(vb, k)
        rest.append(src[k] - dg[k] * x + total)
    right1[2] = restrict01(rest)
    sends_r = []
    for i, o in enumerate((1, -1, 2, -2)):
        copy = remote(right1.at[2], right1.at[2 - o], sr.at[i], dr.at[i], me, slab(o))
        copy.start()
        sends_r.append(copy)

    for copy in sends_q:
        copy.wait_recv()
    wide = perm1[...].reshape(7 * 32, 128)
    wide_row, wide_lane = iota(wide.shape, 0), iota(wide.shape, 1)
    pair = (dom + (doms - 3) + (wide_row >> 5)) & (doms - 1)
    top1 = (pair == doms - 1) & (wide_lane >= 64)
    coefs1 = flat_coefs(wide, 4.0, wide_row & 31, wide_lane & 63, 32, 64, MOVES1, top1)
    for i, value in enumerate(coefs1):
        co1[i] = value[32:192]

    for copy in sends_r[:2]:
        copy.wait_recv()
    b1 = right1[pl.ds(1, 3)].reshape(96, 128)
    inner = [co1[i, 32:128] for i in range(8)]
    v1 = sweep(inner[7] * b1, b1, inner, MOVES1)
    res1 = b1 - inner[6] * v1 + around(v1, inner, MOVES1)
    gr2[dom] = restrict12(res1[32:64])
    gather_to(gr2, sg.at[0], dgs.at[0])

    for copy in sends_r[2:]:
        copy.wait_recv()
    b1 = right1[...].reshape(160, 128)
    all1 = [co1[i] for i in range(8)]
    v1s[...] = sweep(all1[7] * b1, b1, all1, MOVES1)
    for copy in far:
        copy.wait_recv()
    for k in (1, 10):
        sides(k)
    for k in (0, 10):
        face(k)
    for k in (1, 10):
        finish(k)
    for k in (2, 9):
        vb[k] = sweep0(va, k)

    row8, row128 = iota((8, 128), 0), iota((128, 128), 0)
    lane8, lane128 = iota((8, 128), 1), iota((128, 128), 1)
    group = [(iota((8, 256), 1) & 127) >> 4 == g for g in range(8)]

    def restrict23(value):
        both = value + up(value, 0, 4)
        moved = down(both, 0, 4)
        parts = []
        for g in range(8):
            low, high = both[16 * g : 16 * g + 8], moved[16 * g + 8 : 16 * g + 16]
            parts.append(jnp.where(row8 < 4, low, high))
        y = dot3(jnp.concatenate(parts, axis=0), c23)
        total = tree_sum([jnp.where(group[g], y[8 * g : 8 * g + 8], 0.0) for g in range(8)])
        for parity in range(2):
            for q in range(2):
                piece = total[4 * parity : 4 * parity + 4, 128 * q : 128 * q + 128]
                tmp3[pl.ds(8 * parity + q, 4, stride=2), :] = piece
        return tmp3[pl.ds(0, 8), :], tmp3[pl.ds(8, 8), :]

    def prolong23(pair_):
        tmp3[pl.ds(0, 8), :] = pair_[0]
        tmp3[pl.ds(8, 8), :] = pair_[1]
        halves = []
        for q in range(2):
            rows = [tmp3[pl.ds(8 * parity + q, 4, stride=2), :] for parity in range(2)]
            halves.append(jnp.concatenate(rows, axis=0))
        e = jnp.concatenate(halves, axis=1)
        y = dot3(jnp.concatenate([jnp.where(m, e, 0.0) for m in group], axis=0), c32)
        parts = []
        for g in range(8):
            value = y[8 * g : 8 * g + 8]
            other = pltpu.roll(value, 4, 0)
            parts.append(jnp.where(row8 < 4, value, other))
            parts.append(jnp.where(row8 < 4, other, value))
        return jnp.concatenate(parts, axis=0)

    gather_wait(gp2, sp.at[0], dp.at[0]).wait_recv()
    p2 = gp2[...].reshape(128, 128)
    x2 = 4 * (row128 & 3) + (lane128 >> 5)
    coefs2 = flat_coefs(p2, 16.0, x2, lane128 & 31, 16, 32, MOVES2, row128 >= 124)
    for i, value in enumerate(coefs2):
        co2[i] = value
    pa, pb = restrict23(p2)
    pa, pb = 0.125 * pa, 0.125 * pb
    y3 = lane8 & 15
    scale = 64.0
    edges3 = jnp.where(row8 == 0, scale, 0.0) + jnp.where(row8 == 7, scale, 0.0)
    edges3 = edges3 + jnp.where(y3 == 0, scale, 0.0) + jnp.where(y3 == 15, scale, 0.0)

    def sides3(p):
        east = jnp.where(row8 < 7, scale * harmonic(p, up(p, 0)), 0.0)
        north = jnp.where(y3 < 15, scale * harmonic(p, up(p, 1)), 0.0)
        return [down(east, 0), east, down(north, 1), north]

    mid = (16.0 * scale) * harmonic(pa, pb)
    high = jnp.where(lane8 < 112, (16.0 * scale) * harmonic(pb, up(pa, 1, 16)), 0.0)
    low = down(high, 1, 16)
    ca = sides3(pa) + [low, mid]
    cb = sides3(pb) + [mid, high]

    def scaled3(c, p):
        total = (c[0] + c[1]) + (c[2] + c[3]) + (c[4] + c[5]) + edges3 * p
        inverse = OMEGA / total
        return inverse, [inverse * value for value in c]

    ia, ca = scaled3(ca, pa)
    ib, cb = scaled3(cb, pb)
    keep = jnp.full((8, 128), KEEP, F32)
    offsets = ((-1, 0, 0), (1, 0, 0), (0, -1, 0), (0, 1, 0), (0, 0, -1), (0, 0, 1))
    once = {(0, 0, 0): (keep, keep)}
    once.update({o: (a, b) for o, a, b in zip(offsets, ca, cb)})
    twice = compose3(once, once)
    keys = list(twice)
    for i, key in enumerate(keys):
        for parity in range(2):
            m2[parity, i] = twice[key][parity]

    gather_wait(gr2, sg.at[0], dgs.at[0]).wait_recv()
    b2 = gr2[...].reshape(128, 128)
    all2 = [co2[i] for i in range(8)]
    v2 = sweep(all2[7] * b2, b2, all2, MOVES2)
    res2 = b2 - all2[6] * v2 + around(v2, all2, MOVES2)
    ra, rb = restrict23(res2)
    base = (ia * ra, ib * rb)
    base = apply3(once, base, base)

    def coarse(step, value):
        operator = {key: (m2[0, i], m2[1, i]) for i, key in enumerate(keys)}
        return apply3(operator, value, base)

    v2 = v2 + prolong23(lax.fori_loop(0, (COARSE_SWEEPS - 2) // 2, coarse, base))
    for _ in range(2):
        v2 = sweep(v2, b2, all2, MOVES2)
    e2s[...] = v2

    parts = []
    for j in range(-2, 3):
        z = slab(j)
        value = e2s[pl.ds(pl.multiple_of((z // 2) * 8, 8), 8), :]
        parts.append(jnp.where(lax.rem(z, 2) == 0, value, pltpu.roll(value, 4, 0)))
    wide1 = dot3(jnp.concatenate(parts, axis=0), c21)
    for j in range(5):
        for q in range(4):
            piece = wide1[8 * j : 8 * j + 4, 128 * q : 128 * q + 128]
            for i in range(2):
                tmp1[pl.ds(32 * j + 2 * q + i, 4, stride=8), :] = piece
    v1 = v1s[...] + tmp1[...]
    b1 = right1[...].reshape(160, 128)
    all1 = [co1[i] for i in range(8)]
    for _ in range(2):
        v1 = sweep(v1, b1, all1, MOVES1)

    fine = dot3(v1[32:128], c10)
    for k, i, half in ((2, 0, 1), (4, 1, 0), (6, 1, 1), (8, 2, 0)):
        repeat_rows(tmp, fine[32 * i : 32 * i + 32, 128 * half : 128 * half + 128])
        add = tmp[...]
        vb[k] = vb[k] + add
        vb[k + 1] = vb[k + 1] + add
    for k in range(3, 9):
        va[k] = sweep0(vb, k)
    for k in range(4, 8):
        out_ref[k - 4] = sweep0(va, k)

    @pl.when(me == root)
    def _():
        for p in peers:
            remote(cur, cur, s1.at[p], d1.at[0], p, dom).wait_send()

    for copies in (sends_src, near, far, sends_q, sends_r):
        for copy in copies:
            copy.wait_send()
    gather_wait(gp2, sp.at[0], dp.at[0]).wait_send()
    gather_wait(gr2, sg.at[0], dgs.at[0]).wait_send()


def body(states, accepted, noise, source):
    props, doms = lax.axis_size("prop"), lax.axis_size("dom")
    dma = pltpu.SemaphoreType.DMA
    plane = lambda n: pltpu.VMEM((n, 64, 128), F32)
    scratch = [
        plane(4), plane(4),
        plane(12), plane(12),
        plane(12), plane(12), plane(12), plane(12), plane(12), plane(12), plane(12),
        plane(12), plane(12),
        pltpu.VMEM((64, 128), F32),
        pltpu.VMEM((7, 32, 128), F32),
        pltpu.VMEM((5, 32, 128), F32),
        pltpu.VMEM((160, 128), F32),
        pltpu.VMEM((8, 160, 128), F32),
        pltpu.VMEM((160, 128), F32),
        pltpu.VMEM((32, 128), F32),
        pltpu.VMEM((doms, 4, 128), F32),
        pltpu.VMEM((doms, 4, 128), F32),
        pltpu.VMEM((8, 128, 128), F32),
        pltpu.VMEM((2, 25, 8, 128), F32),
        pltpu.VMEM((16, 128), F32),
        pltpu.VMEM((128, 128), F32),
        dma((2,)), dma((props,)), dma((4,)),
        dma((2,)), dma((2,)), dma((2,)), dma((2,)), dma((2,)), dma((2,)),
        dma((6,)), dma((6,)), dma((1,)), dma((1,)), dma((4,)), dma((4,)), dma((1,)), dma((1,)),
        pltpu.SemaphoreType.REGULAR((3, 2)),
    ]
    hbm = pl.BlockSpec(memory_space=pl.ANY)

    def branch(root):
        return pl.pallas_call(
            functools.partial(kernel, props, doms, root),
            out_shape=pltpu.VMEM((4, 64, 128), F32),
            in_specs=[hbm, hbm, hbm],
            out_specs=pl.BlockSpec(memory_space=pltpu.VMEM),
            scratch_shapes=scratch,
            compiler_params=pltpu.CompilerParams(collective_id=root, has_side_effects=True),
            name=f"mcmc_step_{root}",
        )

    branches = [branch(root) for root in range(props)]
    return lax.switch(accepted[0], branches, states[0], noise[0], source)[None]


def solution(mesh):
    in_specs = (
        P("prop", "dom", None, None),
        P(),
        P("prop", "dom", None, None),
        P("dom", None, None),
    )
    out_specs = P("prop", "dom", None, None)
    return jax.shard_map(body, mesh=mesh, in_specs=in_specs, out_specs=out_specs, check_vma=False)
```

```python
import functools
import math

import jax
import jax.numpy as jnp
from jax import lax
from jax.experimental import pallas as pl
from jax.experimental.pallas import tpu as pltpu
from jax.sharding import PartitionSpec as P

OMEGA = 0.7
BETA = 0.4
SHRINK = math.sqrt(1.0 - BETA * BETA)
KEEP = 1.0 - OMEGA
COARSE_SWEEPS = 64
F32 = jnp.float32
BF16 = jnp.bfloat16
MESH = pl.DeviceIdType.MESH


def iota(shape, axis):
    return lax.broadcasted_iota(jnp.int32, shape, axis)


def ones_where(mask):
    return jnp.where(mask, 1.0, 0.0).astype(BF16)


def dot3(x, matrix):
    rows = x.shape[0]
    hi = x.astype(BF16).astype(F32)
    rest = x - hi
    mid = rest.astype(BF16).astype(F32)
    stacked = jnp.concatenate([hi, mid, rest - mid], axis=0).astype(BF16)
    y = jnp.dot(stacked, matrix, preferred_element_type=F32)
    return y[:rows] + y[rows : 2 * rows] + y[2 * rows :]


def up(v, axis, by=1):
    return pltpu.roll(v, v.shape[axis] - by, axis)


def down(v, axis, by=1):
    return pltpu.roll(v, by, axis)


def harmonic(a, b):
    return 2.0 * a * b / (a + b)


def pair_rows(ref, rows):
    return ref[pl.ds(0, rows, stride=2), :] + ref[pl.ds(1, rows, stride=2), :]


def repeat_rows(ref, value):
    rows = value.shape[0]
    ref[pl.ds(0, rows, stride=2), :] = value
    ref[pl.ds(1, rows, stride=2), :] = value


def zup1(v):
    swapped = pltpu.roll(v, 64, 1)
    return jnp.where(iota(v.shape, 1) < 64, swapped, up(swapped, 0, 32))


def zdown1(v):
    swapped = pltpu.roll(v, 64, 1)
    return jnp.where(iota(v.shape, 1) < 64, down(swapped, 0, 32), swapped)


def xup2(v):
    moved = up(v, 1, 32)
    return jnp.where(iota(v.shape, 1) < 96, moved, up(moved, 0))


def xdown2(v):
    moved = down(v, 1, 32)
    return jnp.where(iota(v.shape, 1) < 32, down(moved, 0), moved)


def zup2(v):
    return up(v, 0, 4)


def zdown2(v):
    return down(v, 0, 4)


def xup1(v):
    return up(v, 0)


def xdown1(v):
    return down(v, 0)


MOVES1 = (xdown1, xup1, zdown1, zup1)
MOVES2 = (xdown2, xup2, zdown2, zup2)


def flat_coefs(perm, scale, x, y, nx, ny, moves, top):
    xdown, xup, zdown, zup = moves
    east = jnp.where(x < nx - 1, scale * harmonic(perm, xup(perm)), 0.0)
    north = jnp.where(y < ny - 1, scale * harmonic(perm, up(perm, 1)), 0.0)
    above = jnp.where(top, 0.0, (16.0 * scale) * harmonic(perm, zup(perm)))
    west, south, below = xdown(east), down(north, 1), zdown(above)
    edges = jnp.where(x == 0, scale, 0.0) + jnp.where(x == nx - 1, scale, 0.0)
    edges = edges + jnp.where(y == 0, scale, 0.0) + jnp.where(y == ny - 1, scale, 0.0)
    diag = west + east + south + north + below + above + edges * perm
    return west, east, south, north, below, above, diag, OMEGA / diag


def around(v, c, moves):
    xdown, xup, zdown, zup = moves
    a = c[0] * xdown(v) + c[1] * xup(v)
    b = c[2] * down(v, 1) + c[3] * up(v, 1)
    return (a + b) + (c[4] * zdown(v) + c[5] * zup(v))


def sweep(v, right, c, moves):
    return KEEP * v + c[7] * (right + around(v, c, moves))


def shifted(pair, parity, offset, cache):
    dx, dy, dz = offset
    source = (parity + dz) % 2
    lanes = dy + 16 * ((parity + dz - source) // 2)
    if (source, lanes) not in cache:
        value = pair[source]
        cache[source, lanes] = value if lanes == 0 else pltpu.roll(value, -lanes % 128, 1)
    value = cache[source, lanes]
    return value if dx == 0 else pltpu.roll(value, -dx % 8, 0)


def tree_sum(terms):
    while len(terms) > 1:
        terms = [a + b for a, b in zip(terms[::2], terms[1::2])] + terms[len(terms) & ~1 :]
    return terms[0]


def apply3(operator, pair, base):
    cache = {}
    out = []
    for parity in range(2):
        terms = [base[parity]]
        terms += [c[parity] * shifted(pair, parity, o, cache) for o, c in operator.items()]
        out.append(tree_sum(terms))
    return tuple(out)


def compose3(first, second):
    out = {}
    for o2, c2 in second.items():
        cache = {}
        for o1, c1 in first.items():
            term = [c1[parity] * shifted(c2, parity, o1, cache) for parity in range(2)]
            key = tuple(a + b for a, b in zip(o1, o2))
            out[key] = [a + b for a, b in zip(out[key], term)] if key in out else term
    return out


def kernel(
    props, doms, root, states, noise, source, out_ref,
    cur, nz, perm, src, cw, ce, cs, cn, cu, dg, cc, va, vb, tmp,
    perm1, right1, tmp1, co1, v1s, tmp2, gp2, gr2, co2, m3, tmp3, e2s,
    loc, s1, d1, s2, ss, ds_, sn, dn, sf, df, sq, dq, sp, dp, sr, dr, sg, dgs, word,
):
    me = lax.axis_index("prop")
    dom = lax.axis_index("dom")

    spread = lambda p: -min((p - root) % props, (root - p) % props)
    peers = sorted((p for p in range(props) if p != root), key=spread)

    def slab(o):
        return lax.rem(dom + (o + doms), doms)

    def remote(from_ref, to_ref, send, recv, p, d):
        return pltpu.make_async_remote_copy(
            src_ref=from_ref, dst_ref=to_ref, send_sem=send, recv_sem=recv,
            device_id=(p, d), device_id_type=MESH,
        )

    load_noise = pltpu.make_async_copy(noise, nz, loc.at[0])
    load_source = pltpu.make_async_copy(source, src.at[pl.ds(4, 4)], loc.at[1])
    load_noise.start()
    load_source.start()
    order = (1, 2, 3, 0)

    def load_plane(k):
        return pltpu.make_async_copy(states.at[k], cur.at[k], d1.at[k])

    barrier = pltpu.get_barrier_semaphore()

    @pl.when(me != root)
    def _():
        pl.semaphore_signal(barrier, inc=1, device_id=(root, dom), device_id_type=MESH)

    mate = me + 1 - 2 * lax.rem(me, 2)
    away = me // 2 != root // 2

    @pl.when(away)
    def _():
        pl.semaphore_signal(barrier, inc=1, device_id=(mate, dom), device_id_type=MESH)

    for o in (1, -1, 2, -2, 3, -3):
        pl.semaphore_signal(barrier, inc=1, device_id=(me, slab(o)), device_id_type=MESH)
    extra = jnp.where(me == root, props - 1, jnp.where(away, 1, 0))
    pl.semaphore_wait(barrier, 6 + extra)

    @pl.when(me == root)
    def _():
        for k in order:
            for p in peers:
                if p // 2 == root // 2 or p % 2 == k % 2:
                    remote(states.at[k], cur.at[k], s1.at[p, k], d1.at[k], p, dom).start()
            load_plane(k).start()

    reach = (3, 6, 12)

    def tell(i):
        for side, o in enumerate((reach[i], -reach[i])):
            target = (me, slab(o))
            pl.semaphore_signal(word.at[i, side], inc=1, device_id=target, device_id_type=MESH)

    def hear(i):
        for side in range(2):
            pl.semaphore_wait(word.at[i, side], 1)

    tell(0)

    sends_src = [
        remote(source, src.at[pl.ds(0, 4)], ss.at[0], ds_.at[0], me, slab(1)),
        remote(source, src.at[pl.ds(8, 4)], ss.at[1], ds_.at[1], me, slab(-1)),
    ]
    for copy in sends_src:
        copy.start()

    r01, l01 = iota((256, 128), 0), iota((256, 128), 1)
    c01 = ones_where(l01 == (r01 >> 1))
    r12, l12 = iota((512, 128), 0), iota((512, 128), 1)
    c12 = ones_where(((r12 >> 7) == (l12 >> 5)) & (((r12 & 63) >> 1) == (l12 & 31)))
    r23, l23 = iota((128, 256), 0), iota((128, 256), 1)
    c23 = ones_where(((r23 >> 6) == (l23 >> 7)) & (((r23 & 31) >> 1) == (l23 & 15)))
    r32, l32 = iota((256, 128), 0), iota((256, 128), 1)
    c32 = ones_where(((l32 >> 6) == (r32 >> 7)) & (((l32 & 31) >> 1) == (r32 & 15)))
    r21, l21 = iota((128, 512), 0), iota((128, 512), 1)
    c21 = ones_where(((r21 >> 5) == (l21 >> 7)) & ((r21 & 31) == ((l21 & 63) >> 1)))
    r10, l10 = iota((128, 256), 0), iota((128, 256), 1)
    c10 = ones_where(r10 == (l10 >> 1))
    row, lane = iota((64, 128), 0), iota((64, 128), 1)
    east_in, north_in = row < 63, lane < 127
    edges = jnp.where(row == 0, 1.0, 0.0) + jnp.where(row == 63, 1.0, 0.0)
    edges = edges + jnp.where(lane == 0, 1.0, 0.0) + jnp.where(lane == 127, 1.0, 0.0)

    load_noise.wait()
    hear(0)
    tell(1)
    for k in order:
        load_plane(k).wait()

        @pl.when(away & (lax.rem(me, 2) == k % 2))
        def _(k=k):
            remote(cur.at[k], cur.at[k], s2.at[k], d1.at[k], mate, dom).start()

        perm[4 + k] = jnp.exp(SHRINK * cur[k] + BETA * nz[k])
        here = perm.at[4 + k]
        if k > 0:
            remote(here, perm.at[k], sn.at[0], dn.at[0], me, slab(1)).start()
        if k < 3:
            remote(here, perm.at[8 + k], sf.at[0], df.at[0], me, slab(-1)).start()
    hear(1)
    tell(2)
    near = [
        remote(perm.at[pl.ds(5, 3)], perm.at[pl.ds(1, 3)], sn.at[0], dn.at[0], me, slab(1)),
        remote(perm.at[pl.ds(4, 3)], perm.at[pl.ds(8, 3)], sf.at[0], df.at[0], me, slab(-1)),
    ]
    far = [
        remote(perm.at[4], perm.at[0], sn.at[1], dn.at[1], me, slab(1)),
        remote(perm.at[7], perm.at[11], sf.at[1], df.at[1], me, slab(-1)),
    ]
    for copy in far:
        copy.start()

    def restrict01(planes):
        sums = []
        for i in range(2):
            tmp[...] = planes[2 * i] + planes[2 * i + 1]
            sums.append(pair_rows(tmp, 32))
        return dot3(jnp.concatenate(sums, axis=1), c01)

    def restrict12(value):
        tmp2[...] = value
        parts = []
        for q in range(4):
            low = tmp2[pl.ds(2 * q, 4, stride=8), :]
            parts.append(low + tmp2[pl.ds(2 * q + 1, 4, stride=8), :])
        return dot3(jnp.concatenate(parts, axis=1), c12)

    own1 = 0.125 * restrict01([perm[k] for k in range(4, 8)])
    perm1[3] = own1
    sends_q = []
    for i, o in enumerate((1, -1, 2, -2, 3, -3)):
        copy = remote(perm1.at[3], perm1.at[3 - o], sq.at[i], dq.at[i], me, slab(o))
        copy.start()
        sends_q.append(copy)
    gp2[dom] = 0.125 * restrict12(own1)

    def gather_to(buf, send, recv):
        def go(i, carry):
            step = (i + 1) // 2 * (2 * lax.rem(i, 2) - 1)
            remote(buf.at[dom], buf.at[dom], send, recv, me, slab(doms // 2 + step)).start()
            return carry

        lax.fori_loop(0, doms - 1, go, 0)

    def gather_wait(buf, send, recv):
        part = buf.at[pl.ds(0, doms - 1)]
        return remote(part, part, send, recv, me, slab(1))

    hear(2)
    gather_to(gp2, sp.at[0], dp.at[0])

    def sides(k):
        p = perm[k]
        east = jnp.where(east_in, harmonic(p, up(p, 0)), 0.0)
        north = jnp.where(north_in, harmonic(p, up(p, 1)), 0.0)
        ce[k] = east
        cn[k] = north
        cw[k] = down(east, 0)
        cs[k] = down(north, 1)

    inside_low = jnp.where(dom == 0, 0.0, 16.0)
    inside_high = jnp.where(dom == doms - 1, 0.0, 16.0)

    def face(k):
        factor = {3: inside_low, 7: inside_high}.get(k, 16.0)
        cu[k] = factor * harmonic(perm[k], perm[k + 1])

    def finish(k):
        diag = cw[k] + ce[k] + cs[k] + cn[k] + cu[k - 1] + cu[k] + edges * perm[k]
        dg[k] = diag
        scaled = OMEGA / diag
        cc[k] = scaled
        va[k] = scaled * src[k]

    def around0(v, k):
        x = v[k]
        a = cw[k] * down(x, 0) + ce[k] * up(x, 0)
        b = cs[k] * down(x, 1) + cn[k] * up(x, 1)
        return x, (a + b) + (cu[k - 1] * v[k - 1] + cu[k] * v[k + 1])

    def sweep0(v, k):
        x, total = around0(v, k)
        return KEEP * x + cc[k] * (src[k] + total)

    for k in range(4, 8):
        sides(k)
    for k in range(4, 7):
        face(k)
    load_source.wait()
    for copy in sends_src:
        copy.wait_recv()
    finish(5)
    finish(6)
    for copy in near:
        copy.wait_recv()
    for k in (2, 3, 8, 9):
        sides(k)
    for k in (1, 2, 3, 7, 8, 9):
        face(k)
    for k in (2, 3, 4, 7, 8, 9):
        finish(k)
    for k in range(3, 9):
        vb[k] = sweep0(va, k)
    rest = []
    for k in range(4, 8):
        x, total = around0(vb, k)
        rest.append(src[k] - dg[k] * x + total)
    right1[2] = restrict01(rest)
    sends_r = []
    for i, o in enumerate((1, -1, 2, -2)):
        copy = remote(right1.at[2], right1.at[2 - o], sr.at[i], dr.at[i], me, slab(o))
        copy.start()
        sends_r.append(copy)

    for copy in sends_q:
        copy.wait_recv()
    wide = perm1[...].reshape(7 * 32, 128)
    wide_row, wide_lane = iota(wide.shape, 0), iota(wide.shape, 1)
    pair = (dom + (doms - 3) + (wide_row >> 5)) & (doms - 1)
    top1 = (pair == doms - 1) & (wide_lane >= 64)
    coefs1 = flat_coefs(wide, 4.0, wide_row & 31, wide_lane & 63, 32, 64, MOVES1, top1)
    for i, value in enumerate(coefs1):
        co1[i] = value[32:192]

    for copy in sends_r[:2]:
        copy.wait_recv()
    b1 = right1[pl.ds(1, 3)].reshape(96, 128)
    inner = [co1[i, 32:128] for i in range(8)]
    v1 = sweep(inner[7] * b1, b1, inner, MOVES1)
    res1 = b1 - inner[6] * v1 + around(v1, inner, MOVES1)
    gr2[dom] = restrict12(res1[32:64])
    gather_to(gr2, sg.at[0], dgs.at[0])

    for copy in sends_r[2:]:
        copy.wait_recv()
    b1 = right1[...].reshape(160, 128)
    all1 = [co1[i] for i in range(8)]
    v1s[...] = sweep(all1[7] * b1, b1, all1, MOVES1)
    for copy in far:
        copy.wait_recv()
    for k in (1, 10):
        sides(k)
    for k in (0, 10):
        face(k)
    for k in (1, 10):
        finish(k)
    for k in (2, 9):
        vb[k] = sweep0(va, k)

    row8, row128 = iota((8, 128), 0), iota((128, 128), 0)
    lane8, lane128 = iota((8, 128), 1), iota((128, 128), 1)
    group = [(iota((8, 256), 1) & 127) >> 4 == g for g in range(8)]

    def restrict23(value):
        both = value + up(value, 0, 4)
        moved = down(both, 0, 4)
        parts = []
        for g in range(8):
            low, high = both[16 * g : 16 * g + 8], moved[16 * g + 8 : 16 * g + 16]
            parts.append(jnp.where(row8 < 4, low, high))
        y = dot3(jnp.concatenate(parts, axis=0), c23)
        total = tree_sum([jnp.where(group[g], y[8 * g : 8 * g + 8], 0.0) for g in range(8)])
        for parity in range(2):
            for q in range(2):
                piece = total[4 * parity : 4 * parity + 4, 128 * q : 128 * q + 128]
                tmp3[pl.ds(8 * parity + q, 4, stride=2), :] = piece
        return tmp3[pl.ds(0, 8), :], tmp3[pl.ds(8, 8), :]

    def prolong23(pair_):
        tmp3[pl.ds(0, 8), :] = pair_[0]
        tmp3[pl.ds(8, 8), :] = pair_[1]
        halves = []
        for q in range(2):
            rows = [tmp3[pl.ds(8 * parity + q, 4, stride=2), :] for parity in range(2)]
            halves.append(jnp.concatenate(rows, axis=0))
        e = jnp.concatenate(halves, axis=1)
        y = dot3(jnp.concatenate([jnp.where(m, e, 0.0) for m in group], axis=0), c32)
        parts = []
        for g in range(8):
            value = y[8 * g : 8 * g + 8]
            other = pltpu.roll(value, 4, 0)
            parts.append(jnp.where(row8 < 4, value, other))
            parts.append(jnp.where(row8 < 4, other, value))
        return jnp.concatenate(parts, axis=0)

    gather_wait(gp2, sp.at[0], dp.at[0]).wait_recv()
    p2 = gp2[...].reshape(128, 128)
    x2 = 4 * (row128 & 3) + (lane128 >> 5)
    coefs2 = flat_coefs(p2, 16.0, x2, lane128 & 31, 16, 32, MOVES2, row128 >= 124)
    for i, value in enumerate(coefs2):
        co2[i] = value
    pa, pb = restrict23(p2)
    pa, pb = 0.125 * pa, 0.125 * pb
    y3 = lane8 & 15
    scale = 64.0
    edges3 = jnp.where(row8 == 0, scale, 0.0) + jnp.where(row8 == 7, scale, 0.0)
    edges3 = edges3 + jnp.where(y3 == 0, scale, 0.0) + jnp.where(y3 == 15, scale, 0.0)

    def sides3(p):
        east = jnp.where(row8 < 7, scale * harmonic(p, up(p, 0)), 0.0)
        north = jnp.where(y3 < 15, scale * harmonic(p, up(p, 1)), 0.0)
        return [down(east, 0), east, down(north, 1), north]

    mid = (16.0 * scale) * harmonic(pa, pb)
    high = jnp.where(lane8 < 112, (16.0 * scale) * harmonic(pb, up(pa, 1, 16)), 0.0)
    low = down(high, 1, 16)
    ca = sides3(pa) + [low, mid]
    cb = sides3(pb) + [mid, high]

    def scaled3(c, p):
        total = (c[0] + c[1]) + (c[2] + c[3]) + (c[4] + c[5]) + edges3 * p
        inverse = OMEGA / total
        return inverse, [inverse * value for value in c]

    ia, ca = scaled3(ca, pa)
    ib, cb = scaled3(cb, pb)
    keep = jnp.full((8, 128), KEEP, F32)
    offsets = ((-1, 0, 0), (1, 0, 0), (0, -1, 0), (0, 1, 0), (0, 0, -1), (0, 0, 1))
    once = {(0, 0, 0): (keep, keep)}
    once.update({o: (a, b) for o, a, b in zip(offsets, ca, cb)})
    thrice = compose3(once, compose3(once, once))
    keys = list(thrice)
    for i, key in enumerate(keys):
        for parity in range(2):
            m3[parity, i] = thrice[key][parity]

    gather_wait(gr2, sg.at[0], dgs.at[0]).wait_recv()
    b2 = gr2[...].reshape(128, 128)
    all2 = [co2[i] for i in range(8)]
    v2 = sweep(all2[7] * b2, b2, all2, MOVES2)
    res2 = b2 - all2[6] * v2 + around(v2, all2, MOVES2)
    ra, rb = restrict23(res2)
    base = (ia * ra, ib * rb)
    right3 = base
    base = apply3(once, apply3(once, right3, right3), right3)

    def coarse(step, value):
        operator = {key: (m3[0, i], m3[1, i]) for i, key in enumerate(keys)}
        return apply3(operator, value, base)

    v2 = v2 + prolong23(lax.fori_loop(0, (COARSE_SWEEPS - 1) // 3, coarse, right3))
    for _ in range(2):
        v2 = sweep(v2, b2, all2, MOVES2)
    e2s[...] = v2

    parts = []
    for j in range(-2, 3):
        z = slab(j)
        value = e2s[pl.ds(pl.multiple_of((z // 2) * 8, 8), 8), :]
        parts.append(jnp.where(lax.rem(z, 2) == 0, value, pltpu.roll(value, 4, 0)))
    wide1 = dot3(jnp.concatenate(parts, axis=0), c21)
    for j in range(5):
        for q in range(4):
            piece = wide1[8 * j : 8 * j + 4, 128 * q : 128 * q + 128]
            for i in range(2):
                tmp1[pl.ds(32 * j + 2 * q + i, 4, stride=8), :] = piece
    v1 = v1s[...] + tmp1[...]
    b1 = right1[...].reshape(160, 128)
    all1 = [co1[i] for i in range(8)]
    for _ in range(2):
        v1 = sweep(v1, b1, all1, MOVES1)

    fine = dot3(v1[32:128], c10)
    for k, i, half in ((2, 0, 1), (4, 1, 0), (6, 1, 1), (8, 2, 0)):
        repeat_rows(tmp, fine[32 * i : 32 * i + 32, 128 * half : 128 * half + 128])
        add = tmp[...]
        vb[k] = vb[k] + add
        vb[k + 1] = vb[k + 1] + add
    for k in range(3, 9):
        va[k] = sweep0(vb, k)
    for k in range(4, 8):
        out_ref[k - 4] = sweep0(va, k)

    @pl.when(me == root)
    def _():
        for k in order:
            for p in peers:
                if p // 2 == root // 2 or p % 2 == k % 2:
                    remote(states.at[k], cur.at[k], s1.at[p, k], d1.at[k], p, dom).wait_send()

    for k in order:

        @pl.when(away & (lax.rem(me, 2) == k % 2))
        def _(k=k):
            remote(cur.at[k], cur.at[k], s2.at[k], d1.at[k], mate, dom).wait_send()

    for copies in (sends_src, near, far, sends_q, sends_r):
        for copy in copies:
            copy.wait_send()
    gather_wait(gp2, sp.at[0], dp.at[0]).wait_send()
    gather_wait(gr2, sg.at[0], dgs.at[0]).wait_send()


def body(states, accepted, noise, source):
    props, doms = lax.axis_size("prop"), lax.axis_size("dom")
    dma = pltpu.SemaphoreType.DMA
    plane = lambda n: pltpu.VMEM((n, 64, 128), F32)
    scratch = [
        plane(4), plane(4),
        plane(12), plane(12),
        plane(12), plane(12), plane(12), plane(12), plane(12), plane(12), plane(12),
        plane(12), plane(12),
        pltpu.VMEM((64, 128), F32),
        pltpu.VMEM((7, 32, 128), F32),
        pltpu.VMEM((5, 32, 128), F32),
        pltpu.VMEM((160, 128), F32),
        pltpu.VMEM((8, 160, 128), F32),
        pltpu.VMEM((160, 128), F32),
        pltpu.VMEM((32, 128), F32),
        pltpu.VMEM((doms, 4, 128), F32),
        pltpu.VMEM((doms, 4, 128), F32),
        pltpu.VMEM((8, 128, 128), F32),
        pltpu.VMEM((2, 63, 8, 128), F32),
        pltpu.VMEM((16, 128), F32),
        pltpu.VMEM((128, 128), F32),
        dma((2,)), dma((props, 4)), dma((4,)), dma((4,)),
        dma((2,)), dma((2,)), dma((2,)), dma((2,)), dma((2,)), dma((2,)),
        dma((6,)), dma((6,)), dma((1,)), dma((1,)), dma((4,)), dma((4,)), dma((1,)), dma((1,)),
        pltpu.SemaphoreType.REGULAR((3, 2)),
    ]
    hbm = pl.BlockSpec(memory_space=pl.ANY)

    def branch(root):
        return pl.pallas_call(
            functools.partial(kernel, props, doms, root),
            out_shape=pltpu.VMEM((4, 64, 128), F32),
            in_specs=[hbm, hbm, hbm],
            out_specs=pl.BlockSpec(memory_space=pltpu.VMEM),
            scratch_shapes=scratch,
            compiler_params=pltpu.CompilerParams(collective_id=root, has_side_effects=True),
            name=f"mcmc_step_{root}",
        )

    branches = [branch(root) for root in range(props)]
    return lax.switch(accepted[0], branches, states[0], noise[0], source)[None]


def solution(mesh):
    in_specs = (
        P("prop", "dom", None, None),
        P(),
        P("prop", "dom", None, None),
        P("dom", None, None),
    )
    out_specs = P("prop", "dom", None, None)
    return jax.shard_map(body, mesh=mesh, in_specs=in_specs, out_specs=out_specs, check_vma=False)
```

```python
import functools
import math

import jax
import jax.numpy as jnp
from jax import lax
from jax.experimental import pallas as pl
from jax.experimental.pallas import tpu as pltpu
from jax.sharding import PartitionSpec as P

OMEGA = 0.7
BETA = 0.4
SHRINK = math.sqrt(1.0 - BETA * BETA)
KEEP = 1.0 - OMEGA
COARSE_SWEEPS = 64
F32 = jnp.float32
BF16 = jnp.bfloat16
MESH = pl.DeviceIdType.MESH


def iota(shape, axis):
    return lax.broadcasted_iota(jnp.int32, shape, axis)


def ones_where(mask):
    return jnp.where(mask, 1.0, 0.0).astype(BF16)


def dot3(x, matrix):
    rows = x.shape[0]
    hi = x.astype(BF16).astype(F32)
    rest = x - hi
    mid = rest.astype(BF16).astype(F32)
    stacked = jnp.concatenate([hi, mid, rest - mid], axis=0).astype(BF16)
    y = jnp.dot(stacked, matrix, preferred_element_type=F32)
    return y[:rows] + y[rows : 2 * rows] + y[2 * rows :]


def up(v, axis, by=1):
    return pltpu.roll(v, v.shape[axis] - by, axis)


def down(v, axis, by=1):
    return pltpu.roll(v, by, axis)


def harmonic(a, b):
    return 2.0 * a * b / (a + b)


def pair_rows(ref, rows):
    return ref[pl.ds(0, rows, stride=2), :] + ref[pl.ds(1, rows, stride=2), :]


def repeat_rows(ref, value):
    rows = value.shape[0]
    ref[pl.ds(0, rows, stride=2), :] = value
    ref[pl.ds(1, rows, stride=2), :] = value


def zup1(v):
    swapped = pltpu.roll(v, 64, 1)
    return jnp.where(iota(v.shape, 1) < 64, swapped, up(swapped, 0, 32))


def zdown1(v):
    swapped = pltpu.roll(v, 64, 1)
    return jnp.where(iota(v.shape, 1) < 64, down(swapped, 0, 32), swapped)


def xup2(v):
    moved = up(v, 1, 32)
    return jnp.where(iota(v.shape, 1) < 96, moved, up(moved, 0))


def xdown2(v):
    moved = down(v, 1, 32)
    return jnp.where(iota(v.shape, 1) < 32, down(moved, 0), moved)


def zup2(v):
    return up(v, 0, 4)


def zdown2(v):
    return down(v, 0, 4)


def xup1(v):
    return up(v, 0)


def xdown1(v):
    return down(v, 0)


MOVES1 = (xdown1, xup1, zdown1, zup1)
MOVES2 = (xdown2, xup2, zdown2, zup2)


def flat_coefs(perm, scale, x, y, nx, ny, moves, top):
    xdown, xup, zdown, zup = moves
    east = jnp.where(x < nx - 1, scale * harmonic(perm, xup(perm)), 0.0)
    north = jnp.where(y < ny - 1, scale * harmonic(perm, up(perm, 1)), 0.0)
    above = jnp.where(top, 0.0, (16.0 * scale) * harmonic(perm, zup(perm)))
    west, south, below = xdown(east), down(north, 1), zdown(above)
    edges = jnp.where(x == 0, scale, 0.0) + jnp.where(x == nx - 1, scale, 0.0)
    edges = edges + jnp.where(y == 0, scale, 0.0) + jnp.where(y == ny - 1, scale, 0.0)
    diag = west + east + south + north + below + above + edges * perm
    return west, east, south, north, below, above, diag, OMEGA / diag


def around(v, c, moves):
    xdown, xup, zdown, zup = moves
    a = c[0] * xdown(v) + c[1] * xup(v)
    b = c[2] * down(v, 1) + c[3] * up(v, 1)
    return (a + b) + (c[4] * zdown(v) + c[5] * zup(v))


def sweep(v, right, c, moves):
    return KEEP * v + c[7] * (right + around(v, c, moves))


def shifted(pair, parity, offset, cache):
    dx, dy, dz = offset
    source = (parity + dz) % 2
    lanes = dy + 16 * ((parity + dz - source) // 2)
    if (source, lanes) not in cache:
        value = pair[source]
        cache[source, lanes] = value if lanes == 0 else pltpu.roll(value, -lanes % 128, 1)
    value = cache[source, lanes]
    return value if dx == 0 else pltpu.roll(value, -dx % 8, 0)


def tree_sum(terms):
    while len(terms) > 1:
        terms = [a + b for a, b in zip(terms[::2], terms[1::2])] + terms[len(terms) & ~1 :]
    return terms[0]


def apply3(operator, pair, base):
    cache = {}
    out = []
    for parity in range(2):
        terms = [base[parity]]
        terms += [c[parity] * shifted(pair, parity, o, cache) for o, c in operator.items()]
        out.append(tree_sum(terms))
    return tuple(out)


def compose3(first, second):
    out = {}
    for o2, c2 in second.items():
        cache = {}
        for o1, c1 in first.items():
            term = [c1[parity] * shifted(c2, parity, o1, cache) for parity in range(2)]
            key = tuple(a + b for a, b in zip(o1, o2))
            out[key] = [a + b for a, b in zip(out[key], term)] if key in out else term
    return out


def kernel(
    props, doms, root, states, noise, source, out_ref,
    cur, nz, perm, src, cw, ce, cs, cn, cu, dg, cc, va, vb, tmp,
    perm1, right1, tmp1, co1, v1s, tmp2, gp2, gr2, co2, m3, tmp3, e2s,
    loc, s1, d1, s2, ss, ds_, sn, dn, sf, sq, dq, sp, dp, sr, dr, sg, dgs, word, ready,
):
    me = lax.axis_index("prop")
    dom = lax.axis_index("dom")

    spread = lambda p: -min((p - root) % props, (root - p) % props)
    peers = sorted((p for p in range(props) if p != root), key=spread)

    def slab(o):
        return lax.rem(dom + (o + doms), doms)

    def remote(from_ref, to_ref, send, recv, p, d):
        return pltpu.make_async_remote_copy(
            src_ref=from_ref, dst_ref=to_ref, send_sem=send, recv_sem=recv,
            device_id=(p, d), device_id_type=MESH,
        )

    load_noise = pltpu.make_async_copy(noise, nz, loc.at[0])
    load_source = pltpu.make_async_copy(source, src.at[pl.ds(4, 4)], loc.at[1])
    load_noise.start()
    load_source.start()
    order = (1, 2, 3, 0)

    def load_plane(k):
        return pltpu.make_async_copy(states.at[k], cur.at[k], d1.at[k])

    barrier = pltpu.get_barrier_semaphore()

    mate = me + 1 - 2 * lax.rem(me, 2)
    away = me // 2 != root // 2
    relay = away & (lax.rem(me, 2) == 0)
    leads = relay | (me == root)

    @pl.when(relay)
    def _():
        pl.semaphore_signal(barrier, inc=1, device_id=(root, dom), device_id_type=MESH)

    @pl.when(leads)
    def _():
        pl.semaphore_signal(barrier, inc=1, device_id=(mate, dom), device_id_type=MESH)

    for o in (1, -1, 2, -2, 3, -3):
        pl.semaphore_signal(barrier, inc=1, device_id=(me, slab(o)), device_id_type=MESH)
    extra = jnp.where(me == root, props // 2 - 1, jnp.where(leads, 0, 1))
    pl.semaphore_wait(barrier, 6 + extra)

    @pl.when(jnp.logical_not(leads))
    def _():
        pl.semaphore_signal(ready, inc=1, device_id=(mate, dom), device_id_type=MESH)

    def across(k):
        return [
            remote(states.at[k], cur.at[k], s1.at[p, k], d1.at[k], p, dom)
            for p in peers
            if p // 2 != root // 2 and p % 2 == 0
        ]

    def hand_over(k, from_ref):
        return remote(from_ref, cur.at[k], s2.at[k], d1.at[k], mate, dom)

    @pl.when(me == root)
    def _():
        for k in order:
            for copy in across(k):
                copy.start()
            load_plane(k).start()

    reach = (3, 6, 12)

    def tell(i):
        for side, o in enumerate((reach[i], -reach[i])):
            target = (me, slab(o))
            pl.semaphore_signal(word.at[i, side], inc=1, device_id=target, device_id_type=MESH)

    def hear(i):
        for side in range(2):
            pl.semaphore_wait(word.at[i, side], 1)

    tell(0)

    sends_src = [
        remote(source.at[pl.ds(1, 3)], src.at[pl.ds(1, 3)], ss.at[0], ds_.at[0], me, slab(1)),
        remote(source.at[pl.ds(0, 3)], src.at[pl.ds(8, 3)], ss.at[1], ds_.at[1], me, slab(-1)),
    ]
    for copy in sends_src:
        copy.start()

    r01, l01 = iota((256, 128), 0), iota((256, 128), 1)
    c01 = ones_where(l01 == (r01 >> 1))
    r12, l12 = iota((512, 128), 0), iota((512, 128), 1)
    c12 = ones_where(((r12 >> 7) == (l12 >> 5)) & (((r12 & 63) >> 1) == (l12 & 31)))
    r23, l23 = iota((128, 256), 0), iota((128, 256), 1)
    c23 = ones_where(((r23 >> 6) == (l23 >> 7)) & (((r23 & 31) >> 1) == (l23 & 15)))
    r32, l32 = iota((256, 128), 0), iota((256, 128), 1)
    c32 = ones_where(((l32 >> 6) == (r32 >> 7)) & (((l32 & 31) >> 1) == (r32 & 15)))
    r21, l21 = iota((128, 512), 0), iota((128, 512), 1)
    c21 = ones_where(((r21 >> 5) == (l21 >> 7)) & ((r21 & 31) == ((l21 & 63) >> 1)))
    r10, l10 = iota((128, 256), 0), iota((128, 256), 1)
    c10 = ones_where(r10 == (l10 >> 1))
    row, lane = iota((64, 128), 0), iota((64, 128), 1)
    east_in, north_in = row < 63, lane < 127
    edges = jnp.where(row == 0, 1.0, 0.0) + jnp.where(row == 63, 1.0, 0.0)
    edges = edges + jnp.where(lane == 0, 1.0, 0.0) + jnp.where(lane == 127, 1.0, 0.0)

    load_noise.wait()
    hear(0)
    tell(1)
    @pl.when(me == root)
    def _():
        pl.semaphore_wait(ready, 1)
        for k in order:
            hand_over(k, states.at[k]).start()

    for k in order:
        load_plane(k).wait()

        @pl.when(relay)
        def _(k=k):
            if k == order[0]:
                pl.semaphore_wait(ready, 1)
            hand_over(k, cur.at[k]).start()

        perm[4 + k] = jnp.exp(SHRINK * cur[k] + BETA * nz[k])
        here = perm.at[4 + k]
        if k > 0:
            remote(here, perm.at[k], sn.at[k], dn.at[k], me, slab(1)).start()
        if k < 3:
            remote(here, perm.at[8 + k], sf.at[k], dn.at[8 + k], me, slab(-1)).start()
    hear(1)
    tell(2)
    near = {k: remote(perm.at[4 + k], perm.at[k], sn.at[k], dn.at[k], me, slab(1)) for k in (1, 2, 3)}
    for k in (0, 1, 2):
        near[8 + k] = remote(perm.at[4 + k], perm.at[8 + k], sf.at[k], dn.at[8 + k], me, slab(-1))
    far = [
        remote(perm.at[4], perm.at[0], sn.at[0], dn.at[0], me, slab(1)),
        remote(perm.at[7], perm.at[11], sf.at[3], dn.at[11], me, slab(-1)),
    ]
    for copy in far:
        copy.start()

    def restrict01(planes):
        sums = []
        for i in range(2):
            tmp[...] = planes[2 * i] + planes[2 * i + 1]
            sums.append(pair_rows(tmp, 32))
        return dot3(jnp.concatenate(sums, axis=1), c01)

    def restrict12(value):
        tmp2[...] = value
        parts = []
        for q in range(4):
            low = tmp2[pl.ds(2 * q, 4, stride=8), :]
            parts.append(low + tmp2[pl.ds(2 * q + 1, 4, stride=8), :])
        return dot3(jnp.concatenate(parts, axis=1), c12)

    own1 = 0.125 * restrict01([perm[k] for k in range(4, 8)])
    perm1[3] = own1
    sends_q = []
    for i, o in enumerate((1, -1, 2, -2, 3, -3)):
        copy = remote(perm1.at[3], perm1.at[3 - o], sq.at[i], dq.at[i], me, slab(o))
        copy.start()
        sends_q.append(copy)
    gp2[dom] = 0.125 * restrict12(own1)

    def gather_to(buf, send, recv):
        def go(i, carry):
            step = (i + 1) // 2 * (2 * lax.rem(i, 2) - 1)
            remote(buf.at[dom], buf.at[dom], send, recv, me, slab(doms // 2 + step)).start()
            return carry

        lax.fori_loop(0, doms - 1, go, 0)

    def gather_wait(buf, send, recv):
        part = buf.at[pl.ds(0, doms - 1)]
        return remote(part, part, send, recv, me, slab(1))

    hear(2)
    gather_to(gp2, sp.at[0], dp.at[0])

    def sides(k):
        p = perm[k]
        east = jnp.where(east_in, harmonic(p, up(p, 0)), 0.0)
        north = jnp.where(north_in, harmonic(p, up(p, 1)), 0.0)
        ce[k] = east
        cn[k] = north
        cw[k] = down(east, 0)
        cs[k] = down(north, 1)

    inside_low = jnp.where(dom == 0, 0.0, 16.0)
    inside_high = jnp.where(dom == doms - 1, 0.0, 16.0)

    def face(k):
        factor = {3: inside_low, 7: inside_high}.get(k, 16.0)
        cu[k] = factor * harmonic(perm[k], perm[k + 1])

    def finish(k):
        diag = cw[k] + ce[k] + cs[k] + cn[k] + cu[k - 1] + cu[k] + edges * perm[k]
        dg[k] = diag
        scaled = OMEGA / diag
        cc[k] = scaled
        va[k] = scaled * src[k]

    def around0(v, k):
        x = v[k]
        a = cw[k] * down(x, 0) + ce[k] * up(x, 0)
        b = cs[k] * down(x, 1) + cn[k] * up(x, 1)
        return x, (a + b) + (cu[k - 1] * v[k - 1] + cu[k] * v[k + 1])

    def sweep0(v, k):
        x, total = around0(v, k)
        return KEEP * x + cc[k] * (src[k] + total)

    for k in range(4, 8):
        sides(k)
    for k in range(4, 7):
        face(k)
    load_source.wait()
    for copy in sends_src:
        copy.wait_recv()
    finish(5)
    finish(6)
    for k in (1, 2, 9, 10):
        near[k].wait_recv()
    for k in (2, 9):
        sides(k)
    for k in (1, 9):
        face(k)
    for k in (3, 8):
        near[k].wait_recv()
    for k in (3, 8):
        sides(k)
    for k in (2, 3, 7, 8):
        face(k)
    for k in (2, 3, 4, 7, 8, 9):
        finish(k)
    for k in range(3, 9):
        vb[k] = sweep0(va, k)
    rest = []
    for k in range(4, 8):
        x, total = around0(vb, k)
        rest.append(src[k] - dg[k] * x + total)
    right1[2] = restrict01(rest)
    sends_r = []
    for i, o in enumerate((1, -1, 2, -2)):
        copy = remote(right1.at[2], right1.at[2 - o], sr.at[i], dr.at[i], me, slab(o))
        copy.start()
        sends_r.append(copy)

    for copy in sends_q:
        copy.wait_recv()
    wide = perm1[...].reshape(7 * 32, 128)
    wide_row, wide_lane = iota(wide.shape, 0), iota(wide.shape, 1)
    pair = (dom + (doms - 3) + (wide_row >> 5)) & (doms - 1)
    top1 = (pair == doms - 1) & (wide_lane >= 64)
    coefs1 = flat_coefs(wide, 4.0, wide_row & 31, wide_lane & 63, 32, 64, MOVES1, top1)
    for i, value in enumerate(coefs1):
        co1[i] = value[32:192]

    for copy in sends_r[:2]:
        copy.wait_recv()
    b1 = right1[pl.ds(1, 3)].reshape(96, 128)
    inner = [co1[i, 32:128] for i in range(8)]
    v1 = sweep(inner[7] * b1, b1, inner, MOVES1)
    res1 = b1 - inner[6] * v1 + around(v1, inner, MOVES1)
    gr2[dom] = restrict12(res1[32:64])
    gather_to(gr2, sg.at[0], dgs.at[0])

    for copy in sends_r[2:]:
        copy.wait_recv()
    b1 = right1[...].reshape(160, 128)
    all1 = [co1[i] for i in range(8)]
    v1s[...] = sweep(all1[7] * b1, b1, all1, MOVES1)
    for copy in far:
        copy.wait_recv()
    for k in (1, 10):
        sides(k)
    for k in (0, 10):
        face(k)
    for k in (1, 10):
        finish(k)
    for k in (2, 9):
        vb[k] = sweep0(va, k)

    row8, row128 = iota((8, 128), 0), iota((128, 128), 0)
    lane8, lane128 = iota((8, 128), 1), iota((128, 128), 1)
    group = [(iota((8, 256), 1) & 127) >> 4 == g for g in range(8)]

    def restrict23(value):
        both = value + up(value, 0, 4)
        moved = down(both, 0, 4)
        parts = []
        for g in range(8):
            low, high = both[16 * g : 16 * g + 8], moved[16 * g + 8 : 16 * g + 16]
            parts.append(jnp.where(row8 < 4, low, high))
        y = dot3(jnp.concatenate(parts, axis=0), c23)
        total = tree_sum([jnp.where(group[g], y[8 * g : 8 * g + 8], 0.0) for g in range(8)])
        for parity in range(2):
            for q in range(2):
                piece = total[4 * parity : 4 * parity + 4, 128 * q : 128 * q + 128]
                tmp3[pl.ds(8 * parity + q, 4, stride=2), :] = piece
        return tmp3[pl.ds(0, 8), :], tmp3[pl.ds(8, 8), :]

    def prolong23(pair_):
        tmp3[pl.ds(0, 8), :] = pair_[0]
        tmp3[pl.ds(8, 8), :] = pair_[1]
        halves = []
        for q in range(2):
            rows = [tmp3[pl.ds(8 * parity + q, 4, stride=2), :] for parity in range(2)]
            halves.append(jnp.concatenate(rows, axis=0))
        e = jnp.concatenate(halves, axis=1)
        y = dot3(jnp.concatenate([jnp.where(m, e, 0.0) for m in group], axis=0), c32)
        parts = []
        for g in range(8):
            value = y[8 * g : 8 * g + 8]
            other = pltpu.roll(value, 4, 0)
            parts.append(jnp.where(row8 < 4, value, other))
            parts.append(jnp.where(row8 < 4, other, value))
        return jnp.concatenate(parts, axis=0)

    gather_wait(gp2, sp.at[0], dp.at[0]).wait_recv()
    p2 = gp2[...].reshape(128, 128)
    x2 = 4 * (row128 & 3) + (lane128 >> 5)
    coefs2 = flat_coefs(p2, 16.0, x2, lane128 & 31, 16, 32, MOVES2, row128 >= 124)
    for i, value in enumerate(coefs2):
        co2[i] = value
    pa, pb = restrict23(p2)
    pa, pb = 0.125 * pa, 0.125 * pb
    y3 = lane8 & 15
    scale = 64.0
    edges3 = jnp.where(row8 == 0, scale, 0.0) + jnp.where(row8 == 7, scale, 0.0)
    edges3 = edges3 + jnp.where(y3 == 0, scale, 0.0) + jnp.where(y3 == 15, scale, 0.0)

    def sides3(p):
        east = jnp.where(row8 < 7, scale * harmonic(p, up(p, 0)), 0.0)
        north = jnp.where(y3 < 15, scale * harmonic(p, up(p, 1)), 0.0)
        return [down(east, 0), east, down(north, 1), north]

    mid = (16.0 * scale) * harmonic(pa, pb)
    high = jnp.where(lane8 < 112, (16.0 * scale) * harmonic(pb, up(pa, 1, 16)), 0.0)
    low = down(high, 1, 16)
    ca = sides3(pa) + [low, mid]
    cb = sides3(pb) + [mid, high]

    def scaled3(c, p):
        total = (c[0] + c[1]) + (c[2] + c[3]) + (c[4] + c[5]) + edges3 * p
        inverse = OMEGA / total
        return inverse, [inverse * value for value in c]

    ia, ca = scaled3(ca, pa)
    ib, cb = scaled3(cb, pb)
    keep = jnp.full((8, 128), KEEP, F32)
    offsets = ((-1, 0, 0), (1, 0, 0), (0, -1, 0), (0, 1, 0), (0, 0, -1), (0, 0, 1))
    once = {(0, 0, 0): (keep, keep)}
    once.update({o: (a, b) for o, a, b in zip(offsets, ca, cb)})
    thrice = compose3(once, compose3(once, once))
    keys = list(thrice)
    for i, key in enumerate(keys):
        for parity in range(2):
            m3[parity, i] = thrice[key][parity]

    gather_wait(gr2, sg.at[0], dgs.at[0]).wait_recv()
    b2 = gr2[...].reshape(128, 128)
    all2 = [co2[i] for i in range(8)]
    v2 = sweep(all2[7] * b2, b2, all2, MOVES2)
    res2 = b2 - all2[6] * v2 + around(v2, all2, MOVES2)
    ra, rb = restrict23(res2)
    base = (ia * ra, ib * rb)
    right3 = base
    base = apply3(once, apply3(once, right3, right3), right3)

    def coarse(step, value):
        operator = {key: (m3[0, i], m3[1, i]) for i, key in enumerate(keys)}
        return apply3(operator, value, base)

    v2 = v2 + prolong23(lax.fori_loop(0, (COARSE_SWEEPS - 1) // 3, coarse, right3))
    for _ in range(2):
        v2 = sweep(v2, b2, all2, MOVES2)
    e2s[...] = v2

    parts = []
    for j in range(-2, 3):
        z = slab(j)
        value = e2s[pl.ds(pl.multiple_of((z // 2) * 8, 8), 8), :]
        parts.append(jnp.where(lax.rem(z, 2) == 0, value, pltpu.roll(value, 4, 0)))
    wide1 = dot3(jnp.concatenate(parts, axis=0), c21)
    for j in range(5):
        for q in range(4):
            piece = wide1[8 * j : 8 * j + 4, 128 * q : 128 * q + 128]
            for i in range(2):
                tmp1[pl.ds(32 * j + 2 * q + i, 4, stride=8), :] = piece
    v1 = v1s[...] + tmp1[...]
    b1 = right1[...].reshape(160, 128)
    all1 = [co1[i] for i in range(8)]
    for _ in range(2):
        v1 = sweep(v1, b1, all1, MOVES1)

    fine = dot3(v1[32:128], c10)
    for k, i, half in ((2, 0, 1), (4, 1, 0), (6, 1, 1), (8, 2, 0)):
        repeat_rows(tmp, fine[32 * i : 32 * i + 32, 128 * half : 128 * half + 128])
        add = tmp[...]
        vb[k] = vb[k] + add
        vb[k + 1] = vb[k + 1] + add
    for k in range(3, 9):
        va[k] = sweep0(vb, k)
    for k in range(4, 8):
        out_ref[k - 4] = sweep0(va, k)

    @pl.when(me == root)
    def _():
        for k in order:
            for copy in across(k):
                copy.wait_send()

    @pl.when(leads)
    def _():
        for k in order:
            hand_over(k, cur.at[k]).wait_send()

    for copies in (sends_src, near.values(), far, sends_q, sends_r):
        for copy in copies:
            copy.wait_send()
    gather_wait(gp2, sp.at[0], dp.at[0]).wait_send()
    gather_wait(gr2, sg.at[0], dgs.at[0]).wait_send()


def body(states, accepted, noise, source):
    props, doms = lax.axis_size("prop"), lax.axis_size("dom")
    dma = pltpu.SemaphoreType.DMA
    plane = lambda n: pltpu.VMEM((n, 64, 128), F32)
    scratch = [
        plane(4), plane(4),
        plane(12), plane(12),
        plane(12), plane(12), plane(12), plane(12), plane(12), plane(12), plane(12),
        plane(12), plane(12),
        pltpu.VMEM((64, 128), F32),
        pltpu.VMEM((7, 32, 128), F32),
        pltpu.VMEM((5, 32, 128), F32),
        pltpu.VMEM((160, 128), F32),
        pltpu.VMEM((8, 160, 128), F32),
        pltpu.VMEM((160, 128), F32),
        pltpu.VMEM((32, 128), F32),
        pltpu.VMEM((doms, 4, 128), F32),
        pltpu.VMEM((doms, 4, 128), F32),
        pltpu.VMEM((8, 128, 128), F32),
        pltpu.VMEM((2, 63, 8, 128), F32),
        pltpu.VMEM((16, 128), F32),
        pltpu.VMEM((128, 128), F32),
        dma((2,)), dma((props, 4)), dma((4,)), dma((4,)),
        dma((2,)), dma((2,)), dma((4,)), dma((12,)), dma((4,)),
        dma((6,)), dma((6,)), dma((1,)), dma((1,)), dma((4,)), dma((4,)), dma((1,)), dma((1,)),
        pltpu.SemaphoreType.REGULAR((3, 2)),
        pltpu.SemaphoreType.REGULAR,
    ]
    hbm = pl.BlockSpec(memory_space=pl.ANY)

    def branch(root):
        return pl.pallas_call(
            functools.partial(kernel, props, doms, root),
            out_shape=pltpu.VMEM((4, 64, 128), F32),
            in_specs=[hbm, hbm, hbm],
            out_specs=pl.BlockSpec(memory_space=pltpu.VMEM),
            scratch_shapes=scratch,
            compiler_params=pltpu.CompilerParams(collective_id=root, has_side_effects=True),
            name=f"mcmc_step_{root}",
        )

    branches = [branch(root) for root in range(props)]
    return lax.switch(accepted[0], branches, states[0], noise[0], source)[None]


def solution(mesh):
    in_specs = (
        P("prop", "dom", None, None),
        P(),
        P("prop", "dom", None, None),
        P("dom", None, None),
    )
    out_specs = P("prop", "dom", None, None)
    return jax.shard_map(body, mesh=mesh, in_specs=in_specs, out_specs=out_specs, check_vma=False)
```

```python
import functools
import math

import jax
import jax.numpy as jnp
from jax import lax
from jax.experimental import pallas as pl
from jax.experimental.pallas import tpu as pltpu
from jax.sharding import PartitionSpec as P

OMEGA = 0.7
BETA = 0.4
SHRINK = math.sqrt(1.0 - BETA * BETA)
KEEP = 1.0 - OMEGA
COARSE_SWEEPS = 64
F32 = jnp.float32
BF16 = jnp.bfloat16
MESH = pl.DeviceIdType.MESH


def iota(shape, axis):
    return lax.broadcasted_iota(jnp.int32, shape, axis)


def ones_where(mask):
    return jnp.where(mask, 1.0, 0.0).astype(BF16)


def dot2(x, matrix):
    rows = x.shape[0]
    hi = x.astype(BF16).astype(F32)
    stacked = jnp.concatenate([hi, x - hi], axis=0).astype(BF16)
    y = jnp.dot(stacked, matrix, preferred_element_type=F32)
    return y[:rows] + y[rows:]


def up(v, axis, by=1):
    return pltpu.roll(v, v.shape[axis] - by, axis)


def down(v, axis, by=1):
    return pltpu.roll(v, by, axis)


def harmonic(a, b):
    return 2.0 * a * b / (a + b)


def pair_rows(ref, rows):
    return ref[pl.ds(0, rows, stride=2), :] + ref[pl.ds(1, rows, stride=2), :]


def repeat_rows(ref, value):
    rows = value.shape[0]
    ref[pl.ds(0, rows, stride=2), :] = value
    ref[pl.ds(1, rows, stride=2), :] = value


def zup1(v):
    swapped = pltpu.roll(v, 64, 1)
    return jnp.where(iota(v.shape, 1) < 64, swapped, up(swapped, 0, 32))


def zdown1(v):
    swapped = pltpu.roll(v, 64, 1)
    return jnp.where(iota(v.shape, 1) < 64, down(swapped, 0, 32), swapped)


def xup2(v):
    moved = up(v, 1, 32)
    return jnp.where(iota(v.shape, 1) < 96, moved, up(moved, 0))


def xdown2(v):
    moved = down(v, 1, 32)
    return jnp.where(iota(v.shape, 1) < 32, down(moved, 0), moved)


def zup2(v):
    return up(v, 0, 4)


def zdown2(v):
    return down(v, 0, 4)


def xup1(v):
    return up(v, 0)


def xdown1(v):
    return down(v, 0)


MOVES1 = (xdown1, xup1, zdown1, zup1)
MOVES2 = (xdown2, xup2, zdown2, zup2)


def flat_coefs(perm, scale, x, y, nx, ny, moves, top):
    xdown, xup, zdown, zup = moves
    east = jnp.where(x < nx - 1, scale * harmonic(perm, xup(perm)), 0.0)
    north = jnp.where(y < ny - 1, scale * harmonic(perm, up(perm, 1)), 0.0)
    above = jnp.where(top, 0.0, (16.0 * scale) * harmonic(perm, zup(perm)))
    west, south, below = xdown(east), down(north, 1), zdown(above)
    edges = jnp.where(x == 0, scale, 0.0) + jnp.where(x == nx - 1, scale, 0.0)
    edges = edges + jnp.where(y == 0, scale, 0.0) + jnp.where(y == ny - 1, scale, 0.0)
    diag = west + east + south + north + below + above + edges * perm
    return west, east, south, north, below, above, diag, OMEGA / diag


def around(v, c, moves):
    xdown, xup, zdown, zup = moves
    a = c[0] * xdown(v) + c[1] * xup(v)
    b = c[2] * down(v, 1) + c[3] * up(v, 1)
    return (a + b) + (c[4] * zdown(v) + c[5] * zup(v))


def sweep(v, right, c, moves):
    return KEEP * v + c[7] * (right + around(v, c, moves))


def shifted(pair, parity, offset, cache):
    dx, dy, dz = offset
    source = (parity + dz) % 2
    lanes = dy + 16 * ((parity + dz - source) // 2)
    if (source, lanes) not in cache:
        value = pair[source]
        cache[source, lanes] = value if lanes == 0 else pltpu.roll(value, -lanes % 128, 1)
    value = cache[source, lanes]
    return value if dx == 0 else pltpu.roll(value, -dx % 8, 0)


def tree_sum(terms):
    while len(terms) > 1:
        terms = [a + b for a, b in zip(terms[::2], terms[1::2])] + terms[len(terms) & ~1 :]
    return terms[0]


def apply3(operator, pair, base):
    cache = {}
    out = []
    for parity in range(2):
        terms = [base[parity]]
        terms += [c[parity] * shifted(pair, parity, o, cache) for o, c in operator.items()]
        out.append(tree_sum(terms))
    return tuple(out)


def compose3(first, second):
    out = {}
    for o2, c2 in second.items():
        cache = {}
        for o1, c1 in first.items():
            term = [c1[parity] * shifted(c2, parity, o1, cache) for parity in range(2)]
            key = tuple(a + b for a, b in zip(o1, o2))
            out[key] = [a + b for a, b in zip(out[key], term)] if key in out else term
    return out


def kernel(
    props, doms, root, states, noise, source, out_ref,
    cur, nz, perm, src, cw, ce, cs, cn, cu, dg, cc, va, vb, tmp,
    perm1, right1, tmp1, co1, v1s, tmp2, gp2, gr2, co2, m3, tmp3, e2s,
    loc, s1, d1, s2, ss, ds_, sn, dn, sf, sq, dq, sp, dp, sr, dr, sg, dgs, word, ready,
):
    me = lax.axis_index("prop")
    dom = lax.axis_index("dom")

    spread = lambda p: -min((p - root) % props, (root - p) % props)
    peers = sorted((p for p in range(props) if p != root), key=spread)

    def slab(o):
        return lax.rem(dom + (o + doms), doms)

    def remote(from_ref, to_ref, send, recv, p, d):
        return pltpu.make_async_remote_copy(
            src_ref=from_ref, dst_ref=to_ref, send_sem=send, recv_sem=recv,
            device_id=(p, d), device_id_type=MESH,
        )

    def within(o):
        return (dom + o >= 0) & (dom + o < doms)

    class Along:
        def __init__(self, from_ref, to_ref, send, recv, o):
            self.copy = remote(from_ref, to_ref, send, recv, me, slab(o))
            self.to, self.source = within(o), within(-o)

        def start(self):
            pl.when(self.to)(self.copy.start)

        def wait_send(self):
            pl.when(self.to)(self.copy.wait_send)

        def wait_recv(self):
            pl.when(self.source)(self.copy.wait_recv)

    @pl.when((dom < 3) | (dom >= doms - 3))
    def _():
        for first in (0, 8):
            perm[pl.ds(first, 4)] = jnp.ones((4, 64, 128), F32)
            src[pl.ds(first, 4)] = jnp.zeros((4, 64, 128), F32)
        perm1[...] = jnp.ones(perm1.shape, F32)
        right1[...] = jnp.zeros(right1.shape, F32)

    load_noise = pltpu.make_async_copy(noise, nz, loc.at[0])
    load_source = pltpu.make_async_copy(source, src.at[pl.ds(4, 4)], loc.at[1])
    load_noise.start()
    load_source.start()
    order = (1, 2, 3, 0)

    def load_plane(k):
        return pltpu.make_async_copy(states.at[k], cur.at[k], d1.at[k])

    barrier = pltpu.get_barrier_semaphore()

    mate = me + 1 - 2 * lax.rem(me, 2)
    away = me // 2 != root // 2
    relay = away & (lax.rem(me, 2) == 0)
    leads = relay | (me == root)

    @pl.when(relay)
    def _():
        pl.semaphore_signal(barrier, inc=1, device_id=(root, dom), device_id_type=MESH)

    @pl.when(leads)
    def _():
        pl.semaphore_signal(barrier, inc=1, device_id=(mate, dom), device_id_type=MESH)

    for o in (1, -1, 2, -2, 3, -3, 4, -4):

        @pl.when(within(o))
        def _(o=o):
            pl.semaphore_signal(barrier, inc=1, device_id=(me, slab(o)), device_id_type=MESH)

    beside = jnp.minimum(dom, 4) + jnp.minimum(doms - 1 - dom, 4)
    extra = jnp.where(me == root, props // 2 - 1, jnp.where(leads, 0, 1))
    pl.semaphore_wait(barrier, beside + extra)

    @pl.when(jnp.logical_not(leads))
    def _():
        pl.semaphore_signal(ready, inc=1, device_id=(mate, dom), device_id_type=MESH)

    def across(k):
        return [
            remote(states.at[k], cur.at[k], s1.at[p, k], d1.at[k], p, dom)
            for p in peers
            if p // 2 != root // 2 and p % 2 == 0
        ]

    def hand_over(k, from_ref):
        return remote(from_ref, cur.at[k], s2.at[k], d1.at[k], mate, dom)

    @pl.when(me == root)
    def _():
        for k in order:
            for copy in across(k):
                copy.start()
            load_plane(k).start()

    reach = (4, 8, 16)

    def tell(i):
        for side, o in enumerate((reach[i], -reach[i])):

            @pl.when(within(o))
            def _(side=side, o=o):
                target = (me, slab(o))
                pl.semaphore_signal(word.at[i, side], inc=1, device_id=target, device_id_type=MESH)

    def hear(i):
        for side, o in enumerate((reach[i], -reach[i])):

            @pl.when(within(-o))
            def _(side=side):
                pl.semaphore_wait(word.at[i, side], 1)

    tell(0)

    sends_src = [
        Along(source.at[pl.ds(1, 3)], src.at[pl.ds(1, 3)], ss.at[0], ds_.at[0], 1),
        Along(source.at[pl.ds(0, 3)], src.at[pl.ds(8, 3)], ss.at[1], ds_.at[1], -1),
    ]
    for copy in sends_src:
        copy.start()

    r01, l01 = iota((256, 128), 0), iota((256, 128), 1)
    c01 = ones_where(l01 == (r01 >> 1))
    r12, l12 = iota((512, 128), 0), iota((512, 128), 1)
    c12 = ones_where(((r12 >> 7) == (l12 >> 5)) & (((r12 & 63) >> 1) == (l12 & 31)))
    r23, l23 = iota((128, 256), 0), iota((128, 256), 1)
    c23 = ones_where(((r23 >> 6) == (l23 >> 7)) & (((r23 & 31) >> 1) == (l23 & 15)))
    r32, l32 = iota((256, 128), 0), iota((256, 128), 1)
    c32 = ones_where(((l32 >> 6) == (r32 >> 7)) & (((l32 & 31) >> 1) == (r32 & 15)))
    r21, l21 = iota((128, 512), 0), iota((128, 512), 1)
    c21 = ones_where(((r21 >> 5) == (l21 >> 7)) & ((r21 & 31) == ((l21 & 63) >> 1)))
    r10, l10 = iota((128, 256), 0), iota((128, 256), 1)
    c10 = ones_where(r10 == (l10 >> 1))
    row, lane = iota((64, 128), 0), iota((64, 128), 1)
    east_in, north_in = row < 63, lane < 127
    edges = jnp.where(row == 0, 1.0, 0.0) + jnp.where(row == 63, 1.0, 0.0)
    edges = edges + jnp.where(lane == 0, 1.0, 0.0) + jnp.where(lane == 127, 1.0, 0.0)

    load_noise.wait()
    @pl.when(me == root)
    def _():
        pl.semaphore_wait(ready, 1)
        for k in order:
            hand_over(k, states.at[k]).start()

    near = {k: Along(perm.at[4 + k], perm.at[k], sn.at[k], dn.at[k], 1) for k in (1, 2, 3)}
    for k in (0, 1, 2):
        near[8 + k] = Along(perm.at[4 + k], perm.at[8 + k], sf.at[k], dn.at[8 + k], -1)

    for k in order:
        load_plane(k).wait()

        @pl.when(relay)
        def _(k=k):
            if k == order[0]:
                pl.semaphore_wait(ready, 1)
            hand_over(k, cur.at[k]).start()

        perm[4 + k] = jnp.exp(SHRINK * cur[k] + BETA * nz[k])
        if k > 0:
            near[k].start()
        if k < 3:
            near[8 + k].start()
    hear(0)
    tell(1)
    far = [
        Along(perm.at[4], perm.at[0], sn.at[0], dn.at[0], 1),
        Along(perm.at[7], perm.at[11], sf.at[3], dn.at[11], -1),
    ]
    for copy in far:
        copy.start()

    def restrict01(planes):
        sums = []
        for i in range(2):
            tmp[...] = planes[2 * i] + planes[2 * i + 1]
            sums.append(pair_rows(tmp, 32))
        return dot2(jnp.concatenate(sums, axis=1), c01)

    def restrict12(value):
        tmp2[...] = value
        parts = []
        for q in range(4):
            low = tmp2[pl.ds(2 * q, 4, stride=8), :]
            parts.append(low + tmp2[pl.ds(2 * q + 1, 4, stride=8), :])
        return dot2(jnp.concatenate(parts, axis=1), c12)

    own1 = 0.125 * restrict01([perm[k] for k in range(4, 8)])
    perm1[3] = own1
    sends_q = []
    for i, o in enumerate((1, -1, 2, -2, 3, -3)):
        copy = Along(perm1.at[3], perm1.at[3 - o], sq.at[i], dq.at[i], o)
        copy.start()
        sends_q.append(copy)
    hear(1)
    tell(2)
    gp2[dom] = 0.125 * restrict12(own1)

    def gather_to(buf, send, recv):
        def go(i, carry):
            step = (i + 1) // 2 * (2 * lax.rem(i, 2) - 1)
            remote(buf.at[dom], buf.at[dom], send, recv, me, slab(doms // 2 + step)).start()
            return carry

        lax.fori_loop(0, doms - 1, go, 0)

    def gather_wait(buf, send, recv):
        part = buf.at[pl.ds(0, doms - 1)]
        return remote(part, part, send, recv, me, slab(1))


    def sides(k):
        p = perm[k]
        east = jnp.where(east_in, harmonic(p, up(p, 0)), 0.0)
        north = jnp.where(north_in, harmonic(p, up(p, 1)), 0.0)
        ce[k] = east
        cn[k] = north
        cw[k] = down(east, 0)
        cs[k] = down(north, 1)

    inside_low = jnp.where(dom == 0, 0.0, 16.0)
    inside_high = jnp.where(dom == doms - 1, 0.0, 16.0)

    def face(k):
        factor = {3: inside_low, 7: inside_high}.get(k, 16.0)
        cu[k] = factor * harmonic(perm[k], perm[k + 1])

    def finish(k):
        diag = cw[k] + ce[k] + cs[k] + cn[k] + cu[k - 1] + cu[k] + edges * perm[k]
        dg[k] = diag
        scaled = OMEGA / diag
        cc[k] = scaled
        va[k] = scaled * src[k]

    def around0(v, k):
        x = v[k]
        a = cw[k] * down(x, 0) + ce[k] * up(x, 0)
        b = cs[k] * down(x, 1) + cn[k] * up(x, 1)
        return x, (a + b) + (cu[k - 1] * v[k - 1] + cu[k] * v[k + 1])

    def sweep0(v, k):
        x, total = around0(v, k)
        return KEEP * x + cc[k] * (src[k] + total)

    for k in range(4, 8):
        sides(k)
    for k in range(4, 7):
        face(k)
    load_source.wait()
    for copy in sends_src:
        copy.wait_recv()
    finish(5)
    finish(6)
    for k in (1, 2, 9, 10):
        near[k].wait_recv()
    for k in (2, 9):
        sides(k)
    for k in (1, 9):
        face(k)
    for k in (3, 8):
        near[k].wait_recv()
    for k in (3, 8):
        sides(k)
    for k in (2, 3, 7, 8):
        face(k)
    for k in (2, 3, 4, 7, 8, 9):
        finish(k)
    for k in range(3, 9):
        vb[k] = sweep0(va, k)
    rest = []
    for k in range(4, 8):
        x, total = around0(vb, k)
        rest.append(src[k] - dg[k] * x + total)
    right1[2] = restrict01(rest)
    sends_r = []
    for i, o in enumerate((1, -1, 2, -2)):
        copy = Along(right1.at[2], right1.at[2 - o], sr.at[i], dr.at[i], o)
        copy.start()
        sends_r.append(copy)
    hear(2)
    gather_to(gp2, sp.at[0], dp.at[0])

    for copy in sends_q:
        copy.wait_recv()
    wide = perm1[...].reshape(7 * 32, 128)
    wide_row, wide_lane = iota(wide.shape, 0), iota(wide.shape, 1)
    pair = (dom + (doms - 3) + (wide_row >> 5)) & (doms - 1)
    top1 = (pair == doms - 1) & (wide_lane >= 64)
    coefs1 = flat_coefs(wide, 4.0, wide_row & 31, wide_lane & 63, 32, 64, MOVES1, top1)
    for i, value in enumerate(coefs1):
        co1[i] = value[32:192]

    for copy in sends_r[:2]:
        copy.wait_recv()
    b1 = right1[pl.ds(1, 3)].reshape(96, 128)
    inner = [co1[i, 32:128] for i in range(8)]
    v1 = sweep(inner[7] * b1, b1, inner, MOVES1)
    res1 = b1 - inner[6] * v1 + around(v1, inner, MOVES1)
    gr2[dom] = restrict12(res1[32:64])
    gather_to(gr2, sg.at[0], dgs.at[0])

    for copy in sends_r[2:]:
        copy.wait_recv()
    b1 = right1[...].reshape(160, 128)
    all1 = [co1[i] for i in range(8)]
    v1s[...] = sweep(all1[7] * b1, b1, all1, MOVES1)
    for copy in far:
        copy.wait_recv()
    for k in (1, 10):
        sides(k)
    for k in (0, 10):
        face(k)
    for k in (1, 10):
        finish(k)
    for k in (2, 9):
        vb[k] = sweep0(va, k)

    row8, row128 = iota((8, 128), 0), iota((128, 128), 0)
    lane8, lane128 = iota((8, 128), 1), iota((128, 128), 1)
    group = [(iota((8, 256), 1) & 127) >> 4 == g for g in range(8)]

    def restrict23(value):
        both = value + up(value, 0, 4)
        moved = down(both, 0, 4)
        parts = []
        for g in range(8):
            low, high = both[16 * g : 16 * g + 8], moved[16 * g + 8 : 16 * g + 16]
            parts.append(jnp.where(row8 < 4, low, high))
        y = dot2(jnp.concatenate(parts, axis=0), c23)
        total = tree_sum([jnp.where(group[g], y[8 * g : 8 * g + 8], 0.0) for g in range(8)])
        for parity in range(2):
            for q in range(2):
                piece = total[4 * parity : 4 * parity + 4, 128 * q : 128 * q + 128]
                tmp3[pl.ds(8 * parity + q, 4, stride=2), :] = piece
        return tmp3[pl.ds(0, 8), :], tmp3[pl.ds(8, 8), :]

    def prolong23(pair_):
        tmp3[pl.ds(0, 8), :] = pair_[0]
        tmp3[pl.ds(8, 8), :] = pair_[1]
        halves = []
        for q in range(2):
            rows = [tmp3[pl.ds(8 * parity + q, 4, stride=2), :] for parity in range(2)]
            halves.append(jnp.concatenate(rows, axis=0))
        e = jnp.concatenate(halves, axis=1)
        y = dot2(jnp.concatenate([jnp.where(m, e, 0.0) for m in group], axis=0), c32)
        parts = []
        for g in range(8):
            value = y[8 * g : 8 * g + 8]
            other = pltpu.roll(value, 4, 0)
            parts.append(jnp.where(row8 < 4, value, other))
            parts.append(jnp.where(row8 < 4, other, value))
        return jnp.concatenate(parts, axis=0)

    gather_wait(gp2, sp.at[0], dp.at[0]).wait_recv()
    p2 = gp2[...].reshape(128, 128)
    x2 = 4 * (row128 & 3) + (lane128 >> 5)
    coefs2 = flat_coefs(p2, 16.0, x2, lane128 & 31, 16, 32, MOVES2, row128 >= 124)
    for i, value in enumerate(coefs2):
        co2[i] = value
    pa, pb = restrict23(p2)
    pa, pb = 0.125 * pa, 0.125 * pb
    y3 = lane8 & 15
    scale = 64.0
    edges3 = jnp.where(row8 == 0, scale, 0.0) + jnp.where(row8 == 7, scale, 0.0)
    edges3 = edges3 + jnp.where(y3 == 0, scale, 0.0) + jnp.where(y3 == 15, scale, 0.0)

    def sides3(p):
        east = jnp.where(row8 < 7, scale * harmonic(p, up(p, 0)), 0.0)
        north = jnp.where(y3 < 15, scale * harmonic(p, up(p, 1)), 0.0)
        return [down(east, 0), east, down(north, 1), north]

    mid = (16.0 * scale) * harmonic(pa, pb)
    high = jnp.where(lane8 < 112, (16.0 * scale) * harmonic(pb, up(pa, 1, 16)), 0.0)
    low = down(high, 1, 16)
    ca = sides3(pa) + [low, mid]
    cb = sides3(pb) + [mid, high]

    def scaled3(c, p):
        total = (c[0] + c[1]) + (c[2] + c[3]) + (c[4] + c[5]) + edges3 * p
        inverse = OMEGA / total
        return inverse, [inverse * value for value in c]

    ia, ca = scaled3(ca, pa)
    ib, cb = scaled3(cb, pb)
    keep = jnp.full((8, 128), KEEP, F32)
    offsets = ((-1, 0, 0), (1, 0, 0), (0, -1, 0), (0, 1, 0), (0, 0, -1), (0, 0, 1))
    once = {(0, 0, 0): (keep, keep)}
    once.update({o: (a, b) for o, a, b in zip(offsets, ca, cb)})
    thrice = compose3(once, compose3(once, once))
    keys = list(thrice)
    for i, key in enumerate(keys):
        for parity in range(2):
            m3[parity, i] = thrice[key][parity]

    gather_wait(gr2, sg.at[0], dgs.at[0]).wait_recv()
    b2 = gr2[...].reshape(128, 128)
    all2 = [co2[i] for i in range(8)]
    v2 = sweep(all2[7] * b2, b2, all2, MOVES2)
    res2 = b2 - all2[6] * v2 + around(v2, all2, MOVES2)
    ra, rb = restrict23(res2)
    base = (ia * ra, ib * rb)
    right3 = base
    base = apply3(once, apply3(once, right3, right3), right3)

    def coarse(step, value):
        operator = {key: (m3[0, i], m3[1, i]) for i, key in enumerate(keys)}
        return apply3(operator, value, base)

    v2 = v2 + prolong23(lax.fori_loop(0, (COARSE_SWEEPS - 1) // 3, coarse, right3))
    for _ in range(2):
        v2 = sweep(v2, b2, all2, MOVES2)
    e2s[...] = v2

    parts = []
    for j in range(-2, 3):
        z = slab(j)
        value = e2s[pl.ds(pl.multiple_of((z // 2) * 8, 8), 8), :]
        parts.append(jnp.where(lax.rem(z, 2) == 0, value, pltpu.roll(value, 4, 0)))
    wide1 = dot2(jnp.concatenate(parts, axis=0), c21)
    for j in range(5):
        for q in range(4):
            piece = wide1[8 * j : 8 * j + 4, 128 * q : 128 * q + 128]
            for i in range(2):
                tmp1[pl.ds(32 * j + 2 * q + i, 4, stride=8), :] = piece
    v1 = v1s[...] + tmp1[...]
    b1 = right1[...].reshape(160, 128)
    all1 = [co1[i] for i in range(8)]
    for _ in range(2):
        v1 = sweep(v1, b1, all1, MOVES1)

    fine = dot2(v1[32:128], c10)
    for k, i, half in ((2, 0, 1), (4, 1, 0), (6, 1, 1), (8, 2, 0)):
        repeat_rows(tmp, fine[32 * i : 32 * i + 32, 128 * half : 128 * half + 128])
        add = tmp[...]
        vb[k] = vb[k] + add
        vb[k + 1] = vb[k + 1] + add
    for k in range(3, 9):
        va[k] = sweep0(vb, k)
    for k in range(4, 8):
        out_ref[k - 4] = sweep0(va, k)

    @pl.when(me == root)
    def _():
        for k in order:
            for copy in across(k):
                copy.wait_send()

    @pl.when(leads)
    def _():
        for k in order:
            hand_over(k, cur.at[k]).wait_send()

    for copies in (sends_src, near.values(), far, sends_q, sends_r):
        for copy in copies:
            copy.wait_send()
    gather_wait(gp2, sp.at[0], dp.at[0]).wait_send()
    gather_wait(gr2, sg.at[0], dgs.at[0]).wait_send()


def body(states, accepted, noise, source):
    props, doms = lax.axis_size("prop"), lax.axis_size("dom")
    dma = pltpu.SemaphoreType.DMA
    plane = lambda n: pltpu.VMEM((n, 64, 128), F32)
    scratch = [
        plane(4), plane(4),
        plane(12), plane(12),
        plane(12), plane(12), plane(12), plane(12), plane(12), plane(12), plane(12),
        plane(12), plane(12),
        pltpu.VMEM((64, 128), F32),
        pltpu.VMEM((7, 32, 128), F32),
        pltpu.VMEM((5, 32, 128), F32),
        pltpu.VMEM((160, 128), F32),
        pltpu.VMEM((8, 160, 128), F32),
        pltpu.VMEM((160, 128), F32),
        pltpu.VMEM((32, 128), F32),
        pltpu.VMEM((doms, 4, 128), F32),
        pltpu.VMEM((doms, 4, 128), F32),
        pltpu.VMEM((8, 128, 128), F32),
        pltpu.VMEM((2, 63, 8, 128), F32),
        pltpu.VMEM((16, 128), F32),
        pltpu.VMEM((128, 128), F32),
        dma((2,)), dma((props, 4)), dma((4,)), dma((4,)),
        dma((2,)), dma((2,)), dma((4,)), dma((12,)), dma((4,)),
        dma((6,)), dma((6,)), dma((1,)), dma((1,)), dma((4,)), dma((4,)), dma((1,)), dma((1,)),
        pltpu.SemaphoreType.REGULAR((3, 2)),
        pltpu.SemaphoreType.REGULAR,
    ]
    hbm = pl.BlockSpec(memory_space=pl.ANY)

    def branch(root):
        return pl.pallas_call(
            functools.partial(kernel, props, doms, root),
            out_shape=pltpu.VMEM((4, 64, 128), F32),
            in_specs=[hbm, hbm, hbm],
            out_specs=pl.BlockSpec(memory_space=pltpu.VMEM),
            scratch_shapes=scratch,
            compiler_params=pltpu.CompilerParams(collective_id=root, has_side_effects=True),
            name=f"mcmc_step_{root}",
        )

    branches = [branch(root) for root in range(props)]
    return lax.switch(accepted[0], branches, states[0], noise[0], source)[None]


def solution(mesh):
    in_specs = (
        P("prop", "dom", None, None),
        P(),
        P("prop", "dom", None, None),
        P("dom", None, None),
    )
    out_specs = P("prop", "dom", None, None)
    return jax.shard_map(body, mesh=mesh, in_specs=in_specs, out_specs=out_specs, check_vma=False)
```

```python
import functools
import math

import jax
import jax.numpy as jnp
from jax import lax
from jax.experimental import pallas as pl
from jax.experimental.pallas import tpu as pltpu
from jax.sharding import PartitionSpec as P

OMEGA = 0.7
BETA = 0.4
SHRINK = math.sqrt(1.0 - BETA * BETA)
KEEP = 1.0 - OMEGA
COARSE_SWEEPS = 64
F32 = jnp.float32
BF16 = jnp.bfloat16
MESH = pl.DeviceIdType.MESH


def iota(shape, axis):
    return lax.broadcasted_iota(jnp.int32, shape, axis)


def ones_where(mask):
    return jnp.where(mask, 1.0, 0.0).astype(BF16)


def dot2(x, matrix):
    rows = x.shape[0]
    hi = x.astype(BF16).astype(F32)
    stacked = jnp.concatenate([hi, x - hi], axis=0).astype(BF16)
    y = jnp.dot(stacked, matrix, preferred_element_type=F32)
    return y[:rows] + y[rows:]


def up(v, axis, by=1):
    return pltpu.roll(v, v.shape[axis] - by, axis)


def down(v, axis, by=1):
    return pltpu.roll(v, by, axis)


def harmonic(a, b):
    return 2.0 * a * b / (a + b)


def pair_rows(ref, rows):
    return ref[pl.ds(0, rows, stride=2), :] + ref[pl.ds(1, rows, stride=2), :]


def repeat_rows(ref, value):
    rows = value.shape[0]
    ref[pl.ds(0, rows, stride=2), :] = value
    ref[pl.ds(1, rows, stride=2), :] = value


def zup1(v):
    swapped = pltpu.roll(v, 64, 1)
    return jnp.where(iota(v.shape, 1) < 64, swapped, up(swapped, 0, 32))


def zdown1(v):
    swapped = pltpu.roll(v, 64, 1)
    return jnp.where(iota(v.shape, 1) < 64, down(swapped, 0, 32), swapped)


def xup2(v):
    moved = up(v, 1, 32)
    return jnp.where(iota(v.shape, 1) < 96, moved, up(moved, 0))


def xdown2(v):
    moved = down(v, 1, 32)
    return jnp.where(iota(v.shape, 1) < 32, down(moved, 0), moved)


def zup2(v):
    return up(v, 0, 4)


def zdown2(v):
    return down(v, 0, 4)


def xup1(v):
    return up(v, 0)


def xdown1(v):
    return down(v, 0)


MOVES1 = (xdown1, xup1, zdown1, zup1)
MOVES2 = (xdown2, xup2, zdown2, zup2)


def flat_coefs(perm, scale, x, y, nx, ny, moves, top):
    xdown, xup, zdown, zup = moves
    east = jnp.where(x < nx - 1, scale * harmonic(perm, xup(perm)), 0.0)
    north = jnp.where(y < ny - 1, scale * harmonic(perm, up(perm, 1)), 0.0)
    above = jnp.where(top, 0.0, (16.0 * scale) * harmonic(perm, zup(perm)))
    west, south, below = xdown(east), down(north, 1), zdown(above)
    edges = jnp.where(x == 0, scale, 0.0) + jnp.where(x == nx - 1, scale, 0.0)
    edges = edges + jnp.where(y == 0, scale, 0.0) + jnp.where(y == ny - 1, scale, 0.0)
    diag = west + east + south + north + below + above + edges * perm
    return west, east, south, north, below, above, diag, OMEGA / diag


def around(v, c, moves):
    xdown, xup, zdown, zup = moves
    a = c[0] * xdown(v) + c[1] * xup(v)
    b = c[2] * down(v, 1) + c[3] * up(v, 1)
    return (a + b) + (c[4] * zdown(v) + c[5] * zup(v))


def sweep(v, right, c, moves):
    return KEEP * v + c[7] * (right + around(v, c, moves))


def shifted(pair, parity, offset, cache):
    dx, dy, dz = offset
    source = (parity + dz) % 2
    lanes = dy + 16 * ((parity + dz - source) // 2)
    if (source, lanes) not in cache:
        value = pair[source]
        cache[source, lanes] = value if lanes == 0 else pltpu.roll(value, -lanes % 128, 1)
    value = cache[source, lanes]
    return value if dx == 0 else pltpu.roll(value, -dx % 8, 0)


def tree_sum(terms):
    while len(terms) > 1:
        terms = [a + b for a, b in zip(terms[::2], terms[1::2])] + terms[len(terms) & ~1 :]
    return terms[0]


def apply3(operator, pair, base):
    cache = {}
    out = []
    for parity in range(2):
        terms = [base[parity]]
        terms += [c[parity] * shifted(pair, parity, o, cache) for o, c in operator.items()]
        out.append(tree_sum(terms))
    return tuple(out)


def compose3(first, second):
    out = {}
    for o2, c2 in second.items():
        cache = {}
        for o1, c1 in first.items():
            term = [c1[parity] * shifted(c2, parity, o1, cache) for parity in range(2)]
            key = tuple(a + b for a, b in zip(o1, o2))
            out[key] = [a + b for a, b in zip(out[key], term)] if key in out else term
    return out


def kernel(
    props, doms, root, states, noise, source, out_ref,
    cur, nz, perm, src, cw, ce, cs, cn, cu, dg, cc, va, vb, tmp,
    perm1, right1, tmp1, co1, v1s, tmp2, gp2, gr2, co2, m3, tmp3, e2s,
    loc, s1, d1, s2, ss, ds_, sn, dn, sf, sq, dq, sp, dp, sr, dr, sg, dgs, word, ready,
):
    me = lax.axis_index("prop")
    dom = lax.axis_index("dom")

    spread = lambda p: -min((p - root) % props, (root - p) % props)
    peers = sorted((p for p in range(props) if p != root), key=spread)

    def slab(o):
        return lax.rem(dom + (o + doms), doms)

    def remote(from_ref, to_ref, send, recv, p, d):
        return pltpu.make_async_remote_copy(
            src_ref=from_ref, dst_ref=to_ref, send_sem=send, recv_sem=recv,
            device_id=(p, d), device_id_type=MESH,
        )

    def within(o):
        return (dom + o >= 0) & (dom + o < doms)

    class Along:
        def __init__(self, from_ref, to_ref, send, recv, o):
            self.copy = remote(from_ref, to_ref, send, recv, me, slab(o))
            self.to, self.source = within(o), within(-o)

        def start(self):
            pl.when(self.to)(self.copy.start)

        def wait_send(self):
            pl.when(self.to)(self.copy.wait_send)

        def wait_recv(self):
            pl.when(self.source)(self.copy.wait_recv)

    @pl.when((dom < 3) | (dom >= doms - 3))
    def _():
        for first in (0, 8):
            perm[pl.ds(first, 4)] = jnp.ones((4, 64, 128), F32)
            src[pl.ds(first, 4)] = jnp.zeros((4, 64, 128), F32)
        perm1[...] = jnp.ones(perm1.shape, F32)
        right1[...] = jnp.zeros(right1.shape, F32)

    load_noise = pltpu.make_async_copy(noise, nz, loc.at[0])
    load_source = pltpu.make_async_copy(source, src.at[pl.ds(4, 4)], loc.at[1])
    load_noise.start()
    load_source.start()
    order = (1, 2, 3, 0)

    def load_plane(k):
        return pltpu.make_async_copy(states.at[k], cur.at[k], d1.at[k])

    barrier = pltpu.get_barrier_semaphore()

    mate = me + 1 - 2 * lax.rem(me, 2)
    away = me // 2 != root // 2
    relay = away & (lax.rem(me, 2) == 0)
    leads = relay | (me == root)

    @pl.when(relay)
    def _():
        pl.semaphore_signal(barrier, inc=1, device_id=(root, dom), device_id_type=MESH)

    @pl.when(leads)
    def _():
        pl.semaphore_signal(barrier, inc=1, device_id=(mate, dom), device_id_type=MESH)

    for o in (1, -1, 2, -2, 3, -3, 4, -4):

        @pl.when(within(o))
        def _(o=o):
            pl.semaphore_signal(barrier, inc=1, device_id=(me, slab(o)), device_id_type=MESH)

    beside = jnp.minimum(dom, 4) + jnp.minimum(doms - 1 - dom, 4)
    extra = jnp.where(me == root, props // 2 - 1, jnp.where(leads, 0, 1))
    pl.semaphore_wait(barrier, beside + extra)

    @pl.when(jnp.logical_not(leads))
    def _():
        pl.semaphore_signal(ready, inc=1, device_id=(mate, dom), device_id_type=MESH)

    def across(k):
        return [
            remote(states.at[k], cur.at[k], s1.at[p, k], d1.at[k], p, dom)
            for p in peers
            if p // 2 != root // 2 and p % 2 == 0
        ]

    def hand_over(k, from_ref):
        return remote(from_ref, cur.at[k], s2.at[k], d1.at[k], mate, dom)

    @pl.when(me == root)
    def _():
        for k in order:
            for copy in across(k):
                copy.start()
            load_plane(k).start()

    reach = (4, 8, 16)

    def tell(i):
        for side, o in enumerate((reach[i], -reach[i])):

            @pl.when(within(o))
            def _(side=side, o=o):
                target = (me, slab(o))
                pl.semaphore_signal(word.at[i, side], inc=1, device_id=target, device_id_type=MESH)

    def hear(i):
        for side, o in enumerate((reach[i], -reach[i])):

            @pl.when(within(-o))
            def _(side=side):
                pl.semaphore_wait(word.at[i, side], 1)

    tell(0)

    sends_src = [
        Along(source.at[pl.ds(1, 3)], src.at[pl.ds(1, 3)], ss.at[0], ds_.at[0], 1),
        Along(source.at[pl.ds(0, 3)], src.at[pl.ds(8, 3)], ss.at[1], ds_.at[1], -1),
    ]
    for copy in sends_src:
        copy.start()

    r01, l01 = iota((256, 128), 0), iota((256, 128), 1)
    c01 = ones_where(l01 == (r01 >> 1))
    r12, l12 = iota((512, 128), 0), iota((512, 128), 1)
    c12 = ones_where(((r12 >> 7) == (l12 >> 5)) & (((r12 & 63) >> 1) == (l12 & 31)))
    r23, l23 = iota((128, 256), 0), iota((128, 256), 1)
    c23 = ones_where(((r23 >> 6) == (l23 >> 7)) & (((r23 & 31) >> 1) == (l23 & 15)))
    r32, l32 = iota((256, 128), 0), iota((256, 128), 1)
    c32 = ones_where(((l32 >> 6) == (r32 >> 7)) & (((l32 & 31) >> 1) == (r32 & 15)))
    r21, l21 = iota((128, 512), 0), iota((128, 512), 1)
    c21 = ones_where(((r21 >> 5) == (l21 >> 7)) & ((r21 & 31) == ((l21 & 63) >> 1)))
    r10, l10 = iota((128, 256), 0), iota((128, 256), 1)
    c10 = ones_where(r10 == (l10 >> 1))
    row, lane = iota((64, 128), 0), iota((64, 128), 1)
    east_in, north_in = row < 63, lane < 127
    edges = jnp.where(row == 0, 1.0, 0.0) + jnp.where(row == 63, 1.0, 0.0)
    edges = edges + jnp.where(lane == 0, 1.0, 0.0) + jnp.where(lane == 127, 1.0, 0.0)

    load_noise.wait()
    @pl.when(me == root)
    def _():
        pl.semaphore_wait(ready, 1)
        for k in order:
            hand_over(k, states.at[k]).start()

    near = {k: Along(perm.at[4 + k], perm.at[k], sn.at[k], dn.at[k], 1) for k in (1, 2, 3)}
    for k in (0, 1, 2):
        near[8 + k] = Along(perm.at[4 + k], perm.at[8 + k], sf.at[k], dn.at[8 + k], -1)

    for k in order:
        load_plane(k).wait()

        @pl.when(relay)
        def _(k=k):
            if k == order[0]:
                pl.semaphore_wait(ready, 1)
            hand_over(k, cur.at[k]).start()

        perm[4 + k] = jnp.exp(SHRINK * cur[k] + BETA * nz[k])
        if k > 0:
            near[k].start()
        if k < 3:
            near[8 + k].start()
    hear(0)
    tell(1)
    far = [
        Along(perm.at[4], perm.at[0], sn.at[0], dn.at[0], 1),
        Along(perm.at[7], perm.at[11], sf.at[3], dn.at[11], -1),
    ]
    for copy in far:
        copy.start()

    def restrict01(planes):
        sums = []
        for i in range(2):
            tmp[...] = planes[2 * i] + planes[2 * i + 1]
            sums.append(pair_rows(tmp, 32))
        return dot2(jnp.concatenate(sums, axis=1), c01)

    def restrict12(value):
        tmp2[...] = value
        parts = []
        for q in range(4):
            low = tmp2[pl.ds(2 * q, 4, stride=8), :]
            parts.append(low + tmp2[pl.ds(2 * q + 1, 4, stride=8), :])
        return dot2(jnp.concatenate(parts, axis=1), c12)

    own1 = 0.125 * restrict01([perm[k] for k in range(4, 8)])
    perm1[3] = own1
    sends_q = []
    for i, o in enumerate((1, -1, 2, -2, 3, -3)):
        copy = Along(perm1.at[3], perm1.at[3 - o], sq.at[i], dq.at[i], o)
        copy.start()
        sends_q.append(copy)
    hear(1)
    tell(2)
    gp2[dom] = 0.125 * restrict12(own1)

    def gather_to(buf, send, recv):
        def go(i, carry):
            step = (i + 1) // 2 * (2 * lax.rem(i, 2) - 1)
            remote(buf.at[dom], buf.at[dom], send, recv, me, slab(doms // 2 + step)).start()
            return carry

        lax.fori_loop(0, doms - 1, go, 0)

    def gather_wait(buf, send, recv):
        part = buf.at[pl.ds(0, doms - 1)]
        return remote(part, part, send, recv, me, slab(1))


    def sides(k):
        p = perm[k]
        east = jnp.where(east_in, harmonic(p, up(p, 0)), 0.0)
        north = jnp.where(north_in, harmonic(p, up(p, 1)), 0.0)
        ce[k] = east
        cn[k] = north
        cw[k] = down(east, 0)
        cs[k] = down(north, 1)

    inside_low = jnp.where(dom == 0, 0.0, 16.0)
    inside_high = jnp.where(dom == doms - 1, 0.0, 16.0)

    def face(k):
        factor = {3: inside_low, 7: inside_high}.get(k, 16.0)
        cu[k] = factor * harmonic(perm[k], perm[k + 1])

    def finish(k):
        diag = cw[k] + ce[k] + cs[k] + cn[k] + cu[k - 1] + cu[k] + edges * perm[k]
        dg[k] = diag
        scaled = OMEGA / diag
        cc[k] = scaled
        va[k] = scaled * src[k]

    def around0(v, k):
        x = v[k]
        a = cw[k] * down(x, 0) + ce[k] * up(x, 0)
        b = cs[k] * down(x, 1) + cn[k] * up(x, 1)
        return x, (a + b) + (cu[k - 1] * v[k - 1] + cu[k] * v[k + 1])

    def sweep0(v, k):
        x, total = around0(v, k)
        return KEEP * x + cc[k] * (src[k] + total)

    for k in range(4, 8):
        sides(k)
    for k in range(4, 7):
        face(k)
    load_source.wait()
    for copy in sends_src:
        copy.wait_recv()
    finish(5)
    finish(6)
    for k in (1, 2, 9, 10):
        near[k].wait_recv()
    for k in (2, 9):
        sides(k)
    for k in (1, 9):
        face(k)
    for k in (3, 8):
        near[k].wait_recv()
    for k in (3, 8):
        sides(k)
    for k in (2, 3, 7, 8):
        face(k)
    for k in (2, 3, 4, 7, 8, 9):
        finish(k)
    for k in range(3, 9):
        vb[k] = sweep0(va, k)
    rest = []
    for k in range(4, 8):
        x, total = around0(vb, k)
        rest.append(src[k] - dg[k] * x + total)
    right1[2] = restrict01(rest)
    sends_r = []
    for i, o in enumerate((1, -1, 2, -2)):
        copy = Along(right1.at[2], right1.at[2 - o], sr.at[i], dr.at[i], o)
        copy.start()
        sends_r.append(copy)
    hear(2)
    gather_to(gp2, sp.at[0], dp.at[0])

    for copy in sends_q:
        copy.wait_recv()
    wide = perm1[...].reshape(7 * 32, 128)
    wide_row, wide_lane = iota(wide.shape, 0), iota(wide.shape, 1)
    pair = (dom + (doms - 3) + (wide_row >> 5)) & (doms - 1)
    top1 = (pair == doms - 1) & (wide_lane >= 64)
    coefs1 = flat_coefs(wide, 4.0, wide_row & 31, wide_lane & 63, 32, 64, MOVES1, top1)
    for i, value in enumerate(coefs1):
        co1[i] = value[32:192]

    for copy in sends_r[:2]:
        copy.wait_recv()
    b1 = right1[pl.ds(1, 3)].reshape(96, 128)
    inner = [co1[i, 32:128] for i in range(8)]
    v1 = sweep(inner[7] * b1, b1, inner, MOVES1)
    res1 = b1 - inner[6] * v1 + around(v1, inner, MOVES1)
    gr2[dom] = restrict12(res1[32:64])
    gather_to(gr2, sg.at[0], dgs.at[0])

    for copy in sends_r[2:]:
        copy.wait_recv()
    b1 = right1[...].reshape(160, 128)
    all1 = [co1[i] for i in range(8)]
    v1s[...] = sweep(all1[7] * b1, b1, all1, MOVES1)
    for copy in far:
        copy.wait_recv()
    for k in (1, 10):
        sides(k)
    for k in (0, 10):
        face(k)
    for k in (1, 10):
        finish(k)
    for k in (2, 9):
        vb[k] = sweep0(va, k)

    row8, row128 = iota((8, 128), 0), iota((128, 128), 0)
    lane8, lane128 = iota((8, 128), 1), iota((128, 128), 1)
    group = [(iota((8, 256), 1) & 127) >> 4 == g for g in range(8)]

    def restrict23(value):
        both = value + up(value, 0, 4)
        moved = down(both, 0, 4)
        parts = []
        for g in range(8):
            low, high = both[16 * g : 16 * g + 8], moved[16 * g + 8 : 16 * g + 16]
            parts.append(jnp.where(row8 < 4, low, high))
        y = dot2(jnp.concatenate(parts, axis=0), c23)
        total = tree_sum([jnp.where(group[g], y[8 * g : 8 * g + 8], 0.0) for g in range(8)])
        for parity in range(2):
            for q in range(2):
                piece = total[4 * parity : 4 * parity + 4, 128 * q : 128 * q + 128]
                tmp3[pl.ds(8 * parity + q, 4, stride=2), :] = piece
        return tmp3[pl.ds(0, 8), :], tmp3[pl.ds(8, 8), :]

    def prolong23(pair_):
        tmp3[pl.ds(0, 8), :] = pair_[0]
        tmp3[pl.ds(8, 8), :] = pair_[1]
        halves = []
        for q in range(2):
            rows = [tmp3[pl.ds(8 * parity + q, 4, stride=2), :] for parity in range(2)]
            halves.append(jnp.concatenate(rows, axis=0))
        e = jnp.concatenate(halves, axis=1)
        y = dot2(jnp.concatenate([jnp.where(m, e, 0.0) for m in group], axis=0), c32)
        parts = []
        for g in range(8):
            value = y[8 * g : 8 * g + 8]
            other = pltpu.roll(value, 4, 0)
            parts.append(jnp.where(row8 < 4, value, other))
            parts.append(jnp.where(row8 < 4, other, value))
        return jnp.concatenate(parts, axis=0)

    gather_wait(gp2, sp.at[0], dp.at[0]).wait_recv()
    p2 = gp2[...].reshape(128, 128)
    x2 = 4 * (row128 & 3) + (lane128 >> 5)
    coefs2 = flat_coefs(p2, 16.0, x2, lane128 & 31, 16, 32, MOVES2, row128 >= 124)
    for i, value in enumerate(coefs2):
        co2[i] = value
    pa, pb = restrict23(p2)
    pa, pb = 0.125 * pa, 0.125 * pb
    y3 = lane8 & 15
    scale = 64.0
    edges3 = jnp.where(row8 == 0, scale, 0.0) + jnp.where(row8 == 7, scale, 0.0)
    edges3 = edges3 + jnp.where(y3 == 0, scale, 0.0) + jnp.where(y3 == 15, scale, 0.0)

    def sides3(p):
        east = jnp.where(row8 < 7, scale * harmonic(p, up(p, 0)), 0.0)
        north = jnp.where(y3 < 15, scale * harmonic(p, up(p, 1)), 0.0)
        return [down(east, 0), east, down(north, 1), north]

    mid = (16.0 * scale) * harmonic(pa, pb)
    high = jnp.where(lane8 < 112, (16.0 * scale) * harmonic(pb, up(pa, 1, 16)), 0.0)
    low = down(high, 1, 16)
    ca = sides3(pa) + [low, mid]
    cb = sides3(pb) + [mid, high]

    def scaled3(c, p):
        total = (c[0] + c[1]) + (c[2] + c[3]) + (c[4] + c[5]) + edges3 * p
        inverse = OMEGA / total
        return inverse, [inverse * value for value in c]

    ia, ca = scaled3(ca, pa)
    ib, cb = scaled3(cb, pb)
    keep = jnp.full((8, 128), KEEP, F32)
    offsets = ((-1, 0, 0), (1, 0, 0), (0, -1, 0), (0, 1, 0), (0, 0, -1), (0, 0, 1))
    once = {(0, 0, 0): (keep, keep)}
    once.update({o: (a, b) for o, a, b in zip(offsets, ca, cb)})
    twice = compose3(once, once)
    thrice = compose3(once, twice)
    both = {o: [a + b for a, b in zip(c, once[o])] if o in once else c for o, c in twice.items()}
    keys = list(thrice)
    for i, key in enumerate(keys):
        for parity in range(2):
            m3[parity, i] = thrice[key][parity]

    gather_wait(gr2, sg.at[0], dgs.at[0]).wait_recv()
    b2 = gr2[...].reshape(128, 128)
    all2 = [co2[i] for i in range(8)]
    v2 = sweep(all2[7] * b2, b2, all2, MOVES2)
    res2 = b2 - all2[6] * v2 + around(v2, all2, MOVES2)
    ra, rb = restrict23(res2)
    base = (ia * ra, ib * rb)
    right3 = base
    base = apply3(both, right3, right3)

    def coarse(step, value):
        operator = {key: (m3[0, i], m3[1, i]) for i, key in enumerate(keys)}
        return apply3(operator, value, base)

    v2 = v2 + prolong23(lax.fori_loop(0, (COARSE_SWEEPS - 1) // 3, coarse, right3))
    for _ in range(2):
        v2 = sweep(v2, b2, all2, MOVES2)
    e2s[...] = v2

    parts = []
    for j in range(-2, 3):
        z = slab(j)
        value = e2s[pl.ds(pl.multiple_of((z // 2) * 8, 8), 8), :]
        parts.append(jnp.where(lax.rem(z, 2) == 0, value, pltpu.roll(value, 4, 0)))
    wide1 = dot2(jnp.concatenate(parts, axis=0), c21)
    for j in range(5):
        for q in range(4):
            piece = wide1[8 * j : 8 * j + 4, 128 * q : 128 * q + 128]
            for i in range(2):
                tmp1[pl.ds(32 * j + 2 * q + i, 4, stride=8), :] = piece
    v1 = v1s[...] + tmp1[...]
    b1 = right1[...].reshape(160, 128)
    all1 = [co1[i] for i in range(8)]
    for _ in range(2):
        v1 = sweep(v1, b1, all1, MOVES1)

    fine = dot2(v1[32:128], c10)
    for k, i, half in ((2, 0, 1), (4, 1, 0), (6, 1, 1), (8, 2, 0)):
        repeat_rows(tmp, fine[32 * i : 32 * i + 32, 128 * half : 128 * half + 128])
        add = tmp[...]
        vb[k] = vb[k] + add
        vb[k + 1] = vb[k + 1] + add
    for k in range(3, 9):
        va[k] = sweep0(vb, k)
    for k in range(4, 8):
        out_ref[k - 4] = sweep0(va, k)

    @pl.when(me == root)
    def _():
        for k in order:
            for copy in across(k):
                copy.wait_send()

    @pl.when(leads)
    def _():
        for k in order:
            hand_over(k, cur.at[k]).wait_send()

    for copies in (sends_src, near.values(), far, sends_q, sends_r):
        for copy in copies:
            copy.wait_send()
    gather_wait(gp2, sp.at[0], dp.at[0]).wait_send()
    gather_wait(gr2, sg.at[0], dgs.at[0]).wait_send()


def body(states, accepted, noise, source):
    props, doms = lax.axis_size("prop"), lax.axis_size("dom")
    dma = pltpu.SemaphoreType.DMA
    plane = lambda n: pltpu.VMEM((n, 64, 128), F32)
    scratch = [
        plane(4), plane(4),
        plane(12), plane(12),
        plane(12), plane(12), plane(12), plane(12), plane(12), plane(12), plane(12),
        plane(12), plane(12),
        pltpu.VMEM((64, 128), F32),
        pltpu.VMEM((7, 32, 128), F32),
        pltpu.VMEM((5, 32, 128), F32),
        pltpu.VMEM((160, 128), F32),
        pltpu.VMEM((8, 160, 128), F32),
        pltpu.VMEM((160, 128), F32),
        pltpu.VMEM((32, 128), F32),
        pltpu.VMEM((doms, 4, 128), F32),
        pltpu.VMEM((doms, 4, 128), F32),
        pltpu.VMEM((8, 128, 128), F32),
        pltpu.VMEM((2, 63, 8, 128), F32),
        pltpu.VMEM((16, 128), F32),
        pltpu.VMEM((128, 128), F32),
        dma((2,)), dma((props, 4)), dma((4,)), dma((4,)),
        dma((2,)), dma((2,)), dma((4,)), dma((12,)), dma((4,)),
        dma((6,)), dma((6,)), dma((1,)), dma((1,)), dma((4,)), dma((4,)), dma((1,)), dma((1,)),
        pltpu.SemaphoreType.REGULAR((3, 2)),
        pltpu.SemaphoreType.REGULAR,
    ]
    hbm = pl.BlockSpec(memory_space=pl.ANY)

    def branch(root):
        return pl.pallas_call(
            functools.partial(kernel, props, doms, root),
            out_shape=pltpu.VMEM((4, 64, 128), F32),
            in_specs=[hbm, hbm, hbm],
            out_specs=pl.BlockSpec(memory_space=pltpu.VMEM),
            scratch_shapes=scratch,
            compiler_params=pltpu.CompilerParams(collective_id=root, has_side_effects=True),
            name=f"mcmc_step_{root}",
        )

    branches = [branch(root) for root in range(props)]
    return lax.switch(accepted[0], branches, states[0], noise[0], source)[None]


def solution(mesh):
    in_specs = (
        P("prop", "dom", None, None),
        P(),
        P("prop", "dom", None, None),
        P("dom", None, None),
    )
    out_specs = P("prop", "dom", None, None)
    return jax.shard_map(body, mesh=mesh, in_specs=in_specs, out_specs=out_specs, check_vma=False)
```
